128 devices in a mesh: req: 16 (over y, z), tp: 8 (over x, core).
Axes of the slice: x: 4, y: 4, z: 4, core: 2. Of those that a mesh axis runs over, the one named last changes fastest.
Arguments:
- hidden_in: bfloat16 [4096, 2048], P('req'), may hold values from -40 to 40
- recompute_pos: int32 [16, 256], replicated, may hold values from 0 to 16383, as said below
- req_lengths: int32 [16], replicated, may hold values from 1 to 32, as said below
- stretch_order: int32 [16, 32], replicated, may hold values from 0 to 511, as said below
- page_table: int32 [2, 512], replicated, may hold values from 0 to 31, as said below
- cached_key_pool: bfloat16 [512, 512, 1024], P('req', None, 'tp'), may hold values from -6 to 6
- cached_value_pool: bfloat16 [512, 512, 1024], P('req', None, 'tp'), may hold values from -6 to 6
- attn_gain: float32 [2048], replicated, may hold values from 0.5 to 2
- w_query: bfloat16 [2048, 2048], P(None, 'tp'), may hold values from -1 to 1
- w_key: bfloat16 [2048, 1024], P(None, 'tp'), may hold values from -1 to 1
- value_weight: bfloat16 [2048, 1024], P(None, 'tp'), may hold values from -0.125 to 0.125
- query_gain: float32 [128], replicated, may hold values from 0 to 20
- key_norm_gain: float32 [128], replicated, may hold values from 0 to 20
- w_out: bfloat16 [2048, 2048], P('tp'), may hold values from -0.5 to 0.5
- ffn_gain: float32 [2048], replicated, may hold values from 0.5 to 2
- w_gate: bfloat16 [2048, 6144], P(None, 'tp'), may hold values from -0.125 to 0.125
- w_up: bfloat16 [2048, 6144], P(None, 'tp'), may hold values from -0.125 to 0.125
- w_down: bfloat16 [6144, 2048], P('tp'), may hold values from -0.078125 to 0.078125
Outputs:
- layer_out: bfloat16 [4096, 2048], P('req')
The draws below stay inside these ranges and needn't reach their ends.
Inputs may be any that keep to these rules, and one draw needn't show every extreme that they name: `req_lengths`: on each draw, the requests of one index along req (chosen anew each time) all have 32 stretches; the others have 1 to 32. `stretch_order`: every stretch id appears exactly once over all requests and places, places at or past a request's length included. `page_table`: every slot of every index along req holds exactly one stretch id, and each index holds exactly 2 of the 32 ids listed by the requests of any one index. `recompute_pos`: strictly increasing along a request, below 512 times the request's length; every request recomputes its first and its last position.
All inputs are finite; a program needn't handle non-finite values.
Results may differ from the reference program's by a relative error of at most 0.015.
The reference program's roundings to bfloat16 on the way count: a program that leaves them out, or rounds other values in their place, can miss the bound.
Values may be sent and summed in bfloat16 or wider, within the bound.
No kernel may reach another device: no remote copies, remote signals or barrier semaphores. Data moves between devices by JAX's collectives and lax.ppermute only.
A program may use at most 192 MiB of HBM per device.

```python
import math
import jax
import jax.numpy as jnp
from jax import lax

MODEL_WIDTH = 2048
QUERY_HEADS = 16
KV_HEAD_COUNT = 8
HEAD_SIZE = 128
FF = 6144
STRETCH_TOKENS = 512
MOST_STRETCHES = 32
REQ_DEV = 1
RECOMPUTE_TOKENS = 256
REQUEST_COUNT = 16
TOKENS = 4096
POOL_SLOTS = 32
N_REQ = 16
N_TP = 8


def routing(key):
    base_key = jax.random.fold_in(key, 7001)
    length_key, full_key, offset_key, shuffle_key, stretch_key = jax.random.split(base_key, 5)
    dev_count = REQUEST_COUNT // REQ_DEV
    owner_dev = jnp.arange(REQUEST_COUNT) // REQ_DEV
    lengths = jax.random.randint(length_key, (REQUEST_COUNT,), 1, MOST_STRETCHES + 1)
    full_dev = jax.random.randint(full_key, (), 0, dev_count)
    lengths = jnp.where(owner_dev == full_dev, MOST_STRETCHES, lengths).astype(jnp.int32)
    order_scores = jax.random.randint(offset_key, (dev_count, POOL_SLOTS), 0, 2 ** 16) * POOL_SLOTS + jnp.arange(POOL_SLOTS)[None, :]
    offset = jnp.argsort(order_scores, axis=1).astype(jnp.int32)
    requester = jnp.arange(dev_count)[:, None]
    holder = (requester + offset) % dev_count
    base_slot = requester * (POOL_SLOTS // dev_count) + offset // dev_count
    shuffle_scores = jax.random.randint(shuffle_key, (dev_count, POOL_SLOTS), 0, 2 ** 16) * POOL_SLOTS + jnp.arange(POOL_SLOTS)[None, :]
    shuffle = jnp.argsort(shuffle_scores, axis=1).astype(jnp.int32)
    slot_index = shuffle[holder, base_slot]
    id_count = REQUEST_COUNT * MOST_STRETCHES
    id_scores = jax.random.randint(stretch_key, (id_count,), 0, 2 ** 12) * id_count + jnp.arange(id_count)
    stretch_ids = jnp.argsort(id_scores).astype(jnp.int32)
    page_rows = jnp.zeros((2, id_count), jnp.int32)
    page_rows = page_rows.at[0, stretch_ids].set(holder.reshape(id_count).astype(jnp.int32))
    page_rows = page_rows.at[1, stretch_ids].set(slot_index.reshape(id_count).astype(jnp.int32))
    return (lengths, stretch_ids.reshape(REQUEST_COUNT, MOST_STRETCHES), page_rows)


def positions(key, lengths):
    pos_key = jax.random.fold_in(key, 7002)
    span = MOST_STRETCHES * STRETCH_TOKENS
    place = jnp.arange(span)
    scores = jax.random.randint(pos_key, (REQUEST_COUNT, span), 0, 2 ** 14) * span + place[None, :]
    limit = lengths[:, None] * STRETCH_TOKENS
    scores = jnp.where(place[None, :] >= limit, -1, scores)
    scores = jnp.where((place[None, :] == 0) | (place[None, :] == limit - 1), 2 ** 30, scores)
    chosen = lax.top_k(scores, RECOMPUTE_TOKENS)[1]
    return jnp.sort(chosen, axis=1).astype(jnp.int32)


def draw_req_lengths(key, part):
    return routing(key)[0]


def draw_stretch_order(key, part):
    return routing(key)[1]


def draw_page_table(key, part):
    return routing(key)[2]


def draw_recompute_pos(key, part):
    return positions(key, routing(key)[0])


def draw_hidden_in(key, part):
    base_key = jax.random.fold_in(key, 7101)
    value_key = jax.random.fold_in(base_key, 0)
    row_key = jax.random.fold_in(base_key, 1)
    col_key = jax.random.fold_in(base_key, 2)
    near_key = jax.random.fold_in(base_key, 4)
    pair_count = TOKENS // 2
    row_scale = jnp.exp(jax.random.uniform(row_key, (pair_count, 1), minval=math.log(0.3), maxval=math.log(3.0)))
    col_scale = jnp.exp(jax.random.uniform(col_key, (1, MODEL_WIDTH), minval=math.log(0.3), maxval=math.log(3.0)))
    lead_rows = jax.random.normal(value_key, (pair_count, MODEL_WIDTH))
    near_rows = jax.random.normal(near_key, (pair_count, MODEL_WIDTH))
    paired = jnp.stack([lead_rows * row_scale, near_rows * row_scale], axis=1).reshape(TOKENS, MODEL_WIDTH)
    return jnp.clip(paired * col_scale, -40.0, 40.0).astype(jnp.bfloat16)


def weight_pair(key):
    base_key = jax.random.fold_in(key, 7201)
    query_key, key_random_seed = jax.random.split(base_key, 2)
    spread_width = MODEL_WIDTH ** (-0.5)
    query_matrix = jax.random.normal(query_key, (MODEL_WIDTH, QUERY_HEADS * HEAD_SIZE)) * spread_width
    key_matrix = jax.random.normal(key_random_seed, (MODEL_WIDTH, KV_HEAD_COUNT * HEAD_SIZE)) * spread_width
    return (jnp.clip(query_matrix, -1.0, 1.0), jnp.clip(key_matrix, -1.0, 1.0))


def draw_w_query(key, part):
    return weight_pair(key)[0].astype(jnp.bfloat16)


def draw_w_key(key, part):
    return weight_pair(key)[1].astype(jnp.bfloat16)


def gain_pair(key):
    base_key = jax.random.fold_in(key, 7301)
    query_key, key_random_seed = jax.random.split(base_key)
    query_scale = jnp.exp(jax.random.uniform(query_key, (HEAD_SIZE,), minval=math.log(1.2), maxval=math.log(3.0)))
    key_scale = jnp.exp(jax.random.uniform(key_random_seed, (HEAD_SIZE,), minval=math.log(0.7), maxval=math.log(1.4)))
    return (query_scale, key_scale)


def draw_query_gain(key, part):
    return gain_pair(key)[0].astype(jnp.float32)


def draw_key_norm_gain(key, part):
    return gain_pair(key)[1].astype(jnp.float32)


def level_of(stream_key, shape, pieces, low, top_value):
    factor_of, own = 1.0, jax.random.fold_in(stream_key, 6)
    for axis_at, shards_of in pieces:
        draws = jnp.exp(jax.random.uniform(jax.random.fold_in(own, axis_at), (shards_of,), jnp.float32, low / len(pieces), top_value / len(pieces)))
        factor_of = factor_of * jnp.repeat(draws, shape[axis_at] // shards_of).reshape([-1 if axis == axis_at else 1 for axis in range(len(shape))])
    return factor_of


def scatter_about(key, dims, width, bound, cuts=(), kind=jnp.bfloat16):
    values = jax.random.normal(key, dims, jnp.float32) * width
    if len(cuts) > 0:
        values = level_of(key, dims, cuts, -0.22, 0.18) * values
    return jnp.clip(values, min=-bound, max=bound).astype(kind)


def setup_inputs(seed: int = 0) -> dict:
    streams_of = jax.random.split(jax.random.key(seed), 19)
    hidden_in = draw_hidden_in(jax.random.fold_in(streams_of[18], 71), 0)
    recompute_pos = draw_recompute_pos(jax.random.fold_in(streams_of[18], 71), 0)
    req_lengths = draw_req_lengths(jax.random.fold_in(streams_of[18], 71), 0)
    stretch_order = draw_stretch_order(jax.random.fold_in(streams_of[18], 71), 0)
    page_table = draw_page_table(jax.random.fold_in(streams_of[18], 71), 0)
    cached_key_pool = scatter_about(streams_of[5], (N_REQ * POOL_SLOTS, STRETCH_TOKENS, KV_HEAD_COUNT * HEAD_SIZE), 1.0, 6.0, ((0, 16), (2, 8)))
    cached_value_pool = scatter_about(streams_of[6], (N_REQ * POOL_SLOTS, STRETCH_TOKENS, KV_HEAD_COUNT * HEAD_SIZE), 1.0, 6.0, ((0, 16), (2, 8)))
    attn_gain = jnp.clip(jnp.exp(jax.random.uniform(streams_of[7], (MODEL_WIDTH,), jnp.float32, math.log(0.5), math.log(2.0))), 0.5, 2.0)
    w_query = draw_w_query(jax.random.fold_in(streams_of[18], 71), 0)
    w_key = draw_w_key(jax.random.fold_in(streams_of[18], 71), 0)
    value_weight = scatter_about(streams_of[10], (MODEL_WIDTH, KV_HEAD_COUNT * HEAD_SIZE), MODEL_WIDTH ** -0.5, 0.125, ((1, 8),))
    query_gain = draw_query_gain(jax.random.fold_in(streams_of[18], 71), 0)
    key_norm_gain = draw_key_norm_gain(jax.random.fold_in(streams_of[18], 71), 0)
    w_out = scatter_about(streams_of[13], (QUERY_HEADS * HEAD_SIZE, MODEL_WIDTH), HEAD_SIZE ** -0.5, 0.5, ((0, 8),))
    ffn_gain = jnp.clip(jnp.exp(jax.random.uniform(streams_of[14], (MODEL_WIDTH,), jnp.float32, math.log(0.5), math.log(2.0))), 0.5, 2.0)
    w_gate = scatter_about(streams_of[15], (MODEL_WIDTH, FF), MODEL_WIDTH ** -0.5, 0.125, ((1, 8),))
    w_up = scatter_about(streams_of[16], (MODEL_WIDTH, FF), MODEL_WIDTH ** -0.5, 0.125, ((1, 8),))
    w_down = scatter_about(streams_of[17], (FF, MODEL_WIDTH), FF ** -0.5, 0.078125, ((0, 8),))
    return {"hidden_in": hidden_in, "recompute_pos": recompute_pos, "req_lengths": req_lengths, "stretch_order": stretch_order, "page_table": page_table, "cached_key_pool": cached_key_pool, "cached_value_pool": cached_value_pool, "attn_gain": attn_gain, "w_query": w_query, "w_key": w_key, "value_weight": value_weight, "query_gain": query_gain, "key_norm_gain": key_norm_gain, "w_out": w_out, "ffn_gain": ffn_gain, "w_gate": w_gate, "w_up": w_up, "w_down": w_down}


eps_norm = 1e-06
rope_base = 1000000.0
floor_score = -1e+30

def norm_rows(matrix, gain_vec):
    wide = matrix.astype(jnp.float32)
    factor = lax.rsqrt(lax.optimization_barrier(jnp.mean(wide * wide, axis=-1, keepdims=True)) + eps_norm)
    return wide * factor * gain_vec

def angles(position, head_size):
    half_dim = head_size // 2
    frequency = rope_base ** (-jnp.arange(half_dim, dtype=jnp.float32) / half_dim)
    return position.astype(jnp.float32)[..., None] * frequency

def rotate_halves(vector, angle_arg):
    half_dim = vector.shape[-1] // 2
    lower_half = vector[..., :half_dim]
    upper_half = vector[..., half_dim:]
    cosine = jnp.cos(angle_arg)
    sine_part = jnp.sin(angle_arg)
    return jnp.concatenate([lower_half * cosine - upper_half * sine_part, upper_half * cosine + lower_half * sine_part], axis=-1)

def rotary_heads(raw_proj, gain_vec, position, head_count):
    split_heads = raw_proj.reshape(raw_proj.shape[0], head_count, HEAD_SIZE)
    normed = norm_rows(split_heads, gain_vec)
    return rotate_halves(normed, angles(position, HEAD_SIZE)[:, None, :]).astype(jnp.bfloat16)

def block_stats(grouped_heads, gathered_stretch_keys, values, live_mask):
    scores = jnp.einsum('mhgd,khd->hgmk', grouped_heads.astype(jnp.float32), gathered_stretch_keys.astype(jnp.float32)) * HEAD_SIZE ** (-0.5)
    row_peak = lax.optimization_barrier(jnp.max(jnp.where(live_mask, scores, floor_score), axis=-1))
    weights = jnp.where(live_mask, jnp.exp(scores - row_peak[..., None]), 0.0)
    weight_sum = lax.optimization_barrier(jnp.sum(weights, axis=-1))
    rounded = lax.optimization_barrier(weights.astype(jnp.bfloat16))
    weighted = jnp.einsum('hgmk,khd->hgmd', rounded.astype(jnp.float32), values.astype(jnp.float32))
    return (weighted, row_peak, weight_sum)

def attend(query_tensor, position, length, gathered_stretch_keys, gathered_stretch_values, recomputed_keys, recomputed_values):
    count_of_rows = query_tensor.shape[0]
    grouped_heads = query_tensor.reshape(count_of_rows, KV_HEAD_COUNT, QUERY_HEADS // KV_HEAD_COUNT, HEAD_SIZE)
    key_place = jnp.arange(MOST_STRETCHES * STRETCH_TOKENS)
    live_mask = (key_place[None, :] < position[:, None]) & (key_place[None, :] // STRETCH_TOKENS < length)
    own_mask = position[None, :] <= position[:, None]
    cached_sum, cached_peak, cached_total = block_stats(grouped_heads, gathered_stretch_keys, gathered_stretch_values, live_mask)
    fresh_sum, fresh_peak, fresh_total = block_stats(grouped_heads, recomputed_keys, recomputed_values, own_mask)
    row_top = jnp.maximum(cached_peak, fresh_peak)
    cached_factor = jnp.exp(cached_peak - row_top)
    fresh_factor = jnp.exp(fresh_peak - row_top)
    weighted = cached_sum * cached_factor[..., None] + fresh_sum * fresh_factor[..., None]
    weight_sum = cached_total * cached_factor + fresh_total * fresh_factor
    result = weighted / weight_sum[..., None]
    return result.transpose(2, 0, 1, 3).astype(jnp.bfloat16).reshape(count_of_rows, QUERY_HEADS * HEAD_SIZE)

def group_sum(left_mat, right_mat):
    count_of_rows = left_mat.shape[0]
    terms = jnp.einsum('tnc,ncd->ntd', left_mat.reshape(count_of_rows, N_TP, -1).astype(jnp.float32), right_mat.reshape(N_TP, -1, right_mat.shape[1]).astype(jnp.float32))
    terms = lax.optimization_barrier(terms.astype(jnp.bfloat16))
    return lax.optimization_barrier(jnp.sum(terms.astype(jnp.float32), axis=0))

def reference(hidden_in, recompute_pos, req_lengths, stretch_order, page_table, cached_key_pool, cached_value_pool, attn_gain, w_query, w_key, value_weight, query_gain, key_norm_gain, w_out, ffn_gain, w_gate, w_up, w_down):
    normed = norm_rows(hidden_in, attn_gain).astype(jnp.bfloat16)
    query_raw = jnp.dot(normed, w_query, preferred_element_type=jnp.float32)
    unnormed_keys = jnp.dot(normed, w_key, preferred_element_type=jnp.float32)
    recomputed_values = jnp.dot(normed, value_weight, preferred_element_type=jnp.float32).astype(jnp.bfloat16)
    flattened_position = recompute_pos.reshape(TOKENS)
    queries = rotary_heads(query_raw, query_gain, flattened_position, QUERY_HEADS).reshape(REQUEST_COUNT, RECOMPUTE_TOKENS, QUERY_HEADS, HEAD_SIZE)
    recomputed_keys = rotary_heads(unnormed_keys, key_norm_gain, flattened_position, KV_HEAD_COUNT).reshape(REQUEST_COUNT, RECOMPUTE_TOKENS, KV_HEAD_COUNT, HEAD_SIZE)
    recomputed_values = recomputed_values.reshape(REQUEST_COUNT, RECOMPUTE_TOKENS, KV_HEAD_COUNT, HEAD_SIZE)
    pool_index = (page_table[0] * POOL_SLOTS + page_table[1]).astype(jnp.int32)
    position_shift_angle = angles(jnp.arange(MOST_STRETCHES) * STRETCH_TOKENS, HEAD_SIZE)[:, None, None, :]

    def one_request(packed):
        query_tensor, fkeys, fvalues, position, length, order = packed
        index_value = pool_index[order]
        gathered_stretch_keys = cached_key_pool[index_value].reshape(MOST_STRETCHES, STRETCH_TOKENS, KV_HEAD_COUNT, HEAD_SIZE).astype(jnp.float32)
        gathered_stretch_keys = rotate_halves(gathered_stretch_keys, position_shift_angle).astype(jnp.bfloat16).reshape(MOST_STRETCHES * STRETCH_TOKENS, KV_HEAD_COUNT, HEAD_SIZE)
        gathered_stretch_values = cached_value_pool[index_value].reshape(MOST_STRETCHES * STRETCH_TOKENS, KV_HEAD_COUNT, HEAD_SIZE)
        return attend(query_tensor, position, length, gathered_stretch_keys, gathered_stretch_values, fkeys, fvalues)
    attended = lax.map(one_request, (queries, recomputed_keys, recomputed_values, recompute_pos, req_lengths, stretch_order))
    attended = attended.reshape(TOKENS, QUERY_HEADS * HEAD_SIZE)
    attn_out = group_sum(attended, w_out)
    residual = (hidden_in.astype(jnp.float32) + attn_out).astype(jnp.bfloat16)
    normed_ffn = norm_rows(residual, ffn_gain).astype(jnp.bfloat16)
    gate_proj = jnp.dot(normed_ffn, w_gate, preferred_element_type=jnp.float32)
    up_proj = jnp.dot(normed_ffn, w_up, preferred_element_type=jnp.float32)
    hidden = (jax.nn.silu(gate_proj) * up_proj).astype(jnp.bfloat16)
    return (residual.astype(jnp.float32) + group_sum(hidden, w_down)).astype(jnp.bfloat16)
```

```python
import jax
import jax.numpy as jnp
from jax import lax
from jax.sharding import PartitionSpec as P

STRETCH_TOKENS = 512
MOST_STRETCHES = 32
REQ_DEV = 1
RECOMPUTE_TOKENS = 256


eps_norm = 1e-06
rope_base = 1000000.0
floor_score = -1e30


def norm_rows(matrix, gain_vec):
    wide = matrix.astype(jnp.float32)
    factor = lax.rsqrt(jnp.mean(wide * wide, axis=-1, keepdims=True) + eps_norm)
    return wide * factor * gain_vec


def angles(position, head_size):
    half_dim = head_size // 2
    frequency = rope_base ** (-jnp.arange(half_dim, dtype=jnp.float32) / half_dim)
    return position.astype(jnp.float32)[..., None] * frequency


def rotate_halves(vector, angle_arg):
    half_dim = vector.shape[-1] // 2
    lower_half = vector[..., :half_dim]
    upper_half = vector[..., half_dim:]
    cosine = jnp.cos(angle_arg)
    sine_part = jnp.sin(angle_arg)
    return jnp.concatenate(
        [
            lower_half * cosine - upper_half * sine_part,
            upper_half * cosine + lower_half * sine_part,
        ],
        axis=-1,
    )


def rotary_heads(raw_proj, gain_vec, position, head_count):
    head_size = gain_vec.shape[0]
    split_heads = raw_proj.reshape(raw_proj.shape[0], head_count, head_size)
    normed = norm_rows(split_heads, gain_vec)
    return rotate_halves(normed, angles(position, head_size)[:, None, :]).astype(jnp.bfloat16)


def block_stats(grouped_heads, gathered_stretch_keys, values, live_mask):
    count_of_rows, key_heads, groups, head_size = grouped_heads.shape
    scores = jnp.einsum(
        "mhgd,khd->hgmk", grouped_heads, gathered_stretch_keys, preferred_element_type=jnp.float32
    ) * head_size ** (-0.5)
    row_peak = jnp.max(jnp.where(live_mask, scores, floor_score), axis=-1)
    weights = jnp.where(live_mask, jnp.exp(scores - row_peak[..., None]), 0.0)
    weight_sum = jnp.sum(weights, axis=-1)
    weighted = jnp.einsum(
        "hgmk,khd->mhgd", weights.astype(jnp.bfloat16), values, preferred_element_type=jnp.float32
    )
    head_total = key_heads * groups
    return (
        weighted.reshape(count_of_rows, head_total, head_size),
        row_peak.transpose(2, 0, 1).reshape(count_of_rows, head_total),
        weight_sum.transpose(2, 0, 1).reshape(count_of_rows, head_total),
    )


def merge_stats(weighted, row_peak, weight_sum):
    row_top = jnp.max(row_peak, axis=0)
    factor = jnp.exp(row_peak - row_top[None])
    merged = jnp.sum(weighted * factor[..., None], axis=0)
    total_sum = jnp.sum(weight_sum * factor, axis=0)
    result = (merged / total_sum[..., None]).astype(jnp.bfloat16)
    return result.reshape(result.shape[0], -1)


def swiglu(rows_in, w_gate, w_up):
    gate_proj = jnp.dot(rows_in, w_gate, preferred_element_type=jnp.float32)
    up_proj = jnp.dot(rows_in, w_up, preferred_element_type=jnp.float32)
    return (jax.nn.silu(gate_proj) * up_proj).astype(jnp.bfloat16)


def reduce_rows(terms, tp_count):
    blocks = terms.reshape(tp_count, terms.shape[0] // tp_count, terms.shape[1])
    got = lax.all_to_all(blocks, "tp", 0, 0, tiled=False)
    return jnp.sum(got.astype(jnp.float32), axis=0)


def gather_rows(rows, tp_count):
    tp_index = lax.axis_index("tp")
    parts = [rows]
    for shift in range(1, tp_count):
        pairs = [(i, (i + shift) % tp_count) for i in range(tp_count)]
        parts.append(lax.ppermute(rows, "tp", pairs))
    stacked = jnp.stack(parts)
    source = (tp_index - jnp.arange(tp_count)) % tp_count
    ordered = jnp.take(stacked, jnp.argsort(source), axis=0)
    return ordered.reshape(tp_count * rows.shape[0], rows.shape[1])


def on_device(
    hidden_in,
    recompute_pos,
    req_lengths,
    stretch_order,
    page_table,
    cached_key_pool,
    cached_value_pool,
    attn_gain,
    w_query,
    w_key,
    value_weight,
    query_gain,
    key_norm_gain,
    w_out,
    ffn_gain,
    w_gate,
    w_up,
    w_down,
):
    req_count = lax.axis_size("req")
    my_index = lax.axis_index("req")
    head_size = query_gain.shape[0]
    query_heads = w_query.shape[1] // head_size
    key_heads = w_key.shape[1] // head_size
    groups = query_heads // key_heads
    count_of_rows = hidden_in.shape[0]
    local_reqs = REQ_DEV
    req_rows = RECOMPUTE_TOKENS
    entries = local_reqs * MOST_STRETCHES
    pair_cap = entries // req_count
    normed = norm_rows(hidden_in, attn_gain).astype(jnp.bfloat16)
    query_raw = jnp.dot(normed, w_query, preferred_element_type=jnp.float32)
    unnormed_keys = jnp.dot(normed, w_key, preferred_element_type=jnp.float32)
    recomputed_values = (
        jnp.dot(normed, value_weight, preferred_element_type=jnp.float32)
        .astype(jnp.bfloat16)
        .reshape(count_of_rows, key_heads, head_size)
    )
    my_positions = lax.dynamic_slice_in_dim(recompute_pos, my_index * local_reqs, local_reqs, 0)
    my_lengths = lax.dynamic_slice_in_dim(req_lengths, my_index * local_reqs, local_reqs, 0)
    flattened_position = my_positions.reshape(count_of_rows)
    queries = rotary_heads(query_raw, query_gain, flattened_position, query_heads)
    recomputed_keys = rotary_heads(unnormed_keys, key_norm_gain, flattened_position, key_heads)
    grouped_heads = queries.reshape(count_of_rows, key_heads, groups, head_size)
    row_owner = jnp.arange(count_of_rows) // req_rows
    own_mask = (row_owner[None, :] == row_owner[:, None]) & (
        flattened_position[None, :] <= flattened_position[:, None]
    )
    fresh_sum, fresh_peak, fresh_total = block_stats(
        grouped_heads, recomputed_keys, recomputed_values, own_mask
    )
    holder_table = page_table[0][stretch_order]
    slot_table = page_table[1][stretch_order]
    holder_hits = holder_table[:, :, None] == jnp.arange(req_count)[None, None, :]
    hit_counts = jnp.cumsum(holder_hits.astype(jnp.int32), axis=1)
    pair_rank = jnp.sum(jnp.where(holder_hits, hit_counts - 1, 0), axis=2)
    my_sends = (holder_table == my_index)[:, :, None] & (
        pair_rank[:, :, None] == jnp.arange(pair_cap)[None, None, :]
    )
    send_slot = jnp.sum(jnp.where(my_sends, slot_table[:, :, None], 0), axis=1)
    send_keys = cached_key_pool[send_slot]
    send_values = cached_value_pool[send_slot]
    got_keys, got_values = (
        lax.all_to_all(send_keys, "req", split_axis=0, concat_axis=0, tiled=True),
        lax.all_to_all(send_values, "req", split_axis=0, concat_axis=0, tiled=True),
    )
    my_holder = lax.dynamic_index_in_dim(holder_table, my_index, 0, keepdims=False)
    my_rank = lax.dynamic_index_in_dim(pair_rank, my_index, 0, keepdims=False)
    buffer = my_holder * pair_cap + my_rank
    position_shift_angle = angles(jnp.arange(MOST_STRETCHES) * STRETCH_TOKENS, head_size)[
        None, :, None, None, :
    ]
    gathered_stretch_keys = got_keys.reshape((req_count * pair_cap,) + got_keys.shape[2:])[buffer]
    gathered_stretch_keys = gathered_stretch_keys.reshape(
        local_reqs, MOST_STRETCHES, STRETCH_TOKENS, key_heads, head_size
    )
    gathered_stretch_keys = rotate_halves(
        gathered_stretch_keys.astype(jnp.float32), position_shift_angle
    ).astype(jnp.bfloat16)
    gathered_stretch_keys = gathered_stretch_keys.reshape(
        local_reqs, MOST_STRETCHES * STRETCH_TOKENS, key_heads, head_size
    )
    gathered_stretch_values = got_values.reshape((req_count * pair_cap,) + got_values.shape[2:])[
        buffer
    ]
    gathered_stretch_values = gathered_stretch_values.reshape(
        local_reqs, MOST_STRETCHES * STRETCH_TOKENS, key_heads, head_size
    )
    key_place = jnp.arange(MOST_STRETCHES * STRETCH_TOKENS)

    def cached_stats(packed):
        group_query, position, length, key_block, value_block = packed
        live_mask = (key_place[None, :] < position[:, None]) & (
            key_place[None, :] // STRETCH_TOKENS < length
        )
        return block_stats(group_query, key_block, value_block, live_mask)

    held_sum, held_peak, held_total = lax.map(
        cached_stats,
        (
            grouped_heads.reshape(local_reqs, req_rows, key_heads, groups, head_size),
            my_positions,
            my_lengths,
            gathered_stretch_keys,
            gathered_stretch_values,
        ),
    )
    attended = merge_stats(
        jnp.stack([held_sum.reshape(fresh_sum.shape), fresh_sum]),
        jnp.stack([held_peak.reshape(fresh_peak.shape), fresh_peak]),
        jnp.stack([held_total.reshape(fresh_total.shape), fresh_total]),
    )
    tp_count = lax.axis_size("tp")
    tp_index = lax.axis_index("tp")
    block_rows = count_of_rows // tp_count
    attn_terms = jnp.dot(attended, w_out, preferred_element_type=jnp.float32).astype(jnp.bfloat16)
    attn_out = reduce_rows(attn_terms, tp_count)
    my_hidden = lax.dynamic_slice_in_dim(hidden_in, tp_index * block_rows, block_rows, 0)
    residual = (my_hidden.astype(jnp.float32) + attn_out).astype(jnp.bfloat16)
    normed_ffn = gather_rows(norm_rows(residual, ffn_gain).astype(jnp.bfloat16), tp_count)
    hidden = swiglu(normed_ffn, w_gate, w_up)
    down_terms = jnp.dot(hidden, w_down, preferred_element_type=jnp.float32).astype(jnp.bfloat16)
    ffn_out = reduce_rows(down_terms, tp_count)
    return gather_rows((residual.astype(jnp.float32) + ffn_out).astype(jnp.bfloat16), tp_count)


def solution(mesh):
    return jax.shard_map(
        on_device,
        mesh=mesh,
        in_specs=(
            P("req", None),
            P(),
            P(),
            P(),
            P(),
            P("req", None, "tp"),
            P("req", None, "tp"),
            P(),
            P(None, "tp"),
            P(None, "tp"),
            P(None, "tp"),
            P(),
            P(),
            P("tp", None),
            P(),
            P(None, "tp"),
            P(None, "tp"),
            P("tp", None),
        ),
        out_specs=P("req", None),
        check_vma=False,
    )
```

```python
import jax
import jax.numpy as jnp
from jax import lax
from jax.sharding import PartitionSpec as P

STRETCH_TOKENS = 512
MOST_STRETCHES = 32
REQ_DEV = 1
RECOMPUTE_TOKENS = 256


eps_norm = 1e-06
rope_base = 1000000.0
floor_score = -1e30


def norm_rows(matrix, gain_vec):
    wide = matrix.astype(jnp.float32)
    factor = lax.rsqrt(jnp.mean(wide * wide, axis=-1, keepdims=True) + eps_norm)
    return wide * factor * gain_vec


def angles(position, head_size):
    half_dim = head_size // 2
    frequency = rope_base ** (-jnp.arange(half_dim, dtype=jnp.float32) / half_dim)
    return position.astype(jnp.float32)[..., None] * frequency


def rotate_halves(vector, angle_arg):
    half_dim = vector.shape[-1] // 2
    lower_half = vector[..., :half_dim]
    upper_half = vector[..., half_dim:]
    cosine = jnp.cos(angle_arg)
    sine_part = jnp.sin(angle_arg)
    return jnp.concatenate(
        [
            lower_half * cosine - upper_half * sine_part,
            upper_half * cosine + lower_half * sine_part,
        ],
        axis=-1,
    )


def rotary_heads(raw_proj, gain_vec, position, head_count):
    head_size = gain_vec.shape[0]
    split_heads = raw_proj.reshape(raw_proj.shape[0], head_count, head_size)
    normed = norm_rows(split_heads, gain_vec)
    return rotate_halves(normed, angles(position, head_size)[:, None, :]).astype(jnp.bfloat16)


def block_stats(grouped_heads, gathered_stretch_keys, values, live_mask):
    count_of_rows, key_heads, groups, head_size = grouped_heads.shape
    scores = jnp.einsum(
        "mhgd,khd->hgmk", grouped_heads, gathered_stretch_keys, preferred_element_type=jnp.float32
    ) * head_size ** (-0.5)
    row_peak = jnp.max(jnp.where(live_mask, scores, floor_score), axis=-1)
    weights = jnp.where(live_mask, jnp.exp(scores - row_peak[..., None]), 0.0)
    weight_sum = jnp.sum(weights, axis=-1)
    weighted = jnp.einsum(
        "hgmk,khd->mhgd", weights.astype(jnp.bfloat16), values, preferred_element_type=jnp.float32
    )
    head_total = key_heads * groups
    return (
        weighted.reshape(count_of_rows, head_total, head_size),
        row_peak.transpose(2, 0, 1).reshape(count_of_rows, head_total),
        weight_sum.transpose(2, 0, 1).reshape(count_of_rows, head_total),
    )


def merge_stats(weighted, row_peak, weight_sum):
    row_top = jnp.max(row_peak, axis=0)
    factor = jnp.exp(row_peak - row_top[None])
    merged = jnp.sum(weighted * factor[..., None], axis=0)
    total_sum = jnp.sum(weight_sum * factor, axis=0)
    result = (merged / total_sum[..., None]).astype(jnp.bfloat16)
    return result.reshape(result.shape[0], -1)


def swiglu(rows_in, w_gate, w_up):
    gate_proj = jnp.dot(rows_in, w_gate, preferred_element_type=jnp.float32)
    up_proj = jnp.dot(rows_in, w_up, preferred_element_type=jnp.float32)
    return (jax.nn.silu(gate_proj) * up_proj).astype(jnp.bfloat16)


def reduce_rows(terms, tp_count):
    blocks = terms.reshape(tp_count, terms.shape[0] // tp_count, terms.shape[1])
    got = lax.all_to_all(blocks, "tp", 0, 0, tiled=False)
    return jnp.sum(got.astype(jnp.float32), axis=0)


def gather_rows(rows, tp_count):
    tp_index = lax.axis_index("tp")
    parts = [rows]
    for shift in range(1, tp_count):
        pairs = [(i, (i + shift) % tp_count) for i in range(tp_count)]
        parts.append(lax.ppermute(rows, "tp", pairs))
    stacked = jnp.stack(parts)
    source = (tp_index - jnp.arange(tp_count)) % tp_count
    ordered = jnp.take(stacked, jnp.argsort(source), axis=0)
    return ordered.reshape(tp_count * rows.shape[0], rows.shape[1])


def on_device(
    hidden_in,
    recompute_pos,
    req_lengths,
    stretch_order,
    page_table,
    cached_key_pool,
    cached_value_pool,
    attn_gain,
    w_query,
    w_key,
    value_weight,
    query_gain,
    key_norm_gain,
    w_out,
    ffn_gain,
    w_gate,
    w_up,
    w_down,
):
    req_count = lax.axis_size("req")
    my_index = lax.axis_index("req")
    head_size = query_gain.shape[0]
    query_heads = w_query.shape[1] // head_size
    key_heads = w_key.shape[1] // head_size
    groups = query_heads // key_heads
    count_of_rows = hidden_in.shape[0]
    local_reqs = REQ_DEV
    req_rows = RECOMPUTE_TOKENS
    entries = local_reqs * MOST_STRETCHES
    pair_cap = entries // req_count
    normed = norm_rows(hidden_in, attn_gain).astype(jnp.bfloat16)
    query_raw = jnp.dot(normed, w_query, preferred_element_type=jnp.float32)
    unnormed_keys = jnp.dot(normed, w_key, preferred_element_type=jnp.float32)
    recomputed_values = (
        jnp.dot(normed, value_weight, preferred_element_type=jnp.float32)
        .astype(jnp.bfloat16)
        .reshape(count_of_rows, key_heads, head_size)
    )
    my_positions = lax.dynamic_slice_in_dim(recompute_pos, my_index * local_reqs, local_reqs, 0)
    my_lengths = lax.dynamic_slice_in_dim(req_lengths, my_index * local_reqs, local_reqs, 0)
    flattened_position = my_positions.reshape(count_of_rows)
    queries = rotary_heads(query_raw, query_gain, flattened_position, query_heads)
    recomputed_keys = rotary_heads(unnormed_keys, key_norm_gain, flattened_position, key_heads)
    grouped_heads = queries.reshape(count_of_rows, key_heads, groups, head_size)
    row_owner = jnp.arange(count_of_rows) // req_rows
    own_mask = (row_owner[None, :] == row_owner[:, None]) & (
        flattened_position[None, :] <= flattened_position[:, None]
    )
    fresh_sum, fresh_peak, fresh_total = block_stats(
        grouped_heads, recomputed_keys, recomputed_values, own_mask
    )
    holder_table = page_table[0][stretch_order]
    slot_table = page_table[1][stretch_order]
    holder_hits = holder_table[:, :, None] == jnp.arange(req_count)[None, None, :]
    hit_counts = jnp.cumsum(holder_hits.astype(jnp.int32), axis=1)
    pair_rank = jnp.sum(jnp.where(holder_hits, hit_counts - 1, 0), axis=2)
    my_sends = (holder_table == my_index)[:, :, None] & (
        pair_rank[:, :, None] == jnp.arange(pair_cap)[None, None, :]
    )
    send_slot = jnp.sum(jnp.where(my_sends, slot_table[:, :, None], 0), axis=1)
    send_place = jnp.sum(jnp.where(my_sends, jnp.arange(MOST_STRETCHES)[None, :, None], 0), axis=1)
    request_count = holder_table.shape[0]
    held_count = pair_cap * STRETCH_TOKENS
    held_keys = cached_key_pool[send_slot].reshape(
        request_count, pair_cap, STRETCH_TOKENS, key_heads, head_size
    )
    held_angle = angles(send_place * STRETCH_TOKENS, head_size)[:, :, None, None, :]
    held_keys = rotate_halves(held_keys.astype(jnp.float32), held_angle).astype(jnp.bfloat16)
    held_keys = held_keys.reshape(request_count, held_count, key_heads, head_size)
    held_values = cached_value_pool[send_slot].reshape(request_count, held_count, key_heads, head_size)
    query_copies = jnp.broadcast_to(queries[None], (req_count,) + queries.shape)
    all_queries = lax.all_to_all(query_copies, "req", 0, 0, tiled=False)
    all_queries = all_queries.reshape(request_count, req_rows, key_heads, groups, head_size)
    key_pos = (
        send_place[:, :, None] * STRETCH_TOKENS + jnp.arange(STRETCH_TOKENS)[None, None, :]
    ).reshape(request_count, held_count)
    key_ok = jnp.repeat(send_place < req_lengths[:, None], STRETCH_TOKENS, axis=1)
    live = key_ok[:, None, :] & (key_pos[:, None, :] < recompute_pos[:, :, None])
    scores = jnp.einsum(
        "rmhgd,rkhd->rhgmk", all_queries, held_keys, preferred_element_type=jnp.float32
    ) * head_size ** (-0.5)
    live = live[:, None, None]
    held_peak = jnp.max(jnp.where(live, scores, floor_score), axis=-1)
    weights = jnp.where(live, jnp.exp(scores - held_peak[..., None]), 0.0)
    held_total = jnp.sum(weights, axis=-1)
    held_sum = jnp.einsum(
        "rhgmk,rkhd->rmhgd", weights.astype(jnp.bfloat16), held_values, preferred_element_type=jnp.float32
    )
    got_sum = lax.all_to_all(held_sum, "req", 0, 0, tiled=False)
    got_stats = lax.all_to_all(jnp.stack([held_peak, held_total], axis=1), "req", 0, 0, tiled=False)
    head_total = key_heads * groups
    got_stats = got_stats.transpose(0, 1, 4, 2, 3).reshape(req_count, 2, count_of_rows, head_total)
    attended = merge_stats(
        jnp.concatenate([got_sum.reshape(req_count, count_of_rows, head_total, head_size), fresh_sum[None]]),
        jnp.concatenate([got_stats[:, 0], fresh_peak[None]]),
        jnp.concatenate([got_stats[:, 1], fresh_total[None]]),
    )
    tp_count = lax.axis_size("tp")
    tp_index = lax.axis_index("tp")
    block_rows = count_of_rows // tp_count
    attn_terms = jnp.dot(attended, w_out, preferred_element_type=jnp.float32).astype(jnp.bfloat16)
    attn_out = reduce_rows(attn_terms, tp_count)
    my_hidden = lax.dynamic_slice_in_dim(hidden_in, tp_index * block_rows, block_rows, 0)
    residual = (my_hidden.astype(jnp.float32) + attn_out).astype(jnp.bfloat16)
    normed_ffn = gather_rows(norm_rows(residual, ffn_gain).astype(jnp.bfloat16), tp_count)
    hidden = swiglu(normed_ffn, w_gate, w_up)
    down_terms = jnp.dot(hidden, w_down, preferred_element_type=jnp.float32).astype(jnp.bfloat16)
    ffn_out = reduce_rows(down_terms, tp_count)
    return gather_rows((residual.astype(jnp.float32) + ffn_out).astype(jnp.bfloat16), tp_count)


def solution(mesh):
    return jax.shard_map(
        on_device,
        mesh=mesh,
        in_specs=(
            P("req", None),
            P(),
            P(),
            P(),
            P(),
            P("req", None, "tp"),
            P("req", None, "tp"),
            P(),
            P(None, "tp"),
            P(None, "tp"),
            P(None, "tp"),
            P(),
            P(),
            P("tp", None),
            P(),
            P(None, "tp"),
            P(None, "tp"),
            P("tp", None),
        ),
        out_specs=P("req", None),
        check_vma=False,
    )
```

```python
import jax
import jax.numpy as jnp
from jax import lax
from jax.sharding import PartitionSpec as P
from jax.experimental import pallas as pl
from jax.experimental.pallas import tpu as pltpu

STRETCH_TOKENS = 512
MOST_STRETCHES = 32
REQ_DEV = 1
RECOMPUTE_TOKENS = 256


eps_norm = 1e-06
rope_base = 1000000.0
floor_score = -1e30


def norm_rows(matrix, gain_vec):
    wide = matrix.astype(jnp.float32)
    factor = lax.rsqrt(jnp.mean(wide * wide, axis=-1, keepdims=True) + eps_norm)
    return wide * factor * gain_vec


def angles(position, head_size):
    half_dim = head_size // 2
    frequency = rope_base ** (-jnp.arange(half_dim, dtype=jnp.float32) / half_dim)
    return position.astype(jnp.float32)[..., None] * frequency


def rotate_halves(vector, angle_arg):
    half_dim = vector.shape[-1] // 2
    lower_half = vector[..., :half_dim]
    upper_half = vector[..., half_dim:]
    cosine = jnp.cos(angle_arg)
    sine_part = jnp.sin(angle_arg)
    return jnp.concatenate(
        [
            lower_half * cosine - upper_half * sine_part,
            upper_half * cosine + lower_half * sine_part,
        ],
        axis=-1,
    )


def rotary_heads(raw_proj, gain_vec, position, head_count):
    head_size = gain_vec.shape[0]
    split_heads = raw_proj.reshape(raw_proj.shape[0], head_count, head_size)
    normed = norm_rows(split_heads, gain_vec)
    return rotate_halves(normed, angles(position, head_size)[:, None, :]).astype(jnp.bfloat16)


def block_stats(grouped_heads, gathered_stretch_keys, values, live_mask):
    count_of_rows, key_heads, groups, head_size = grouped_heads.shape
    scores = jnp.einsum(
        "mhgd,khd->hgmk", grouped_heads, gathered_stretch_keys, preferred_element_type=jnp.float32
    ) * head_size ** (-0.5)
    row_peak = jnp.max(jnp.where(live_mask, scores, floor_score), axis=-1)
    weights = jnp.where(live_mask, jnp.exp(scores - row_peak[..., None]), 0.0)
    weight_sum = jnp.sum(weights, axis=-1)
    weighted = jnp.einsum(
        "hgmk,khd->mhgd", weights.astype(jnp.bfloat16), values, preferred_element_type=jnp.float32
    )
    head_total = key_heads * groups
    return (
        weighted.reshape(count_of_rows, head_total, head_size),
        row_peak.transpose(2, 0, 1).reshape(count_of_rows, head_total),
        weight_sum.transpose(2, 0, 1).reshape(count_of_rows, head_total),
    )


def merge_stats(weighted, row_peak, weight_sum):
    row_top = jnp.max(row_peak, axis=0)
    factor = jnp.exp(row_peak - row_top[None])
    merged = jnp.sum(weighted * factor[..., None], axis=0)
    total_sum = jnp.sum(weight_sum * factor, axis=0)
    result = (merged / total_sum[..., None]).astype(jnp.bfloat16)
    return result.reshape(result.shape[0], -1)


def swiglu(rows_in, w_gate, w_up):
    gate_proj = jnp.dot(rows_in, w_gate, preferred_element_type=jnp.float32)
    up_proj = jnp.dot(rows_in, w_up, preferred_element_type=jnp.float32)
    return (jax.nn.silu(gate_proj) * up_proj).astype(jnp.bfloat16)


far_position = 1 << 30


def held_block_kernel(slot_ref, q_ref, k0_ref, k1_ref, v0_ref, v1_ref, cos_ref, sin_ref, qpos_ref, kpos_ref, sum_ref, stat_ref):
    query = q_ref[0]
    query_pos = qpos_ref[0]
    scale = (query.shape[-1]) ** (-0.5)

    def scores_of(k_ref, j):
        key = k_ref[0].astype(jnp.float32)
        half = key.shape[-1] // 2
        rotated = (key * cos_ref[0, j] + pltpu.roll(key, half, 1) * sin_ref[0, j]).astype(jnp.bfloat16)
        raw = lax.dot_general(query, rotated, (((1,), (1,)), ((), ())), preferred_element_type=jnp.float32)
        return raw * scale, kpos_ref[0, j] < query_pos

    s0, l0 = scores_of(k0_ref, 0)
    s1, l1 = scores_of(k1_ref, 1)
    peak = jnp.maximum(
        jnp.max(jnp.where(l0, s0, floor_score), axis=1, keepdims=True),
        jnp.max(jnp.where(l1, s1, floor_score), axis=1, keepdims=True),
    )
    w0 = jnp.where(l0, jnp.exp(s0 - peak), 0.0)
    w1 = jnp.where(l1, jnp.exp(s1 - peak), 0.0)
    total = jnp.sum(w0, axis=1, keepdims=True) + jnp.sum(w1, axis=1, keepdims=True)
    sum_ref[0] = jnp.dot(w0.astype(jnp.bfloat16), v0_ref[0], preferred_element_type=jnp.float32) + jnp.dot(
        w1.astype(jnp.bfloat16), v1_ref[0], preferred_element_type=jnp.float32
    )
    stat_ref[0] = jnp.concatenate([peak, total], axis=1)


def held_blocks(slots, queries, key_pool, value_pool, cos_table, sin_table, query_pos, key_pos):
    requests, rows, head_size = queries.shape
    stretch = key_pool.shape[1]

    def pool_spec(j):
        return pl.BlockSpec((1, stretch, head_size), lambda r, slot: (slot[2 * r + j], 0, 0))

    grid_spec = pltpu.PrefetchScalarGridSpec(
        num_scalar_prefetch=1,
        grid=(requests,),
        in_specs=[
            pl.BlockSpec((1, rows, head_size), lambda r, slot: (r, 0, 0)),
            pool_spec(0),
            pool_spec(1),
            pool_spec(0),
            pool_spec(1),
            pl.BlockSpec((1, 2, 1, head_size), lambda r, slot: (r, 0, 0, 0)),
            pl.BlockSpec((1, 2, 1, head_size), lambda r, slot: (r, 0, 0, 0)),
            pl.BlockSpec((1, rows, 1), lambda r, slot: (r, 0, 0)),
            pl.BlockSpec((1, 2, 1, stretch), lambda r, slot: (r, 0, 0, 0)),
        ],
        out_specs=[
            pl.BlockSpec((1, rows, head_size), lambda r, slot: (r, 0, 0)),
            pl.BlockSpec((1, rows, 2), lambda r, slot: (r, 0, 0)),
        ],
    )
    return pl.pallas_call(
        held_block_kernel,
        grid_spec=grid_spec,
        out_shape=[
            jax.ShapeDtypeStruct((requests, rows, head_size), jnp.float32),
            jax.ShapeDtypeStruct((requests, rows, 2), jnp.float32),
        ],
        compiler_params=pltpu.CompilerParams(dimension_semantics=("arbitrary",)),
    )(slots, queries, key_pool, key_pool, value_pool, value_pool, cos_table, sin_table, query_pos, key_pos)


def reduce_rows(terms, tp_count):
    blocks = terms.reshape(tp_count, terms.shape[0] // tp_count, terms.shape[1])
    got = lax.all_to_all(blocks, "tp", 0, 0, tiled=False)
    return jnp.sum(got.astype(jnp.float32), axis=0)


def gather_rows(rows, tp_count):
    tp_index = lax.axis_index("tp")
    parts = [rows]
    for shift in range(1, tp_count):
        pairs = [(i, (i + shift) % tp_count) for i in range(tp_count)]
        parts.append(lax.ppermute(rows, "tp", pairs))
    stacked = jnp.stack(parts)
    source = (tp_index - jnp.arange(tp_count)) % tp_count
    ordered = jnp.take(stacked, jnp.argsort(source), axis=0)
    return ordered.reshape(tp_count * rows.shape[0], rows.shape[1])


def on_device(
    hidden_in,
    recompute_pos,
    req_lengths,
    stretch_order,
    page_table,
    cached_key_pool,
    cached_value_pool,
    attn_gain,
    w_query,
    w_key,
    value_weight,
    query_gain,
    key_norm_gain,
    w_out,
    ffn_gain,
    w_gate,
    w_up,
    w_down,
):
    req_count = lax.axis_size("req")
    my_index = lax.axis_index("req")
    head_size = query_gain.shape[0]
    query_heads = w_query.shape[1] // head_size
    key_heads = w_key.shape[1] // head_size
    groups = query_heads // key_heads
    count_of_rows = hidden_in.shape[0]
    local_reqs = REQ_DEV
    req_rows = RECOMPUTE_TOKENS
    entries = local_reqs * MOST_STRETCHES
    pair_cap = entries // req_count
    normed = norm_rows(hidden_in, attn_gain).astype(jnp.bfloat16)
    query_raw = jnp.dot(normed, w_query, preferred_element_type=jnp.float32)
    unnormed_keys = jnp.dot(normed, w_key, preferred_element_type=jnp.float32)
    recomputed_values = (
        jnp.dot(normed, value_weight, preferred_element_type=jnp.float32)
        .astype(jnp.bfloat16)
        .reshape(count_of_rows, key_heads, head_size)
    )
    my_positions = lax.dynamic_slice_in_dim(recompute_pos, my_index * local_reqs, local_reqs, 0)
    my_lengths = lax.dynamic_slice_in_dim(req_lengths, my_index * local_reqs, local_reqs, 0)
    flattened_position = my_positions.reshape(count_of_rows)
    queries = rotary_heads(query_raw, query_gain, flattened_position, query_heads)
    recomputed_keys = rotary_heads(unnormed_keys, key_norm_gain, flattened_position, key_heads)
    grouped_heads = queries.reshape(count_of_rows, key_heads, groups, head_size)
    row_owner = jnp.arange(count_of_rows) // req_rows
    own_mask = (row_owner[None, :] == row_owner[:, None]) & (
        flattened_position[None, :] <= flattened_position[:, None]
    )
    fresh_sum, fresh_peak, fresh_total = block_stats(
        grouped_heads, recomputed_keys, recomputed_values, own_mask
    )
    holder_table = page_table[0][stretch_order]
    slot_table = page_table[1][stretch_order]
    holder_hits = holder_table[:, :, None] == jnp.arange(req_count)[None, None, :]
    hit_counts = jnp.cumsum(holder_hits.astype(jnp.int32), axis=1)
    pair_rank = jnp.sum(jnp.where(holder_hits, hit_counts - 1, 0), axis=2)
    my_sends = (holder_table == my_index)[:, :, None] & (
        pair_rank[:, :, None] == jnp.arange(pair_cap)[None, None, :]
    )
    send_slot = jnp.sum(jnp.where(my_sends, slot_table[:, :, None], 0), axis=1)
    send_place = jnp.sum(jnp.where(my_sends, jnp.arange(MOST_STRETCHES)[None, :, None], 0), axis=1)
    request_count = holder_table.shape[0]
    pool_slots = cached_key_pool.shape[0]
    slots = jnp.clip(send_slot, 0, pool_slots - 1).reshape(request_count * pair_cap).astype(jnp.int32)
    held_angle = angles(send_place * STRETCH_TOKENS, head_size)
    cos_table = jnp.cos(held_angle)
    sin_table = jnp.sin(held_angle)
    cos_table = jnp.concatenate([cos_table, cos_table], axis=-1)[:, :, None, :]
    sin_table = jnp.concatenate([-sin_table, sin_table], axis=-1)[:, :, None, :]
    query_copies = jnp.broadcast_to(queries[None], (req_count,) + queries.shape)
    all_queries = lax.all_to_all(query_copies, "req", 0, 0, tiled=False)
    all_queries = all_queries.reshape(request_count, req_rows * groups, head_size)
    query_pos = jnp.repeat(recompute_pos, groups, axis=1)[:, :, None]
    key_pos = jnp.where(
        (send_place < req_lengths[:, None])[:, :, None],
        send_place[:, :, None] * STRETCH_TOKENS + jnp.arange(STRETCH_TOKENS)[None, None, :],
        far_position,
    )[:, :, None, :]
    held_sum, held_stats = held_blocks(
        slots, all_queries, cached_key_pool, cached_value_pool, cos_table, sin_table, query_pos, key_pos
    )
    got_sum = lax.all_to_all(held_sum, "req", 0, 0, tiled=False)
    got_stats = lax.all_to_all(held_stats, "req", 0, 0, tiled=False)
    head_total = key_heads * groups
    got_stats = got_stats.reshape(req_count, count_of_rows, head_total, 2)
    attended = merge_stats(
        jnp.concatenate([got_sum.reshape(req_count, count_of_rows, head_total, head_size), fresh_sum[None]]),
        jnp.concatenate([got_stats[..., 0], fresh_peak[None]]),
        jnp.concatenate([got_stats[..., 1], fresh_total[None]]),
    )
    tp_count = lax.axis_size("tp")
    tp_index = lax.axis_index("tp")
    block_rows = count_of_rows // tp_count
    attn_terms = jnp.dot(attended, w_out, preferred_element_type=jnp.float32).astype(jnp.bfloat16)
    attn_out = reduce_rows(attn_terms, tp_count)
    my_hidden = lax.dynamic_slice_in_dim(hidden_in, tp_index * block_rows, block_rows, 0)
    residual = (my_hidden.astype(jnp.float32) + attn_out).astype(jnp.bfloat16)
    normed_ffn = gather_rows(norm_rows(residual, ffn_gain).astype(jnp.bfloat16), tp_count)
    hidden = swiglu(normed_ffn, w_gate, w_up)
    down_terms = jnp.dot(hidden, w_down, preferred_element_type=jnp.float32).astype(jnp.bfloat16)
    ffn_out = reduce_rows(down_terms, tp_count)
    return gather_rows((residual.astype(jnp.float32) + ffn_out).astype(jnp.bfloat16), tp_count)


def solution(mesh):
    return jax.shard_map(
        on_device,
        mesh=mesh,
        in_specs=(
            P("req", None),
            P(),
            P(),
            P(),
            P(),
            P("req", None, "tp"),
            P("req", None, "tp"),
            P(),
            P(None, "tp"),
            P(None, "tp"),
            P(None, "tp"),
            P(),
            P(),
            P("tp", None),
            P(),
            P(None, "tp"),
            P(None, "tp"),
            P("tp", None),
        ),
        out_specs=P("req", None),
        check_vma=False,
    )
```

```python
import jax
import jax.numpy as jnp
from jax import lax
from jax.sharding import PartitionSpec as P
from jax.experimental import pallas as pl
from jax.experimental.pallas import tpu as pltpu

STRETCH_TOKENS = 512
MOST_STRETCHES = 32
REQ_DEV = 1
RECOMPUTE_TOKENS = 256


eps_norm = 1e-06
rope_base = 1000000.0
floor_score = -1e30


def norm_rows(matrix, gain_vec):
    wide = matrix.astype(jnp.float32)
    factor = lax.rsqrt(jnp.mean(wide * wide, axis=-1, keepdims=True) + eps_norm)
    return wide * factor * gain_vec


def angles(position, head_size):
    half_dim = head_size // 2
    frequency = rope_base ** (-jnp.arange(half_dim, dtype=jnp.float32) / half_dim)
    return position.astype(jnp.float32)[..., None] * frequency


def rotate_halves(vector, angle_arg):
    half_dim = vector.shape[-1] // 2
    lower_half = vector[..., :half_dim]
    upper_half = vector[..., half_dim:]
    cosine = jnp.cos(angle_arg)
    sine_part = jnp.sin(angle_arg)
    return jnp.concatenate(
        [
            lower_half * cosine - upper_half * sine_part,
            upper_half * cosine + lower_half * sine_part,
        ],
        axis=-1,
    )


def rotary_heads(raw_proj, gain_vec, position, head_count):
    head_size = gain_vec.shape[0]
    split_heads = raw_proj.reshape(raw_proj.shape[0], head_count, head_size)
    normed = norm_rows(split_heads, gain_vec)
    return rotate_halves(normed, angles(position, head_size)[:, None, :]).astype(jnp.bfloat16)


def block_stats(grouped_heads, gathered_stretch_keys, values, live_mask):
    count_of_rows, key_heads, groups, head_size = grouped_heads.shape
    scores = jnp.einsum(
        "mhgd,khd->hgmk", grouped_heads, gathered_stretch_keys, preferred_element_type=jnp.float32
    ) * head_size ** (-0.5)
    row_peak = jnp.max(jnp.where(live_mask, scores, floor_score), axis=-1)
    weights = jnp.where(live_mask, jnp.exp(scores - row_peak[..., None]), 0.0)
    weight_sum = jnp.sum(weights, axis=-1)
    weighted = jnp.einsum(
        "hgmk,khd->mhgd", weights.astype(jnp.bfloat16), values, preferred_element_type=jnp.float32
    )
    head_total = key_heads * groups
    return (
        weighted.reshape(count_of_rows, head_total, head_size),
        row_peak.transpose(2, 0, 1).reshape(count_of_rows, head_total),
        weight_sum.transpose(2, 0, 1).reshape(count_of_rows, head_total),
    )


def merge_stats(weighted, row_peak, weight_sum):
    row_top = jnp.max(row_peak, axis=0)
    factor = jnp.exp(row_peak - row_top[None])
    merged = jnp.sum(weighted * factor[..., None], axis=0)
    total_sum = jnp.sum(weight_sum * factor, axis=0)
    result = (merged / total_sum[..., None]).astype(jnp.bfloat16)
    return result.reshape(result.shape[0], -1)


def swiglu(rows_in, w_gate, w_up):
    gate_proj = jnp.dot(rows_in, w_gate, preferred_element_type=jnp.float32)
    up_proj = jnp.dot(rows_in, w_up, preferred_element_type=jnp.float32)
    return (jax.nn.silu(gate_proj) * up_proj).astype(jnp.bfloat16)


far_position = 1 << 30


def held_block_kernel(slot_ref, alive_ref, q_ref, k0_ref, k1_ref, v0_ref, v1_ref, cos_ref, sin_ref, qpos_ref, kpos_ref, sum_ref, stat_ref):
    step = pl.program_id(0)
    key_refs = (k0_ref, k1_ref)
    value_refs = (v0_ref, v1_ref)

    def run(parts):
        query = q_ref[0]
        query_pos = qpos_ref[0]
        scale = (query.shape[-1]) ** (-0.5)
        masked = []
        for j in parts:
            key = key_refs[j][0].astype(jnp.float32)
            half = key.shape[-1] // 2
            rotated = (key * cos_ref[0, j] + pltpu.roll(key, half, 1) * sin_ref[0, j]).astype(jnp.bfloat16)
            raw = lax.dot_general(query, rotated, (((1,), (1,)), ((), ())), preferred_element_type=jnp.float32)
            masked.append(jnp.where(kpos_ref[0, j] < query_pos, raw * scale, floor_score))
        peak = jnp.max(masked[0], axis=1, keepdims=True)
        for extra in masked[1:]:
            peak = jnp.maximum(peak, jnp.max(extra, axis=1, keepdims=True))
        safe_peak = jnp.where(peak == floor_score, 0.0, peak)
        total = None
        weighted = None
        for j, block in zip(parts, masked):
            w = jnp.exp(block - safe_peak)
            part_total = jnp.sum(w, axis=1, keepdims=True)
            part_sum = jnp.dot(w.astype(jnp.bfloat16), value_refs[j][0], preferred_element_type=jnp.float32)
            total = part_total if total is None else total + part_total
            weighted = part_sum if weighted is None else weighted + part_sum
        sum_ref[0] = weighted
        stat_ref[0] = jnp.concatenate([peak, total], axis=1)

    live0 = alive_ref[2 * step] > 0
    live1 = alive_ref[2 * step + 1] > 0
    pl.when(live0 & live1)(lambda: run((0, 1)))
    pl.when(live0 & jnp.logical_not(live1))(lambda: run((0,)))
    pl.when(jnp.logical_not(live0) & live1)(lambda: run((1,)))

    @pl.when(jnp.logical_not(live0) & jnp.logical_not(live1))
    def _():
        sum_ref[0] = jnp.zeros(sum_ref.shape[1:], jnp.float32)
        rows = stat_ref.shape[1]
        stat_ref[0] = jnp.concatenate(
            [jnp.full((rows, 1), floor_score, jnp.float32), jnp.zeros((rows, 1), jnp.float32)], axis=1
        )


def held_blocks(slots, alive, queries, key_pool, value_pool, cos_table, sin_table, query_pos, key_pos):
    requests, rows, head_size = queries.shape
    stretch = key_pool.shape[1]

    def pool_spec(j):
        return pl.BlockSpec((1, stretch, head_size), lambda r, slot, alive: (slot[2 * r + j], 0, 0))

    grid_spec = pltpu.PrefetchScalarGridSpec(
        num_scalar_prefetch=2,
        grid=(requests,),
        in_specs=[
            pl.BlockSpec((1, rows, head_size), lambda r, slot, alive: (r, 0, 0)),
            pool_spec(0),
            pool_spec(1),
            pool_spec(0),
            pool_spec(1),
            pl.BlockSpec((1, 2, 1, head_size), lambda r, slot, alive: (r, 0, 0, 0)),
            pl.BlockSpec((1, 2, 1, head_size), lambda r, slot, alive: (r, 0, 0, 0)),
            pl.BlockSpec((1, rows, 1), lambda r, slot, alive: (r, 0, 0)),
            pl.BlockSpec((1, 2, 1, stretch), lambda r, slot, alive: (r, 0, 0, 0)),
        ],
        out_specs=[
            pl.BlockSpec((1, rows, head_size), lambda r, slot, alive: (r, 0, 0)),
            pl.BlockSpec((1, rows, 2), lambda r, slot, alive: (r, 0, 0)),
        ],
    )
    return pl.pallas_call(
        held_block_kernel,
        grid_spec=grid_spec,
        out_shape=[
            jax.ShapeDtypeStruct((requests, rows, head_size), jnp.float32),
            jax.ShapeDtypeStruct((requests, rows, 2), jnp.float32),
        ],
        compiler_params=pltpu.CompilerParams(dimension_semantics=("arbitrary",)),
    )(slots, alive, queries, key_pool, key_pool, value_pool, value_pool, cos_table, sin_table, query_pos, key_pos)


def reduce_rows(terms, tp_count):
    blocks = terms.reshape(tp_count, terms.shape[0] // tp_count, terms.shape[1])
    got = lax.all_to_all(blocks, "tp", 0, 0, tiled=False)
    return jnp.sum(got.astype(jnp.float32), axis=0)


def gather_rows(rows, tp_count):
    tp_index = lax.axis_index("tp")
    parts = [rows]
    for shift in range(1, tp_count):
        pairs = [(i, (i + shift) % tp_count) for i in range(tp_count)]
        parts.append(lax.ppermute(rows, "tp", pairs))
    stacked = jnp.stack(parts)
    source = (tp_index - jnp.arange(tp_count)) % tp_count
    ordered = jnp.take(stacked, jnp.argsort(source), axis=0)
    return ordered.reshape(tp_count * rows.shape[0], rows.shape[1])


def on_device(
    hidden_in,
    recompute_pos,
    req_lengths,
    stretch_order,
    page_table,
    cached_key_pool,
    cached_value_pool,
    attn_gain,
    w_query,
    w_key,
    value_weight,
    query_gain,
    key_norm_gain,
    w_out,
    ffn_gain,
    w_gate,
    w_up,
    w_down,
):
    req_count = lax.axis_size("req")
    my_index = lax.axis_index("req")
    head_size = query_gain.shape[0]
    query_heads = w_query.shape[1] // head_size
    key_heads = w_key.shape[1] // head_size
    groups = query_heads // key_heads
    count_of_rows = hidden_in.shape[0]
    local_reqs = REQ_DEV
    req_rows = RECOMPUTE_TOKENS
    entries = local_reqs * MOST_STRETCHES
    pair_cap = entries // req_count
    normed = norm_rows(hidden_in, attn_gain).astype(jnp.bfloat16)
    query_raw = jnp.dot(normed, w_query, preferred_element_type=jnp.float32)
    unnormed_keys = jnp.dot(normed, w_key, preferred_element_type=jnp.float32)
    recomputed_values = (
        jnp.dot(normed, value_weight, preferred_element_type=jnp.float32)
        .astype(jnp.bfloat16)
        .reshape(count_of_rows, key_heads, head_size)
    )
    my_positions = lax.dynamic_slice_in_dim(recompute_pos, my_index * local_reqs, local_reqs, 0)
    my_lengths = lax.dynamic_slice_in_dim(req_lengths, my_index * local_reqs, local_reqs, 0)
    flattened_position = my_positions.reshape(count_of_rows)
    queries = rotary_heads(query_raw, query_gain, flattened_position, query_heads)
    recomputed_keys = rotary_heads(unnormed_keys, key_norm_gain, flattened_position, key_heads)
    grouped_heads = queries.reshape(count_of_rows, key_heads, groups, head_size)
    row_owner = jnp.arange(count_of_rows) // req_rows
    own_mask = (row_owner[None, :] == row_owner[:, None]) & (
        flattened_position[None, :] <= flattened_position[:, None]
    )
    fresh_sum, fresh_peak, fresh_total = block_stats(
        grouped_heads, recomputed_keys, recomputed_values, own_mask
    )
    holder_table = page_table[0][stretch_order]
    slot_table = page_table[1][stretch_order]
    holder_hits = holder_table[:, :, None] == jnp.arange(req_count)[None, None, :]
    hit_counts = jnp.cumsum(holder_hits.astype(jnp.int32), axis=1)
    pair_rank = jnp.sum(jnp.where(holder_hits, hit_counts - 1, 0), axis=2)
    my_sends = (holder_table == my_index)[:, :, None] & (
        pair_rank[:, :, None] == jnp.arange(pair_cap)[None, None, :]
    )
    send_slot = jnp.sum(jnp.where(my_sends, slot_table[:, :, None], 0), axis=1)
    send_place = jnp.sum(jnp.where(my_sends, jnp.arange(MOST_STRETCHES)[None, :, None], 0), axis=1)
    request_count = holder_table.shape[0]
    pool_slots = cached_key_pool.shape[0]
    slots = jnp.clip(send_slot, 0, pool_slots - 1).reshape(request_count * pair_cap).astype(jnp.int32)
    held_angle = angles(send_place * STRETCH_TOKENS, head_size)
    cos_table = jnp.cos(held_angle)
    sin_table = jnp.sin(held_angle)
    cos_table = jnp.concatenate([cos_table, cos_table], axis=-1)[:, :, None, :]
    sin_table = jnp.concatenate([-sin_table, sin_table], axis=-1)[:, :, None, :]
    query_copies = jnp.broadcast_to(queries[None], (req_count,) + queries.shape)
    all_queries = lax.all_to_all(query_copies, "req", 0, 0, tiled=False)
    all_queries = all_queries.reshape(request_count, req_rows * groups, head_size)
    query_pos = jnp.repeat(recompute_pos, groups, axis=1)[:, :, None]
    key_pos = jnp.where(
        (send_place < req_lengths[:, None])[:, :, None],
        send_place[:, :, None] * STRETCH_TOKENS + jnp.arange(STRETCH_TOKENS)[None, None, :],
        far_position,
    )[:, :, None, :]
    alive = (send_place < req_lengths[:, None]).reshape(request_count * pair_cap).astype(jnp.int32)
    held_sum, held_stats = held_blocks(
        slots, alive, all_queries, cached_key_pool, cached_value_pool, cos_table, sin_table, query_pos, key_pos
    )
    sum_width = req_rows * groups * head_size
    payload = jnp.concatenate(
        [held_sum.reshape(request_count, sum_width), held_stats.reshape(request_count, req_rows * groups * 2)], axis=1
    )
    got = lax.all_to_all(payload, "req", 0, 0, tiled=False)
    got_sum = got[:, :sum_width]
    head_total = key_heads * groups
    got_stats = got[:, sum_width:].reshape(req_count, count_of_rows, head_total, 2)
    attended = merge_stats(
        jnp.concatenate([got_sum.reshape(req_count, count_of_rows, head_total, head_size), fresh_sum[None]]),
        jnp.concatenate([got_stats[..., 0], fresh_peak[None]]),
        jnp.concatenate([got_stats[..., 1], fresh_total[None]]),
    )
    tp_count = lax.axis_size("tp")
    tp_index = lax.axis_index("tp")
    block_rows = count_of_rows // tp_count
    attn_terms = jnp.dot(attended, w_out, preferred_element_type=jnp.float32).astype(jnp.bfloat16)
    attn_out = reduce_rows(attn_terms, tp_count)
    my_hidden = lax.dynamic_slice_in_dim(hidden_in, tp_index * block_rows, block_rows, 0)
    residual = (my_hidden.astype(jnp.float32) + attn_out).astype(jnp.bfloat16)
    normed_ffn = gather_rows(norm_rows(residual, ffn_gain).astype(jnp.bfloat16), tp_count)
    hidden = swiglu(normed_ffn, w_gate, w_up)
    down_terms = jnp.dot(hidden, w_down, preferred_element_type=jnp.float32).astype(jnp.bfloat16)
    ffn_out = reduce_rows(down_terms, tp_count)
    return gather_rows((residual.astype(jnp.float32) + ffn_out).astype(jnp.bfloat16), tp_count)


def solution(mesh):
    return jax.shard_map(
        on_device,
        mesh=mesh,
        in_specs=(
            P("req", None),
            P(),
            P(),
            P(),
            P(),
            P("req", None, "tp"),
            P("req", None, "tp"),
            P(),
            P(None, "tp"),
            P(None, "tp"),
            P(None, "tp"),
            P(),
            P(),
            P("tp", None),
            P(),
            P(None, "tp"),
            P(None, "tp"),
            P("tp", None),
        ),
        out_specs=P("req", None),
        check_vma=False,
    )
```

```python
import jax
import jax.numpy as jnp
from jax import lax
from jax.sharding import PartitionSpec as P
from jax.experimental import pallas as pl
from jax.experimental.pallas import tpu as pltpu

STRETCH_TOKENS = 512
MOST_STRETCHES = 32
REQ_DEV = 1
RECOMPUTE_TOKENS = 256


eps_norm = 1e-06
rope_base = 1000000.0
floor_score = -1e30


def norm_rows(matrix, gain_vec):
    wide = matrix.astype(jnp.float32)
    factor = lax.rsqrt(jnp.mean(wide * wide, axis=-1, keepdims=True) + eps_norm)
    return wide * factor * gain_vec


def angles(position, head_size):
    half_dim = head_size // 2
    frequency = rope_base ** (-jnp.arange(half_dim, dtype=jnp.float32) / half_dim)
    return position.astype(jnp.float32)[..., None] * frequency


def rotate_halves(vector, angle_arg):
    half_dim = vector.shape[-1] // 2
    lower_half = vector[..., :half_dim]
    upper_half = vector[..., half_dim:]
    cosine = jnp.cos(angle_arg)
    sine_part = jnp.sin(angle_arg)
    return jnp.concatenate(
        [
            lower_half * cosine - upper_half * sine_part,
            upper_half * cosine + lower_half * sine_part,
        ],
        axis=-1,
    )


def rotary_heads(raw_proj, gain_vec, position, head_count):
    head_size = gain_vec.shape[0]
    split_heads = raw_proj.reshape(raw_proj.shape[0], head_count, head_size)
    normed = norm_rows(split_heads, gain_vec)
    return rotate_halves(normed, angles(position, head_size)[:, None, :]).astype(jnp.bfloat16)


def block_stats(grouped_heads, gathered_stretch_keys, values, live_mask):
    count_of_rows, key_heads, groups, head_size = grouped_heads.shape
    scores = jnp.einsum(
        "mhgd,khd->hgmk", grouped_heads, gathered_stretch_keys, preferred_element_type=jnp.float32
    ) * head_size ** (-0.5)
    row_peak = jnp.max(jnp.where(live_mask, scores, floor_score), axis=-1)
    weights = jnp.where(live_mask, jnp.exp(scores - row_peak[..., None]), 0.0)
    weight_sum = jnp.sum(weights, axis=-1)
    weighted = jnp.einsum(
        "hgmk,khd->mhgd", weights.astype(jnp.bfloat16), values, preferred_element_type=jnp.float32
    )
    head_total = key_heads * groups
    return (
        weighted.reshape(count_of_rows, head_total, head_size),
        row_peak.transpose(2, 0, 1).reshape(count_of_rows, head_total),
        weight_sum.transpose(2, 0, 1).reshape(count_of_rows, head_total),
    )


def merge_stats(weighted, row_peak, weight_sum):
    row_top = jnp.max(row_peak, axis=0)
    factor = jnp.exp(row_peak - row_top[None])
    merged = jnp.sum(weighted * factor[..., None], axis=0)
    total_sum = jnp.sum(weight_sum * factor, axis=0)
    result = (merged / total_sum[..., None]).astype(jnp.bfloat16)
    return result.reshape(result.shape[0], -1)


def swiglu(rows_in, w_gate, w_up):
    gate_proj = jnp.dot(rows_in, w_gate, preferred_element_type=jnp.float32)
    up_proj = jnp.dot(rows_in, w_up, preferred_element_type=jnp.float32)
    return (jax.nn.silu(gate_proj) * up_proj).astype(jnp.bfloat16)


far_position = 1 << 30


def held_block_kernel(slot_ref, alive_ref, q_ref, k0_ref, k1_ref, v0_ref, v1_ref, cos_ref, sin_ref, qpos_ref, kpos_ref, out_ref):
    step = pl.program_id(0)
    key_refs = (k0_ref, k1_ref)

    def store(weighted, peak, total):
        rows, lanes = weighted.shape
        chunks = rows // lanes
        lane = lax.broadcasted_iota(jnp.int32, (rows, lanes), 1)
        packed = jnp.where(lane == 0, peak, jnp.where(lane == 1, total, 0.0)).T
        out_ref[0, :rows] = weighted
        out_ref[0, rows:rows + chunks] = jnp.concatenate(
            [packed[0:1, c * lanes:(c + 1) * lanes] for c in range(chunks)], axis=0
        )
        out_ref[0, rows + chunks:rows + 2 * chunks] = jnp.concatenate(
            [packed[1:2, c * lanes:(c + 1) * lanes] for c in range(chunks)], axis=0
        )
    value_refs = (v0_ref, v1_ref)

    def run(parts):
        query = q_ref[0]
        query_pos = qpos_ref[0]
        scale = (query.shape[-1]) ** (-0.5)
        masked = []
        for j in parts:
            key = key_refs[j][0].astype(jnp.float32)
            half = key.shape[-1] // 2
            rotated = (key * cos_ref[0, j] + pltpu.roll(key, half, 1) * sin_ref[0, j]).astype(jnp.bfloat16)
            raw = lax.dot_general(query, rotated, (((1,), (1,)), ((), ())), preferred_element_type=jnp.float32)
            masked.append(jnp.where(kpos_ref[0, j] < query_pos, raw * scale, floor_score))
        peak = jnp.max(masked[0], axis=1, keepdims=True)
        for extra in masked[1:]:
            peak = jnp.maximum(peak, jnp.max(extra, axis=1, keepdims=True))
        safe_peak = jnp.where(peak == floor_score, 0.0, peak)
        total = None
        weighted = None
        for j, block in zip(parts, masked):
            w = jnp.exp(block - safe_peak)
            part_total = jnp.sum(w, axis=1, keepdims=True)
            part_sum = jnp.dot(w.astype(jnp.bfloat16), value_refs[j][0], preferred_element_type=jnp.float32)
            total = part_total if total is None else total + part_total
            weighted = part_sum if weighted is None else weighted + part_sum
        store(weighted, peak, total)

    live0 = alive_ref[2 * step] > 0
    live1 = alive_ref[2 * step + 1] > 0
    pl.when(live0 & live1)(lambda: run((0, 1)))
    pl.when(live0 & jnp.logical_not(live1))(lambda: run((0,)))
    pl.when(jnp.logical_not(live0) & live1)(lambda: run((1,)))

    @pl.when(jnp.logical_not(live0) & jnp.logical_not(live1))
    def _():
        rows, lanes = q_ref.shape[1], q_ref.shape[2]
        out_ref[0, :rows] = jnp.zeros((rows, lanes), jnp.float32)
        chunks = rows // lanes
        out_ref[0, rows:rows + chunks] = jnp.full((chunks, lanes), floor_score, jnp.float32)
        out_ref[0, rows + chunks:rows + 2 * chunks] = jnp.zeros((chunks, lanes), jnp.float32)


def held_blocks(slots, alive, queries, key_pool, value_pool, cos_table, sin_table, query_pos, key_pos):
    requests, rows, head_size = queries.shape
    stretch = key_pool.shape[1]

    def pool_spec(j):
        return pl.BlockSpec((1, stretch, head_size), lambda r, slot, alive: (slot[2 * r + j], 0, 0))

    grid_spec = pltpu.PrefetchScalarGridSpec(
        num_scalar_prefetch=2,
        grid=(requests,),
        in_specs=[
            pl.BlockSpec((1, rows, head_size), lambda r, slot, alive: (r, 0, 0)),
            pool_spec(0),
            pool_spec(1),
            pool_spec(0),
            pool_spec(1),
            pl.BlockSpec((1, 2, 1, head_size), lambda r, slot, alive: (r, 0, 0, 0)),
            pl.BlockSpec((1, 2, 1, head_size), lambda r, slot, alive: (r, 0, 0, 0)),
            pl.BlockSpec((1, rows, 1), lambda r, slot, alive: (r, 0, 0)),
            pl.BlockSpec((1, 2, 1, stretch), lambda r, slot, alive: (r, 0, 0, 0)),
        ],
        out_specs=pl.BlockSpec((1, rows + 2 * rows // head_size, head_size), lambda r, slot, alive: (r, 0, 0)),
    )
    return pl.pallas_call(
        held_block_kernel,
        grid_spec=grid_spec,
        out_shape=jax.ShapeDtypeStruct((requests, rows + 2 * rows // head_size, head_size), jnp.float32),
        compiler_params=pltpu.CompilerParams(dimension_semantics=("arbitrary",)),
    )(slots, alive, queries, key_pool, key_pool, value_pool, value_pool, cos_table, sin_table, query_pos, key_pos)


def reduce_rows(terms, tp_count):
    blocks = terms.reshape(tp_count, terms.shape[0] // tp_count, terms.shape[1])
    got = lax.all_to_all(blocks, "tp", 0, 0, tiled=False)
    return jnp.sum(got.astype(jnp.float32), axis=0)


def gather_rows(rows, tp_count):
    tp_index = lax.axis_index("tp")
    parts = [rows]
    for shift in range(1, tp_count):
        pairs = [(i, (i + shift) % tp_count) for i in range(tp_count)]
        parts.append(lax.ppermute(rows, "tp", pairs))
    stacked = jnp.stack(parts)
    source = (tp_index - jnp.arange(tp_count)) % tp_count
    ordered = jnp.take(stacked, jnp.argsort(source), axis=0)
    return ordered.reshape(tp_count * rows.shape[0], rows.shape[1])


def on_device(
    hidden_in,
    recompute_pos,
    req_lengths,
    stretch_order,
    page_table,
    cached_key_pool,
    cached_value_pool,
    attn_gain,
    w_query,
    w_key,
    value_weight,
    query_gain,
    key_norm_gain,
    w_out,
    ffn_gain,
    w_gate,
    w_up,
    w_down,
):
    req_count = lax.axis_size("req")
    my_index = lax.axis_index("req")
    head_size = query_gain.shape[0]
    query_heads = w_query.shape[1] // head_size
    key_heads = w_key.shape[1] // head_size
    groups = query_heads // key_heads
    count_of_rows = hidden_in.shape[0]
    local_reqs = REQ_DEV
    req_rows = RECOMPUTE_TOKENS
    entries = local_reqs * MOST_STRETCHES
    pair_cap = entries // req_count
    normed = norm_rows(hidden_in, attn_gain).astype(jnp.bfloat16)
    query_raw = jnp.dot(normed, w_query, preferred_element_type=jnp.float32)
    unnormed_keys = jnp.dot(normed, w_key, preferred_element_type=jnp.float32)
    recomputed_values = (
        jnp.dot(normed, value_weight, preferred_element_type=jnp.float32)
        .astype(jnp.bfloat16)
        .reshape(count_of_rows, key_heads, head_size)
    )
    my_positions = lax.dynamic_slice_in_dim(recompute_pos, my_index * local_reqs, local_reqs, 0)
    my_lengths = lax.dynamic_slice_in_dim(req_lengths, my_index * local_reqs, local_reqs, 0)
    flattened_position = my_positions.reshape(count_of_rows)
    queries = rotary_heads(query_raw, query_gain, flattened_position, query_heads)
    recomputed_keys = rotary_heads(unnormed_keys, key_norm_gain, flattened_position, key_heads)
    grouped_heads = queries.reshape(count_of_rows, key_heads, groups, head_size)
    row_owner = jnp.arange(count_of_rows) // req_rows
    own_mask = (row_owner[None, :] == row_owner[:, None]) & (
        flattened_position[None, :] <= flattened_position[:, None]
    )
    fresh_sum, fresh_peak, fresh_total = block_stats(
        grouped_heads, recomputed_keys, recomputed_values, own_mask
    )
    holder_table = page_table[0][stretch_order]
    slot_table = page_table[1][stretch_order]
    holder_hits = holder_table[:, :, None] == jnp.arange(req_count)[None, None, :]
    hit_counts = jnp.cumsum(holder_hits.astype(jnp.int32), axis=1)
    pair_rank = jnp.sum(jnp.where(holder_hits, hit_counts - 1, 0), axis=2)
    my_sends = (holder_table == my_index)[:, :, None] & (
        pair_rank[:, :, None] == jnp.arange(pair_cap)[None, None, :]
    )
    send_slot = jnp.sum(jnp.where(my_sends, slot_table[:, :, None], 0), axis=1)
    send_place = jnp.sum(jnp.where(my_sends, jnp.arange(MOST_STRETCHES)[None, :, None], 0), axis=1)
    request_count = holder_table.shape[0]
    pool_slots = cached_key_pool.shape[0]
    slots = jnp.clip(send_slot, 0, pool_slots - 1).reshape(request_count * pair_cap).astype(jnp.int32)
    held_angle = angles(send_place * STRETCH_TOKENS, head_size)
    cos_table = jnp.cos(held_angle)
    sin_table = jnp.sin(held_angle)
    cos_table = jnp.concatenate([cos_table, cos_table], axis=-1)[:, :, None, :]
    sin_table = jnp.concatenate([-sin_table, sin_table], axis=-1)[:, :, None, :]
    query_copies = jnp.broadcast_to(queries[None], (req_count,) + queries.shape)
    all_queries = lax.all_to_all(query_copies, "req", 0, 0, tiled=False)
    all_queries = all_queries.reshape(request_count, req_rows * groups, head_size)
    query_pos = jnp.repeat(recompute_pos, groups, axis=1)[:, :, None]
    key_pos = jnp.where(
        (send_place < req_lengths[:, None])[:, :, None],
        send_place[:, :, None] * STRETCH_TOKENS + jnp.arange(STRETCH_TOKENS)[None, None, :],
        far_position,
    )[:, :, None, :]
    alive = (send_place < req_lengths[:, None]).reshape(request_count * pair_cap).astype(jnp.int32)
    held = held_blocks(
        slots, alive, all_queries, cached_key_pool, cached_value_pool, cos_table, sin_table, query_pos, key_pos
    )
    got = lax.all_to_all(held, "req", 0, 0, tiled=False)
    sum_rows = req_rows * groups
    chunks = sum_rows // head_size
    head_total = key_heads * groups
    got_sum = got[:, :sum_rows]
    got_peak = got[:, sum_rows:sum_rows + chunks].reshape(req_count, count_of_rows, head_total)
    got_total = got[:, sum_rows + chunks:].reshape(req_count, count_of_rows, head_total)
    attended = merge_stats(
        jnp.concatenate([got_sum.reshape(req_count, count_of_rows, head_total, head_size), fresh_sum[None]]),
        jnp.concatenate([got_peak, fresh_peak[None]]),
        jnp.concatenate([got_total, fresh_total[None]]),
    )
    tp_count = lax.axis_size("tp")
    tp_index = lax.axis_index("tp")
    block_rows = count_of_rows // tp_count
    attn_terms = jnp.dot(attended, w_out, preferred_element_type=jnp.float32).astype(jnp.bfloat16)
    attn_out = reduce_rows(attn_terms, tp_count)
    my_hidden = lax.dynamic_slice_in_dim(hidden_in, tp_index * block_rows, block_rows, 0)
    residual = (my_hidden.astype(jnp.float32) + attn_out).astype(jnp.bfloat16)
    normed_ffn = gather_rows(norm_rows(residual, ffn_gain).astype(jnp.bfloat16), tp_count)
    hidden = swiglu(normed_ffn, w_gate, w_up)
    down_terms = jnp.dot(hidden, w_down, preferred_element_type=jnp.float32).astype(jnp.bfloat16)
    ffn_out = reduce_rows(down_terms, tp_count)
    return gather_rows((residual.astype(jnp.float32) + ffn_out).astype(jnp.bfloat16), tp_count)


def solution(mesh):
    return jax.shard_map(
        on_device,
        mesh=mesh,
        in_specs=(
            P("req", None),
            P(),
            P(),
            P(),
            P(),
            P("req", None, "tp"),
            P("req", None, "tp"),
            P(),
            P(None, "tp"),
            P(None, "tp"),
            P(None, "tp"),
            P(),
            P(),
            P("tp", None),
            P(),
            P(None, "tp"),
            P(None, "tp"),
            P("tp", None),
        ),
        out_specs=P("req", None),
        check_vma=False,
    )
```

```python
import jax
import jax.numpy as jnp
from jax import lax
from jax.sharding import PartitionSpec as P
from jax.experimental import pallas as pl
from jax.experimental.pallas import tpu as pltpu

STRETCH_TOKENS = 512
MOST_STRETCHES = 32
REQ_DEV = 1
RECOMPUTE_TOKENS = 256


eps_norm = 1e-06
rope_base = 1000000.0
floor_score = -1e30


def norm_rows(matrix, gain_vec):
    wide = matrix.astype(jnp.float32)
    factor = lax.rsqrt(jnp.mean(wide * wide, axis=-1, keepdims=True) + eps_norm)
    return wide * factor * gain_vec


def angles(position, head_size):
    half_dim = head_size // 2
    frequency = rope_base ** (-jnp.arange(half_dim, dtype=jnp.float32) / half_dim)
    return position.astype(jnp.float32)[..., None] * frequency


def rotate_halves(vector, angle_arg):
    half_dim = vector.shape[-1] // 2
    lower_half = vector[..., :half_dim]
    upper_half = vector[..., half_dim:]
    cosine = jnp.cos(angle_arg)
    sine_part = jnp.sin(angle_arg)
    return jnp.concatenate(
        [
            lower_half * cosine - upper_half * sine_part,
            upper_half * cosine + lower_half * sine_part,
        ],
        axis=-1,
    )


def rotary_heads(raw_proj, gain_vec, position, head_count):
    head_size = gain_vec.shape[0]
    split_heads = raw_proj.reshape(raw_proj.shape[0], head_count, head_size)
    normed = norm_rows(split_heads, gain_vec)
    return rotate_halves(normed, angles(position, head_size)[:, None, :]).astype(jnp.bfloat16)


def block_stats(grouped_heads, gathered_stretch_keys, values, live_mask):
    count_of_rows, key_heads, groups, head_size = grouped_heads.shape
    scores = jnp.einsum(
        "mhgd,khd->hgmk", grouped_heads, gathered_stretch_keys, preferred_element_type=jnp.float32
    ) * head_size ** (-0.5)
    row_peak = jnp.max(jnp.where(live_mask, scores, floor_score), axis=-1)
    weights = jnp.where(live_mask, jnp.exp(scores - row_peak[..., None]), 0.0)
    weight_sum = jnp.sum(weights, axis=-1)
    weighted = jnp.einsum(
        "hgmk,khd->mhgd", weights.astype(jnp.bfloat16), values, preferred_element_type=jnp.float32
    )
    head_total = key_heads * groups
    return (
        weighted.reshape(count_of_rows, head_total, head_size),
        row_peak.transpose(2, 0, 1).reshape(count_of_rows, head_total),
        weight_sum.transpose(2, 0, 1).reshape(count_of_rows, head_total),
    )


def merge_stats(weighted, row_peak, weight_sum):
    row_top = jnp.max(row_peak, axis=0)
    factor = jnp.exp(row_peak - row_top[None])
    merged = jnp.sum(weighted * factor[..., None], axis=0)
    total_sum = jnp.sum(weight_sum * factor, axis=0)
    result = (merged / total_sum[..., None]).astype(jnp.bfloat16)
    return result.reshape(result.shape[0], -1)


def swiglu(rows_in, w_gate, w_up):
    gate_proj = jnp.dot(rows_in, w_gate, preferred_element_type=jnp.float32)
    up_proj = jnp.dot(rows_in, w_up, preferred_element_type=jnp.float32)
    return (jax.nn.silu(gate_proj) * up_proj).astype(jnp.bfloat16)


far_position = 1 << 30


def held_block_kernel(slot_ref, alive_ref, q_ref, k0_ref, k1_ref, v0_ref, v1_ref, cos_ref, sin_ref, qpos_ref, kpos_ref, out_ref, stat_ref):
    step = pl.program_id(0)
    key_refs = (k0_ref, k1_ref)

    def store(weighted, peak, total):
        rows, lanes = weighted.shape
        chunks = rows // lanes
        lane = lax.broadcasted_iota(jnp.int32, (rows, lanes), 1)
        packed = jnp.where(lane == 0, peak, jnp.where(lane == 1, total, 0.0)).T
        out_ref[0] = weighted.astype(out_ref.dtype)
        stat_ref[0, 0:chunks] = jnp.concatenate(
            [packed[0:1, c * lanes:(c + 1) * lanes] for c in range(chunks)], axis=0
        )
        stat_ref[0, chunks:2 * chunks] = jnp.concatenate(
            [packed[1:2, c * lanes:(c + 1) * lanes] for c in range(chunks)], axis=0
        )
    value_refs = (v0_ref, v1_ref)

    def run(parts):
        query = q_ref[0]
        query_pos = qpos_ref[0]
        scale = (query.shape[-1]) ** (-0.5)
        masked = []
        for j in parts:
            key = key_refs[j][0].astype(jnp.float32)
            half = key.shape[-1] // 2
            rotated = (key * cos_ref[0, j] + pltpu.roll(key, half, 1) * sin_ref[0, j]).astype(jnp.bfloat16)
            raw = lax.dot_general(query, rotated, (((1,), (1,)), ((), ())), preferred_element_type=jnp.float32)
            masked.append(jnp.where(kpos_ref[0, j] < query_pos, raw * scale, floor_score))
        peak = jnp.max(masked[0], axis=1, keepdims=True)
        for extra in masked[1:]:
            peak = jnp.maximum(peak, jnp.max(extra, axis=1, keepdims=True))
        safe_peak = jnp.where(peak == floor_score, 0.0, peak)
        total = None
        weighted = None
        for j, block in zip(parts, masked):
            w = jnp.exp(block - safe_peak)
            part_total = jnp.sum(w, axis=1, keepdims=True)
            part_sum = jnp.dot(w.astype(jnp.bfloat16), value_refs[j][0], preferred_element_type=jnp.float32)
            total = part_total if total is None else total + part_total
            weighted = part_sum if weighted is None else weighted + part_sum
        store(weighted, peak, total)

    live0 = alive_ref[2 * step] > 0
    live1 = alive_ref[2 * step + 1] > 0
    pl.when(live0 & live1)(lambda: run((0, 1)))
    pl.when(live0 & jnp.logical_not(live1))(lambda: run((0,)))
    pl.when(jnp.logical_not(live0) & live1)(lambda: run((1,)))

    @pl.when(jnp.logical_not(live0) & jnp.logical_not(live1))
    def _():
        rows, lanes = q_ref.shape[1], q_ref.shape[2]
        out_ref[0] = jnp.zeros((rows, lanes), out_ref.dtype)
        chunks = rows // lanes
        stat_ref[0, 0:chunks] = jnp.full((chunks, lanes), floor_score, jnp.float32)
        stat_ref[0, chunks:2 * chunks] = jnp.zeros((chunks, lanes), jnp.float32)


def held_blocks(slots, alive, queries, key_pool, value_pool, cos_table, sin_table, query_pos, key_pos):
    requests, rows, head_size = queries.shape
    stretch = key_pool.shape[1]

    def pool_spec(j):
        return pl.BlockSpec((1, stretch, head_size), lambda r, slot, alive: (slot[2 * r + j], 0, 0))

    grid_spec = pltpu.PrefetchScalarGridSpec(
        num_scalar_prefetch=2,
        grid=(requests,),
        in_specs=[
            pl.BlockSpec((1, rows, head_size), lambda r, slot, alive: (r, 0, 0)),
            pool_spec(0),
            pool_spec(1),
            pool_spec(0),
            pool_spec(1),
            pl.BlockSpec((1, 2, 1, head_size), lambda r, slot, alive: (r, 0, 0, 0)),
            pl.BlockSpec((1, 2, 1, head_size), lambda r, slot, alive: (r, 0, 0, 0)),
            pl.BlockSpec((1, rows, 1), lambda r, slot, alive: (r, 0, 0)),
            pl.BlockSpec((1, 2, 1, stretch), lambda r, slot, alive: (r, 0, 0, 0)),
        ],
        out_specs=[
            pl.BlockSpec((1, rows, head_size), lambda r, slot, alive: (r, 0, 0)),
            pl.BlockSpec((1, 2 * rows // head_size, head_size), lambda r, slot, alive: (r, 0, 0)),
        ],
    )
    return pl.pallas_call(
        held_block_kernel,
        grid_spec=grid_spec,
        out_shape=[
            jax.ShapeDtypeStruct((requests, rows, head_size), jnp.bfloat16),
            jax.ShapeDtypeStruct((requests, 2 * rows // head_size, head_size), jnp.float32),
        ],
        compiler_params=pltpu.CompilerParams(dimension_semantics=("arbitrary",)),
    )(slots, alive, queries, key_pool, key_pool, value_pool, value_pool, cos_table, sin_table, query_pos, key_pos)


def reduce_rows(terms, tp_count):
    blocks = terms.reshape(tp_count, terms.shape[0] // tp_count, terms.shape[1])
    got = lax.all_to_all(blocks, "tp", 0, 0, tiled=False)
    return jnp.sum(got.astype(jnp.float32), axis=0)


def gather_rows(rows, tp_count):
    tp_index = lax.axis_index("tp")
    parts = [rows]
    for shift in range(1, tp_count):
        pairs = [(i, (i + shift) % tp_count) for i in range(tp_count)]
        parts.append(lax.ppermute(rows, "tp", pairs))
    stacked = jnp.stack(parts)
    source = (tp_index - jnp.arange(tp_count)) % tp_count
    ordered = jnp.take(stacked, jnp.argsort(source), axis=0)
    return ordered.reshape(tp_count * rows.shape[0], rows.shape[1])


def on_device(
    hidden_in,
    recompute_pos,
    req_lengths,
    stretch_order,
    page_table,
    cached_key_pool,
    cached_value_pool,
    attn_gain,
    w_query,
    w_key,
    value_weight,
    query_gain,
    key_norm_gain,
    w_out,
    ffn_gain,
    w_gate,
    w_up,
    w_down,
):
    req_count = lax.axis_size("req")
    my_index = lax.axis_index("req")
    head_size = query_gain.shape[0]
    query_heads = w_query.shape[1] // head_size
    key_heads = w_key.shape[1] // head_size
    groups = query_heads // key_heads
    count_of_rows = hidden_in.shape[0]
    local_reqs = REQ_DEV
    req_rows = RECOMPUTE_TOKENS
    entries = local_reqs * MOST_STRETCHES
    pair_cap = entries // req_count
    normed = norm_rows(hidden_in, attn_gain).astype(jnp.bfloat16)
    query_raw = jnp.dot(normed, w_query, preferred_element_type=jnp.float32)
    unnormed_keys = jnp.dot(normed, w_key, preferred_element_type=jnp.float32)
    recomputed_values = (
        jnp.dot(normed, value_weight, preferred_element_type=jnp.float32)
        .astype(jnp.bfloat16)
        .reshape(count_of_rows, key_heads, head_size)
    )
    my_positions = lax.dynamic_slice_in_dim(recompute_pos, my_index * local_reqs, local_reqs, 0)
    my_lengths = lax.dynamic_slice_in_dim(req_lengths, my_index * local_reqs, local_reqs, 0)
    flattened_position = my_positions.reshape(count_of_rows)
    queries = rotary_heads(query_raw, query_gain, flattened_position, query_heads)
    recomputed_keys = rotary_heads(unnormed_keys, key_norm_gain, flattened_position, key_heads)
    grouped_heads = queries.reshape(count_of_rows, key_heads, groups, head_size)
    row_owner = jnp.arange(count_of_rows) // req_rows
    own_mask = (row_owner[None, :] == row_owner[:, None]) & (
        flattened_position[None, :] <= flattened_position[:, None]
    )
    fresh_sum, fresh_peak, fresh_total = block_stats(
        grouped_heads, recomputed_keys, recomputed_values, own_mask
    )
    holder_table = page_table[0][stretch_order]
    slot_table = page_table[1][stretch_order]
    holder_hits = holder_table[:, :, None] == jnp.arange(req_count)[None, None, :]
    hit_counts = jnp.cumsum(holder_hits.astype(jnp.int32), axis=1)
    pair_rank = jnp.sum(jnp.where(holder_hits, hit_counts - 1, 0), axis=2)
    my_sends = (holder_table == my_index)[:, :, None] & (
        pair_rank[:, :, None] == jnp.arange(pair_cap)[None, None, :]
    )
    send_slot = jnp.sum(jnp.where(my_sends, slot_table[:, :, None], 0), axis=1)
    send_place = jnp.sum(jnp.where(my_sends, jnp.arange(MOST_STRETCHES)[None, :, None], 0), axis=1)
    request_count = holder_table.shape[0]
    pool_slots = cached_key_pool.shape[0]
    slots = jnp.clip(send_slot, 0, pool_slots - 1).reshape(request_count * pair_cap).astype(jnp.int32)
    held_angle = angles(send_place * STRETCH_TOKENS, head_size)
    cos_table = jnp.cos(held_angle)
    sin_table = jnp.sin(held_angle)
    cos_table = jnp.concatenate([cos_table, cos_table], axis=-1)[:, :, None, :]
    sin_table = jnp.concatenate([-sin_table, sin_table], axis=-1)[:, :, None, :]
    query_copies = jnp.broadcast_to(queries[None], (req_count,) + queries.shape)
    all_queries = lax.all_to_all(query_copies, "req", 0, 0, tiled=False)
    all_queries = all_queries.reshape(request_count, req_rows * groups, head_size)
    query_pos = jnp.repeat(recompute_pos, groups, axis=1)[:, :, None]
    key_pos = jnp.where(
        (send_place < req_lengths[:, None])[:, :, None],
        send_place[:, :, None] * STRETCH_TOKENS + jnp.arange(STRETCH_TOKENS)[None, None, :],
        far_position,
    )[:, :, None, :]
    alive = (send_place < req_lengths[:, None]).reshape(request_count * pair_cap).astype(jnp.int32)
    held_sum, held_stats = held_blocks(
        slots, alive, all_queries, cached_key_pool, cached_value_pool, cos_table, sin_table, query_pos, key_pos
    )
    got_sum = lax.all_to_all(held_sum, "req", 0, 0, tiled=False).astype(jnp.float32)
    got_stats = lax.all_to_all(held_stats, "req", 0, 0, tiled=False)
    chunks = req_rows * groups // head_size
    head_total = key_heads * groups
    got_peak = got_stats[:, :chunks].reshape(req_count, count_of_rows, head_total)
    got_total = got_stats[:, chunks:].reshape(req_count, count_of_rows, head_total)
    attended = merge_stats(
        jnp.concatenate([got_sum.reshape(req_count, count_of_rows, head_total, head_size), fresh_sum[None]]),
        jnp.concatenate([got_peak, fresh_peak[None]]),
        jnp.concatenate([got_total, fresh_total[None]]),
    )
    tp_count = lax.axis_size("tp")
    tp_index = lax.axis_index("tp")
    block_rows = count_of_rows // tp_count
    attn_terms = jnp.dot(attended, w_out, preferred_element_type=jnp.float32).astype(jnp.bfloat16)
    attn_out = reduce_rows(attn_terms, tp_count)
    my_hidden = lax.dynamic_slice_in_dim(hidden_in, tp_index * block_rows, block_rows, 0)
    residual = (my_hidden.astype(jnp.float32) + attn_out).astype(jnp.bfloat16)
    normed_ffn = gather_rows(norm_rows(residual, ffn_gain).astype(jnp.bfloat16), tp_count)
    hidden = swiglu(normed_ffn, w_gate, w_up)
    down_terms = jnp.dot(hidden, w_down, preferred_element_type=jnp.float32).astype(jnp.bfloat16)
    ffn_out = reduce_rows(down_terms, tp_count)
    return gather_rows((residual.astype(jnp.float32) + ffn_out).astype(jnp.bfloat16), tp_count)


def solution(mesh):
    return jax.shard_map(
        on_device,
        mesh=mesh,
        in_specs=(
            P("req", None),
            P(),
            P(),
            P(),
            P(),
            P("req", None, "tp"),
            P("req", None, "tp"),
            P(),
            P(None, "tp"),
            P(None, "tp"),
            P(None, "tp"),
            P(),
            P(),
            P("tp", None),
            P(),
            P(None, "tp"),
            P(None, "tp"),
            P("tp", None),
        ),
        out_specs=P("req", None),
        check_vma=False,
    )
```

```python
import jax
import jax.numpy as jnp
from jax import lax
from jax.sharding import PartitionSpec as P
from jax.experimental import pallas as pl
from jax.experimental.pallas import tpu as pltpu

STRETCH_TOKENS = 512
MOST_STRETCHES = 32
REQ_DEV = 1
RECOMPUTE_TOKENS = 256


eps_norm = 1e-06
rope_base = 1000000.0
floor_score = -1e30


def norm_rows(matrix, gain_vec):
    wide = matrix.astype(jnp.float32)
    factor = lax.rsqrt(jnp.mean(wide * wide, axis=-1, keepdims=True) + eps_norm)
    return wide * factor * gain_vec


def angles(position, head_size):
    half_dim = head_size // 2
    frequency = rope_base ** (-jnp.arange(half_dim, dtype=jnp.float32) / half_dim)
    return position.astype(jnp.float32)[..., None] * frequency


def rotate_halves(vector, angle_arg):
    half_dim = vector.shape[-1] // 2
    lower_half = vector[..., :half_dim]
    upper_half = vector[..., half_dim:]
    cosine = jnp.cos(angle_arg)
    sine_part = jnp.sin(angle_arg)
    return jnp.concatenate(
        [
            lower_half * cosine - upper_half * sine_part,
            upper_half * cosine + lower_half * sine_part,
        ],
        axis=-1,
    )


def rotary_heads(raw_proj, gain_vec, position, head_count):
    head_size = gain_vec.shape[0]
    split_heads = raw_proj.reshape(raw_proj.shape[0], head_count, head_size)
    normed = norm_rows(split_heads, gain_vec)
    return rotate_halves(normed, angles(position, head_size)[:, None, :]).astype(jnp.bfloat16)


def block_stats(grouped_heads, gathered_stretch_keys, values, live_mask):
    count_of_rows, key_heads, groups, head_size = grouped_heads.shape
    scores = jnp.einsum(
        "mhgd,khd->hgmk", grouped_heads, gathered_stretch_keys, preferred_element_type=jnp.float32
    ) * head_size ** (-0.5)
    row_peak = jnp.max(jnp.where(live_mask, scores, floor_score), axis=-1)
    weights = jnp.where(live_mask, jnp.exp(scores - row_peak[..., None]), 0.0)
    weight_sum = jnp.sum(weights, axis=-1)
    weighted = jnp.einsum(
        "hgmk,khd->mhgd", weights.astype(jnp.bfloat16), values, preferred_element_type=jnp.float32
    )
    head_total = key_heads * groups
    return (
        weighted.reshape(count_of_rows, head_total, head_size),
        row_peak.transpose(2, 0, 1).reshape(count_of_rows, head_total),
        weight_sum.transpose(2, 0, 1).reshape(count_of_rows, head_total),
    )


def merge_stats(weighted, row_peak, weight_sum):
    row_top = jnp.max(row_peak, axis=0)
    factor = jnp.exp(row_peak - row_top[None])
    merged = jnp.sum(weighted * factor[..., None], axis=0)
    total_sum = jnp.sum(weight_sum * factor, axis=0)
    result = (merged / total_sum[..., None]).astype(jnp.bfloat16)
    return result.reshape(result.shape[0], -1)


def swiglu(rows_in, w_gate, w_up):
    gate_proj = jnp.dot(rows_in, w_gate, preferred_element_type=jnp.float32)
    up_proj = jnp.dot(rows_in, w_up, preferred_element_type=jnp.float32)
    return (jax.nn.silu(gate_proj) * up_proj).astype(jnp.bfloat16)


far_position = 1 << 30


def held_block_kernel(slot_ref, alive_ref, q_ref, k0_ref, k1_ref, v0_ref, v1_ref, cos_ref, sin_ref, qpos_ref, kpos_ref, out_ref):
    step = pl.program_id(0)
    key_refs = (k0_ref, k1_ref)

    def store_stats(peak_rows, total_rows):
        pieces = []
        for value in (peak_rows, total_rows):
            rest = value
            for _ in range(3):
                piece = rest.astype(jnp.bfloat16).astype(jnp.float32)
                pieces.append(piece)
                rest = rest - piece
        rows = q_ref.shape[1]
        spare = out_ref.shape[1] - rows - 6 * peak_rows.shape[0]
        pieces.append(jnp.zeros((spare, peak_rows.shape[1]), jnp.float32))
        out_ref[0, rows:] = jnp.concatenate(pieces, axis=0).astype(out_ref.dtype)

    def store(weighted, peak, total):
        rows, lanes = weighted.shape
        chunks = rows // lanes
        lane = lax.broadcasted_iota(jnp.int32, (rows, lanes), 1)
        packed = jnp.where(lane == 0, peak, jnp.where(lane == 1, total, 0.0)).T
        out_ref[0, :rows] = weighted.astype(out_ref.dtype)
        peak_rows = jnp.concatenate([packed[0:1, c * lanes:(c + 1) * lanes] for c in range(chunks)], axis=0)
        total_rows = jnp.concatenate([packed[1:2, c * lanes:(c + 1) * lanes] for c in range(chunks)], axis=0)
        store_stats(peak_rows, total_rows)
    value_refs = (v0_ref, v1_ref)

    def run(parts):
        query = q_ref[0]
        query_pos = qpos_ref[0]
        scale = (query.shape[-1]) ** (-0.5)
        masked = []
        for j in parts:
            key = key_refs[j][0].astype(jnp.float32)
            half = key.shape[-1] // 2
            rotated = (key * cos_ref[0, j] + pltpu.roll(key, half, 1) * sin_ref[0, j]).astype(jnp.bfloat16)
            raw = lax.dot_general(query, rotated, (((1,), (1,)), ((), ())), preferred_element_type=jnp.float32)
            masked.append(jnp.where(kpos_ref[0, j] < query_pos, raw * scale, floor_score))
        peak = jnp.max(masked[0], axis=1, keepdims=True)
        for extra in masked[1:]:
            peak = jnp.maximum(peak, jnp.max(extra, axis=1, keepdims=True))
        safe_peak = jnp.where(peak == floor_score, 0.0, peak)
        total = None
        weighted = None
        for j, block in zip(parts, masked):
            w = jnp.exp(block - safe_peak)
            part_total = jnp.sum(w, axis=1, keepdims=True)
            part_sum = jnp.dot(w.astype(jnp.bfloat16), value_refs[j][0], preferred_element_type=jnp.float32)
            total = part_total if total is None else total + part_total
            weighted = part_sum if weighted is None else weighted + part_sum
        store(weighted, peak, total)

    live0 = alive_ref[2 * step] > 0
    live1 = alive_ref[2 * step + 1] > 0
    pl.when(live0 & live1)(lambda: run((0, 1)))
    pl.when(live0 & jnp.logical_not(live1))(lambda: run((0,)))
    pl.when(jnp.logical_not(live0) & live1)(lambda: run((1,)))

    @pl.when(jnp.logical_not(live0) & jnp.logical_not(live1))
    def _():
        rows, lanes = q_ref.shape[1], q_ref.shape[2]
        out_ref[0, :rows] = jnp.zeros((rows, lanes), out_ref.dtype)
        chunks = rows // lanes
        store_stats(jnp.full((chunks, lanes), floor_score, jnp.float32), jnp.zeros((chunks, lanes), jnp.float32))


def held_blocks(slots, alive, queries, key_pool, value_pool, cos_table, sin_table, query_pos, key_pos):
    requests, rows, head_size = queries.shape
    stretch = key_pool.shape[1]
    stat_rows = -(-6 * rows // head_size // 16) * 16

    def pool_spec(j):
        return pl.BlockSpec((1, stretch, head_size), lambda r, slot, alive: (slot[2 * r + j], 0, 0))

    grid_spec = pltpu.PrefetchScalarGridSpec(
        num_scalar_prefetch=2,
        grid=(requests,),
        in_specs=[
            pl.BlockSpec((1, rows, head_size), lambda r, slot, alive: (r, 0, 0)),
            pool_spec(0),
            pool_spec(1),
            pool_spec(0),
            pool_spec(1),
            pl.BlockSpec((1, 2, 1, head_size), lambda r, slot, alive: (r, 0, 0, 0)),
            pl.BlockSpec((1, 2, 1, head_size), lambda r, slot, alive: (r, 0, 0, 0)),
            pl.BlockSpec((1, rows, 1), lambda r, slot, alive: (r, 0, 0)),
            pl.BlockSpec((1, 2, 1, stretch), lambda r, slot, alive: (r, 0, 0, 0)),
        ],
        out_specs=pl.BlockSpec((1, rows + stat_rows, head_size), lambda r, slot, alive: (r, 0, 0)),
    )
    return pl.pallas_call(
        held_block_kernel,
        grid_spec=grid_spec,
        out_shape=jax.ShapeDtypeStruct((requests, rows + stat_rows, head_size), jnp.bfloat16),
        compiler_params=pltpu.CompilerParams(dimension_semantics=("arbitrary",)),
    )(slots, alive, queries, key_pool, key_pool, value_pool, value_pool, cos_table, sin_table, query_pos, key_pos)


def reduce_rows(terms, tp_count):
    blocks = terms.reshape(tp_count, terms.shape[0] // tp_count, terms.shape[1])
    got = lax.all_to_all(blocks, "tp", 0, 0, tiled=False)
    return jnp.sum(got.astype(jnp.float32), axis=0)


def gather_rows(rows, tp_count):
    tp_index = lax.axis_index("tp")
    parts = [rows]
    for shift in range(1, tp_count):
        pairs = [(i, (i + shift) % tp_count) for i in range(tp_count)]
        parts.append(lax.ppermute(rows, "tp", pairs))
    stacked = jnp.stack(parts)
    source = (tp_index - jnp.arange(tp_count)) % tp_count
    ordered = jnp.take(stacked, jnp.argsort(source), axis=0)
    return ordered.reshape(tp_count * rows.shape[0], rows.shape[1])


def on_device(
    hidden_in,
    recompute_pos,
    req_lengths,
    stretch_order,
    page_table,
    cached_key_pool,
    cached_value_pool,
    attn_gain,
    w_query,
    w_key,
    value_weight,
    query_gain,
    key_norm_gain,
    w_out,
    ffn_gain,
    w_gate,
    w_up,
    w_down,
):
    req_count = lax.axis_size("req")
    my_index = lax.axis_index("req")
    head_size = query_gain.shape[0]
    query_heads = w_query.shape[1] // head_size
    key_heads = w_key.shape[1] // head_size
    groups = query_heads // key_heads
    count_of_rows = hidden_in.shape[0]
    local_reqs = REQ_DEV
    req_rows = RECOMPUTE_TOKENS
    entries = local_reqs * MOST_STRETCHES
    pair_cap = entries // req_count
    normed = norm_rows(hidden_in, attn_gain).astype(jnp.bfloat16)
    query_raw = jnp.dot(normed, w_query, preferred_element_type=jnp.float32)
    unnormed_keys = jnp.dot(normed, w_key, preferred_element_type=jnp.float32)
    recomputed_values = (
        jnp.dot(normed, value_weight, preferred_element_type=jnp.float32)
        .astype(jnp.bfloat16)
        .reshape(count_of_rows, key_heads, head_size)
    )
    my_positions = lax.dynamic_slice_in_dim(recompute_pos, my_index * local_reqs, local_reqs, 0)
    my_lengths = lax.dynamic_slice_in_dim(req_lengths, my_index * local_reqs, local_reqs, 0)
    flattened_position = my_positions.reshape(count_of_rows)
    queries = rotary_heads(query_raw, query_gain, flattened_position, query_heads)
    recomputed_keys = rotary_heads(unnormed_keys, key_norm_gain, flattened_position, key_heads)
    grouped_heads = queries.reshape(count_of_rows, key_heads, groups, head_size)
    row_owner = jnp.arange(count_of_rows) // req_rows
    own_mask = (row_owner[None, :] == row_owner[:, None]) & (
        flattened_position[None, :] <= flattened_position[:, None]
    )
    fresh_sum, fresh_peak, fresh_total = block_stats(
        grouped_heads, recomputed_keys, recomputed_values, own_mask
    )
    holder_table = page_table[0][stretch_order]
    slot_table = page_table[1][stretch_order]
    holder_hits = holder_table[:, :, None] == jnp.arange(req_count)[None, None, :]
    hit_counts = jnp.cumsum(holder_hits.astype(jnp.int32), axis=1)
    pair_rank = jnp.sum(jnp.where(holder_hits, hit_counts - 1, 0), axis=2)
    my_sends = (holder_table == my_index)[:, :, None] & (
        pair_rank[:, :, None] == jnp.arange(pair_cap)[None, None, :]
    )
    send_slot = jnp.sum(jnp.where(my_sends, slot_table[:, :, None], 0), axis=1)
    send_place = jnp.sum(jnp.where(my_sends, jnp.arange(MOST_STRETCHES)[None, :, None], 0), axis=1)
    request_count = holder_table.shape[0]
    pool_slots = cached_key_pool.shape[0]
    slots = jnp.clip(send_slot, 0, pool_slots - 1).reshape(request_count * pair_cap).astype(jnp.int32)
    held_angle = angles(send_place * STRETCH_TOKENS, head_size)
    cos_table = jnp.cos(held_angle)
    sin_table = jnp.sin(held_angle)
    cos_table = jnp.concatenate([cos_table, cos_table], axis=-1)[:, :, None, :]
    sin_table = jnp.concatenate([-sin_table, sin_table], axis=-1)[:, :, None, :]
    query_copies = jnp.broadcast_to(queries[None], (req_count,) + queries.shape)
    all_queries = lax.all_to_all(query_copies, "req", 0, 0, tiled=False)
    all_queries = all_queries.reshape(request_count, req_rows * groups, head_size)
    query_pos = jnp.repeat(recompute_pos, groups, axis=1)[:, :, None]
    key_pos = jnp.where(
        (send_place < req_lengths[:, None])[:, :, None],
        send_place[:, :, None] * STRETCH_TOKENS + jnp.arange(STRETCH_TOKENS)[None, None, :],
        far_position,
    )[:, :, None, :]
    alive = (send_place < req_lengths[:, None]).reshape(request_count * pair_cap).astype(jnp.int32)
    held = held_blocks(
        slots, alive, all_queries, cached_key_pool, cached_value_pool, cos_table, sin_table, query_pos, key_pos
    )
    got = lax.all_to_all(held, "req", 0, 0, tiled=False)
    sum_rows = req_rows * groups
    chunks = sum_rows // head_size
    head_total = key_heads * groups
    got_sum = got[:, :sum_rows].astype(jnp.float32)

    def stat_of(k):
        base = sum_rows + 3 * k * chunks
        hi, mid, lo = (got[:, base + i * chunks:base + (i + 1) * chunks].astype(jnp.float32) for i in range(3))
        return ((hi + mid) + lo).reshape(req_count, count_of_rows, head_total)

    got_peak = stat_of(0)
    got_total = stat_of(1)
    attended = merge_stats(
        jnp.concatenate([got_sum.reshape(req_count, count_of_rows, head_total, head_size), fresh_sum[None]]),
        jnp.concatenate([got_peak, fresh_peak[None]]),
        jnp.concatenate([got_total, fresh_total[None]]),
    )
    tp_count = lax.axis_size("tp")
    tp_index = lax.axis_index("tp")
    block_rows = count_of_rows // tp_count
    attn_terms = jnp.dot(attended, w_out, preferred_element_type=jnp.float32).astype(jnp.bfloat16)
    attn_out = reduce_rows(attn_terms, tp_count)
    my_hidden = lax.dynamic_slice_in_dim(hidden_in, tp_index * block_rows, block_rows, 0)
    residual = (my_hidden.astype(jnp.float32) + attn_out).astype(jnp.bfloat16)
    normed_ffn = gather_rows(norm_rows(residual, ffn_gain).astype(jnp.bfloat16), tp_count)
    hidden = swiglu(normed_ffn, w_gate, w_up)
    down_terms = jnp.dot(hidden, w_down, preferred_element_type=jnp.float32).astype(jnp.bfloat16)
    ffn_out = reduce_rows(down_terms, tp_count)
    return gather_rows((residual.astype(jnp.float32) + ffn_out).astype(jnp.bfloat16), tp_count)


def solution(mesh):
    return jax.shard_map(
        on_device,
        mesh=mesh,
        in_specs=(
            P("req", None),
            P(),
            P(),
            P(),
            P(),
            P("req", None, "tp"),
            P("req", None, "tp"),
            P(),
            P(None, "tp"),
            P(None, "tp"),
            P(None, "tp"),
            P(),
            P(),
            P("tp", None),
            P(),
            P(None, "tp"),
            P(None, "tp"),
            P("tp", None),
        ),
        out_specs=P("req", None),
        check_vma=False,
    )
```

```python
import jax
import jax.numpy as jnp
from jax import lax
from jax.sharding import PartitionSpec as P
from jax.experimental import pallas as pl
from jax.experimental.pallas import tpu as pltpu

STRETCH_TOKENS = 512
MOST_STRETCHES = 32
REQ_DEV = 1
RECOMPUTE_TOKENS = 256


eps_norm = 1e-06
rope_base = 1000000.0
floor_score = -1e30


def norm_rows(matrix, gain_vec):
    wide = matrix.astype(jnp.float32)
    factor = lax.rsqrt(jnp.mean(wide * wide, axis=-1, keepdims=True) + eps_norm)
    return wide * factor * gain_vec


def angles(position, head_size):
    half_dim = head_size // 2
    frequency = rope_base ** (-jnp.arange(half_dim, dtype=jnp.float32) / half_dim)
    return position.astype(jnp.float32)[..., None] * frequency


def rotate_halves(vector, angle_arg):
    half_dim = vector.shape[-1] // 2
    lower_half = vector[..., :half_dim]
    upper_half = vector[..., half_dim:]
    cosine = jnp.cos(angle_arg)
    sine_part = jnp.sin(angle_arg)
    return jnp.concatenate(
        [
            lower_half * cosine - upper_half * sine_part,
            upper_half * cosine + lower_half * sine_part,
        ],
        axis=-1,
    )


def rotary_heads(raw_proj, gain_vec, position, head_count):
    head_size = gain_vec.shape[0]
    split_heads = raw_proj.reshape(raw_proj.shape[0], head_count, head_size)
    normed = norm_rows(split_heads, gain_vec)
    return rotate_halves(normed, angles(position, head_size)[:, None, :]).astype(jnp.bfloat16)


def block_stats(grouped_heads, gathered_stretch_keys, values, live_mask):
    count_of_rows, key_heads, groups, head_size = grouped_heads.shape
    scores = jnp.einsum(
        "mhgd,khd->hgmk", grouped_heads, gathered_stretch_keys, preferred_element_type=jnp.float32
    ) * head_size ** (-0.5)
    row_peak = jnp.max(jnp.where(live_mask, scores, floor_score), axis=-1)
    weights = jnp.where(live_mask, jnp.exp(scores - row_peak[..., None]), 0.0)
    weight_sum = jnp.sum(weights, axis=-1)
    weighted = jnp.einsum(
        "hgmk,khd->mhgd", weights.astype(jnp.bfloat16), values, preferred_element_type=jnp.float32
    )
    head_total = key_heads * groups
    return (
        weighted.reshape(count_of_rows, head_total, head_size),
        row_peak.transpose(2, 0, 1).reshape(count_of_rows, head_total),
        weight_sum.transpose(2, 0, 1).reshape(count_of_rows, head_total),
    )


def merge_stats(weighted, row_peak, weight_sum):
    row_top = jnp.max(row_peak, axis=0)
    factor = jnp.exp(row_peak - row_top[None])
    merged = jnp.sum(weighted * factor[..., None], axis=0)
    total_sum = jnp.sum(weight_sum * factor, axis=0)
    result = (merged / total_sum[..., None]).astype(jnp.bfloat16)
    return result.reshape(result.shape[0], -1)


def swiglu(rows_in, w_gate, w_up):
    gate_proj = jnp.dot(rows_in, w_gate, preferred_element_type=jnp.float32)
    up_proj = jnp.dot(rows_in, w_up, preferred_element_type=jnp.float32)
    return (jax.nn.silu(gate_proj) * up_proj).astype(jnp.bfloat16)


far_position = 1 << 30


def held_block_kernel(slot_ref, alive_ref, q_ref, k0_ref, k1_ref, v0_ref, v1_ref, cos_ref, sin_ref, qpos_ref, kpos_ref, out_ref):
    step = pl.program_id(0)
    key_refs = (k0_ref, k1_ref)

    def store_stats(peak_rows, total_rows):
        pieces = []
        for value in (peak_rows, total_rows):
            rest = value
            for _ in range(3):
                piece = rest.astype(jnp.bfloat16).astype(jnp.float32)
                pieces.append(piece)
                rest = rest - piece
        rows = q_ref.shape[1]
        spare = out_ref.shape[1] - rows - 6 * peak_rows.shape[0]
        pieces.append(jnp.zeros((spare, peak_rows.shape[1]), jnp.float32))
        out_ref[0, rows:] = jnp.concatenate(pieces, axis=0).astype(out_ref.dtype)

    def store(weighted, peak, total):
        rows, lanes = weighted.shape
        chunks = rows // lanes
        lane = lax.broadcasted_iota(jnp.int32, (rows, lanes), 1)
        packed = jnp.where(lane == 0, peak, jnp.where(lane == 1, total, 0.0)).T
        out_ref[0, :rows] = weighted.astype(out_ref.dtype)
        peak_rows = jnp.concatenate([packed[0:1, c * lanes:(c + 1) * lanes] for c in range(chunks)], axis=0)
        total_rows = jnp.concatenate([packed[1:2, c * lanes:(c + 1) * lanes] for c in range(chunks)], axis=0)
        store_stats(peak_rows, total_rows)
    value_refs = (v0_ref, v1_ref)

    def run(parts):
        query = q_ref[0]
        query_pos = qpos_ref[0]
        scale = (query.shape[-1]) ** (-0.5)
        masked = []
        for j in parts:
            key = key_refs[j][0].astype(jnp.float32)
            half = key.shape[-1] // 2
            rotated = (key * cos_ref[0, j] + pltpu.roll(key, half, 1) * sin_ref[0, j]).astype(jnp.bfloat16)
            raw = lax.dot_general(query, rotated, (((1,), (1,)), ((), ())), preferred_element_type=jnp.float32)
            masked.append(jnp.where(kpos_ref[0, j] < query_pos, raw * scale, floor_score))
        peak = jnp.max(masked[0], axis=1, keepdims=True)
        for extra in masked[1:]:
            peak = jnp.maximum(peak, jnp.max(extra, axis=1, keepdims=True))
        safe_peak = jnp.where(peak == floor_score, 0.0, peak)
        total = None
        weighted = None
        for j, block in zip(parts, masked):
            w = jnp.exp(block - safe_peak)
            part_total = jnp.sum(w, axis=1, keepdims=True)
            part_sum = jnp.dot(w.astype(jnp.bfloat16), value_refs[j][0], preferred_element_type=jnp.float32)
            total = part_total if total is None else total + part_total
            weighted = part_sum if weighted is None else weighted + part_sum
        store(weighted, peak, total)

    live0 = alive_ref[2 * step] > 0
    live1 = alive_ref[2 * step + 1] > 0
    pl.when(live0 & live1)(lambda: run((0, 1)))
    pl.when(live0 & jnp.logical_not(live1))(lambda: run((0,)))
    pl.when(jnp.logical_not(live0) & live1)(lambda: run((1,)))

    @pl.when(jnp.logical_not(live0) & jnp.logical_not(live1))
    def _():
        rows, lanes = q_ref.shape[1], q_ref.shape[2]
        out_ref[0, :rows] = jnp.zeros((rows, lanes), out_ref.dtype)
        chunks = rows // lanes
        store_stats(jnp.full((chunks, lanes), floor_score, jnp.float32), jnp.zeros((chunks, lanes), jnp.float32))


def held_blocks(slots, alive, queries, key_pool, value_pool, cos_table, sin_table, query_pos, key_pos):
    requests, rows, head_size = queries.shape
    stretch = key_pool.shape[1]
    stat_rows = -(-6 * rows // head_size // 16) * 16

    def pool_spec(j):
        return pl.BlockSpec((1, stretch, head_size), lambda r, slot, alive: (slot[2 * r + j], 0, 0))

    grid_spec = pltpu.PrefetchScalarGridSpec(
        num_scalar_prefetch=2,
        grid=(requests,),
        in_specs=[
            pl.BlockSpec((1, rows, head_size), lambda r, slot, alive: (r, 0, 0)),
            pool_spec(0),
            pool_spec(1),
            pool_spec(0),
            pool_spec(1),
            pl.BlockSpec((1, 2, 1, head_size), lambda r, slot, alive: (r, 0, 0, 0)),
            pl.BlockSpec((1, 2, 1, head_size), lambda r, slot, alive: (r, 0, 0, 0)),
            pl.BlockSpec((1, rows, 1), lambda r, slot, alive: (r, 0, 0)),
            pl.BlockSpec((1, 2, 1, stretch), lambda r, slot, alive: (r, 0, 0, 0)),
        ],
        out_specs=pl.BlockSpec((1, rows + stat_rows, head_size), lambda r, slot, alive: (r, 0, 0)),
    )
    return pl.pallas_call(
        held_block_kernel,
        grid_spec=grid_spec,
        out_shape=jax.ShapeDtypeStruct((requests, rows + stat_rows, head_size), jnp.bfloat16),
        compiler_params=pltpu.CompilerParams(dimension_semantics=("arbitrary",)),
    )(slots, alive, queries, key_pool, key_pool, value_pool, value_pool, cos_table, sin_table, query_pos, key_pos)


def reduce_rows(terms, tp_count):
    blocks = terms.reshape(tp_count, terms.shape[0] // tp_count, terms.shape[1])
    got = lax.all_to_all(blocks, "tp", 0, 0, tiled=False)
    return jnp.sum(got.astype(jnp.float32), axis=0)


def gather_rows(rows, tp_count):
    tp_index = lax.axis_index("tp")
    parts = [rows]
    for shift in range(1, tp_count):
        pairs = [(i, (i + shift) % tp_count) for i in range(tp_count)]
        parts.append(lax.ppermute(rows, "tp", pairs))
    stacked = jnp.stack(parts)
    source = (tp_index - jnp.arange(tp_count)) % tp_count
    ordered = jnp.take(stacked, jnp.argsort(source), axis=0)
    return ordered.reshape(tp_count * rows.shape[0], rows.shape[1])


def on_device(
    hidden_in,
    recompute_pos,
    req_lengths,
    stretch_order,
    page_table,
    cached_key_pool,
    cached_value_pool,
    attn_gain,
    w_query,
    w_key,
    value_weight,
    query_gain,
    key_norm_gain,
    w_out,
    ffn_gain,
    w_gate,
    w_up,
    w_down,
):
    req_count = lax.axis_size("req")
    my_index = lax.axis_index("req")
    head_size = query_gain.shape[0]
    query_heads = w_query.shape[1] // head_size
    key_heads = w_key.shape[1] // head_size
    groups = query_heads // key_heads
    count_of_rows = hidden_in.shape[0]
    local_reqs = REQ_DEV
    req_rows = RECOMPUTE_TOKENS
    entries = local_reqs * MOST_STRETCHES
    pair_cap = entries // req_count
    normed = norm_rows(hidden_in, attn_gain).astype(jnp.bfloat16)
    query_raw = jnp.dot(normed, w_query, preferred_element_type=jnp.float32)
    unnormed_keys = jnp.dot(normed, w_key, preferred_element_type=jnp.float32)
    recomputed_values = (
        jnp.dot(normed, value_weight, preferred_element_type=jnp.float32)
        .astype(jnp.bfloat16)
        .reshape(count_of_rows, key_heads, head_size)
    )
    my_positions = lax.dynamic_slice_in_dim(recompute_pos, my_index * local_reqs, local_reqs, 0)
    my_lengths = lax.dynamic_slice_in_dim(req_lengths, my_index * local_reqs, local_reqs, 0)
    flattened_position = my_positions.reshape(count_of_rows)
    queries = rotary_heads(query_raw, query_gain, flattened_position, query_heads)
    recomputed_keys = rotary_heads(unnormed_keys, key_norm_gain, flattened_position, key_heads)
    grouped_heads = queries.reshape(count_of_rows, key_heads, groups, head_size)
    row_owner = jnp.arange(count_of_rows) // req_rows
    own_mask = (row_owner[None, :] == row_owner[:, None]) & (
        flattened_position[None, :] <= flattened_position[:, None]
    )
    fresh_sum, fresh_peak, fresh_total = block_stats(
        grouped_heads, recomputed_keys, recomputed_values, own_mask
    )
    holder_table = page_table[0][stretch_order]
    slot_table = page_table[1][stretch_order]
    holder_hits = holder_table[:, :, None] == jnp.arange(req_count)[None, None, :]
    hit_counts = jnp.cumsum(holder_hits.astype(jnp.int32), axis=1)
    pair_rank = jnp.sum(jnp.where(holder_hits, hit_counts - 1, 0), axis=2)
    my_sends = (holder_table == my_index)[:, :, None] & (
        pair_rank[:, :, None] == jnp.arange(pair_cap)[None, None, :]
    )
    send_slot = jnp.sum(jnp.where(my_sends, slot_table[:, :, None], 0), axis=1)
    send_place = jnp.sum(jnp.where(my_sends, jnp.arange(MOST_STRETCHES)[None, :, None], 0), axis=1)
    request_count = holder_table.shape[0]
    pool_slots = cached_key_pool.shape[0]
    slots = jnp.clip(send_slot, 0, pool_slots - 1).reshape(request_count * pair_cap).astype(jnp.int32)
    held_angle = angles(send_place * STRETCH_TOKENS, head_size)
    cos_table = jnp.cos(held_angle)
    sin_table = jnp.sin(held_angle)
    cos_table = jnp.concatenate([cos_table, cos_table], axis=-1)[:, :, None, :]
    sin_table = jnp.concatenate([-sin_table, sin_table], axis=-1)[:, :, None, :]
    query_pos = jnp.repeat(recompute_pos, groups, axis=1)[:, :, None]
    key_pos = jnp.where(
        (send_place < req_lengths[:, None])[:, :, None],
        send_place[:, :, None] * STRETCH_TOKENS + jnp.arange(STRETCH_TOKENS)[None, None, :],
        far_position,
    )[:, :, None, :]
    alive = (send_place < req_lengths[:, None]).reshape(request_count * pair_cap).astype(jnp.int32)
    halves = 2
    part_rows = req_rows // halves
    sum_rows = part_rows * groups
    chunks = sum_rows // head_size
    head_total = key_heads * groups
    got_sums, got_peaks, got_totals = [], [], []
    for part in range(halves):
        part_queries = queries[part * part_rows:(part + 1) * part_rows]
        query_copies = jnp.broadcast_to(part_queries[None], (req_count,) + part_queries.shape)
        all_queries = lax.all_to_all(query_copies, "req", 0, 0, tiled=False)
        all_queries = all_queries.reshape(request_count, sum_rows, head_size)
        held = held_blocks(
            slots,
            alive,
            all_queries,
            cached_key_pool,
            cached_value_pool,
            cos_table,
            sin_table,
            query_pos[:, part * sum_rows:(part + 1) * sum_rows],
            key_pos,
        )
        got = lax.all_to_all(held, "req", 0, 0, tiled=False)
        got_sums.append(got[:, :sum_rows].astype(jnp.float32).reshape(req_count, part_rows, head_total, head_size))

        def stat_of(k):
            base = sum_rows + 3 * k * chunks
            hi, mid, lo = (got[:, base + i * chunks:base + (i + 1) * chunks].astype(jnp.float32) for i in range(3))
            return ((hi + mid) + lo).reshape(req_count, part_rows, head_total)

        got_peaks.append(stat_of(0))
        got_totals.append(stat_of(1))
    got_sum = jnp.concatenate(got_sums, axis=1)
    got_peak = jnp.concatenate(got_peaks, axis=1)
    got_total = jnp.concatenate(got_totals, axis=1)
    attended = merge_stats(
        jnp.concatenate([got_sum.reshape(req_count, count_of_rows, head_total, head_size), fresh_sum[None]]),
        jnp.concatenate([got_peak, fresh_peak[None]]),
        jnp.concatenate([got_total, fresh_total[None]]),
    )
    tp_count = lax.axis_size("tp")
    tp_index = lax.axis_index("tp")
    block_rows = count_of_rows // tp_count
    attn_terms = jnp.dot(attended, w_out, preferred_element_type=jnp.float32).astype(jnp.bfloat16)
    attn_out = reduce_rows(attn_terms, tp_count)
    my_hidden = lax.dynamic_slice_in_dim(hidden_in, tp_index * block_rows, block_rows, 0)
    residual = (my_hidden.astype(jnp.float32) + attn_out).astype(jnp.bfloat16)
    normed_ffn = gather_rows(norm_rows(residual, ffn_gain).astype(jnp.bfloat16), tp_count)
    hidden = swiglu(normed_ffn, w_gate, w_up)
    down_terms = jnp.dot(hidden, w_down, preferred_element_type=jnp.float32).astype(jnp.bfloat16)
    ffn_out = reduce_rows(down_terms, tp_count)
    return gather_rows((residual.astype(jnp.float32) + ffn_out).astype(jnp.bfloat16), tp_count)


def solution(mesh):
    return jax.shard_map(
        on_device,
        mesh=mesh,
        in_specs=(
            P("req", None),
            P(),
            P(),
            P(),
            P(),
            P("req", None, "tp"),
            P("req", None, "tp"),
            P(),
            P(None, "tp"),
            P(None, "tp"),
            P(None, "tp"),
            P(),
            P(),
            P("tp", None),
            P(),
            P(None, "tp"),
            P(None, "tp"),
            P("tp", None),
        ),
        out_specs=P("req", None),
        check_vma=False,
    )
```

```python
import jax
import jax.numpy as jnp
from jax import lax
from jax.sharding import PartitionSpec as P
from jax.experimental import pallas as pl
from jax.experimental.pallas import tpu as pltpu

STRETCH_TOKENS = 512
MOST_STRETCHES = 32
REQ_DEV = 1
RECOMPUTE_TOKENS = 256


eps_norm = 1e-06
rope_base = 1000000.0
floor_score = -1e30


def norm_rows(matrix, gain_vec):
    wide = matrix.astype(jnp.float32)
    factor = lax.rsqrt(jnp.mean(wide * wide, axis=-1, keepdims=True) + eps_norm)
    return wide * factor * gain_vec


def angles(position, head_size):
    half_dim = head_size // 2
    frequency = rope_base ** (-jnp.arange(half_dim, dtype=jnp.float32) / half_dim)
    return position.astype(jnp.float32)[..., None] * frequency


def rotate_halves(vector, angle_arg):
    half_dim = vector.shape[-1] // 2
    lower_half = vector[..., :half_dim]
    upper_half = vector[..., half_dim:]
    cosine = jnp.cos(angle_arg)
    sine_part = jnp.sin(angle_arg)
    return jnp.concatenate(
        [
            lower_half * cosine - upper_half * sine_part,
            upper_half * cosine + lower_half * sine_part,
        ],
        axis=-1,
    )


def rotary_heads(raw_proj, gain_vec, position, head_count):
    head_size = gain_vec.shape[0]
    split_heads = raw_proj.reshape(raw_proj.shape[0], head_count, head_size)
    normed = norm_rows(split_heads, gain_vec)
    return rotate_halves(normed, angles(position, head_size)[:, None, :]).astype(jnp.bfloat16)


def block_stats(grouped_heads, gathered_stretch_keys, values, live_mask):
    count_of_rows, key_heads, groups, head_size = grouped_heads.shape
    scores = jnp.einsum(
        "mhgd,khd->hgmk", grouped_heads, gathered_stretch_keys, preferred_element_type=jnp.float32
    ) * head_size ** (-0.5)
    row_peak = jnp.max(jnp.where(live_mask, scores, floor_score), axis=-1)
    weights = jnp.where(live_mask, jnp.exp(scores - row_peak[..., None]), 0.0)
    weight_sum = jnp.sum(weights, axis=-1)
    weighted = jnp.einsum(
        "hgmk,khd->mhgd", weights.astype(jnp.bfloat16), values, preferred_element_type=jnp.float32
    )
    head_total = key_heads * groups
    return (
        weighted.reshape(count_of_rows, head_total, head_size),
        row_peak.transpose(2, 0, 1).reshape(count_of_rows, head_total),
        weight_sum.transpose(2, 0, 1).reshape(count_of_rows, head_total),
    )


def merge_stats(weighted, row_peak, weight_sum):
    row_top = jnp.max(row_peak, axis=0)
    factor = jnp.exp(row_peak - row_top[None])
    merged = jnp.sum(weighted * factor[..., None], axis=0)
    total_sum = jnp.sum(weight_sum * factor, axis=0)
    result = (merged / total_sum[..., None]).astype(jnp.bfloat16)
    return result.reshape(result.shape[0], -1)


def swiglu(rows_in, w_gate, w_up):
    gate_proj = jnp.dot(rows_in, w_gate, preferred_element_type=jnp.float32)
    up_proj = jnp.dot(rows_in, w_up, preferred_element_type=jnp.float32)
    return (jax.nn.silu(gate_proj) * up_proj).astype(jnp.bfloat16)


far_position = 1 << 30


def held_block_kernel(slot_ref, alive_ref, q_ref, k0_ref, k1_ref, v0_ref, v1_ref, cos_ref, sin_ref, qpos_ref, kpos_ref, out_ref):
    step = pl.program_id(0)
    key_refs = (k0_ref, k1_ref)

    def store_stats(peak_rows, total_rows):
        pieces = []
        for value in (peak_rows, total_rows):
            rest = value
            for _ in range(3):
                piece = rest.astype(jnp.bfloat16).astype(jnp.float32)
                pieces.append(piece)
                rest = rest - piece
        rows = q_ref.shape[1]
        spare = out_ref.shape[1] - rows - 6 * peak_rows.shape[0]
        pieces.append(jnp.zeros((spare, peak_rows.shape[1]), jnp.float32))
        out_ref[0, rows:] = jnp.concatenate(pieces, axis=0).astype(out_ref.dtype)

    def store(weighted, peak, total):
        rows, lanes = weighted.shape
        chunks = rows // lanes
        lane = lax.broadcasted_iota(jnp.int32, (rows, lanes), 1)
        packed = jnp.where(lane == 0, peak, jnp.where(lane == 1, total, 0.0)).T
        out_ref[0, :rows] = weighted.astype(out_ref.dtype)
        peak_rows = jnp.concatenate([packed[0:1, c * lanes:(c + 1) * lanes] for c in range(chunks)], axis=0)
        total_rows = jnp.concatenate([packed[1:2, c * lanes:(c + 1) * lanes] for c in range(chunks)], axis=0)
        store_stats(peak_rows, total_rows)
    value_refs = (v0_ref, v1_ref)

    def run(parts):
        query = q_ref[0]
        rows, lanes = query.shape
        pos_t = qpos_ref[0].T
        query_pos = jnp.concatenate([pos_t[:, c:c + 1] for c in range(rows // lanes)], axis=0)
        scale = (query.shape[-1]) ** (-0.5)
        masked = []
        for j in parts:
            key = key_refs[j][0].astype(jnp.float32)
            half = key.shape[-1] // 2
            rotated = (key * cos_ref[0, j] + pltpu.roll(key, half, 1) * sin_ref[0, j]).astype(jnp.bfloat16)
            raw = lax.dot_general(query, rotated, (((1,), (1,)), ((), ())), preferred_element_type=jnp.float32)
            masked.append(jnp.where(kpos_ref[0, j] < query_pos, raw * scale, floor_score))
        peak = jnp.max(masked[0], axis=1, keepdims=True)
        for extra in masked[1:]:
            peak = jnp.maximum(peak, jnp.max(extra, axis=1, keepdims=True))
        safe_peak = jnp.where(peak == floor_score, 0.0, peak)
        total = None
        weighted = None
        for j, block in zip(parts, masked):
            w = jnp.exp(block - safe_peak)
            part_total = jnp.sum(w, axis=1, keepdims=True)
            part_sum = jnp.dot(w.astype(jnp.bfloat16), value_refs[j][0], preferred_element_type=jnp.float32)
            total = part_total if total is None else total + part_total
            weighted = part_sum if weighted is None else weighted + part_sum
        store(weighted, peak, total)

    live0 = alive_ref[2 * step] > 0
    live1 = alive_ref[2 * step + 1] > 0
    pl.when(live0 & live1)(lambda: run((0, 1)))
    pl.when(live0 & jnp.logical_not(live1))(lambda: run((0,)))
    pl.when(jnp.logical_not(live0) & live1)(lambda: run((1,)))

    @pl.when(jnp.logical_not(live0) & jnp.logical_not(live1))
    def _():
        rows, lanes = q_ref.shape[1], q_ref.shape[2]
        out_ref[0, :rows] = jnp.zeros((rows, lanes), out_ref.dtype)
        chunks = rows // lanes
        store_stats(jnp.full((chunks, lanes), floor_score, jnp.float32), jnp.zeros((chunks, lanes), jnp.float32))


def held_blocks(slots, alive, queries, key_pool, value_pool, cos_table, sin_table, query_pos, key_pos):
    requests, rows, head_size = queries.shape
    stretch = key_pool.shape[1]
    stat_rows = -(-6 * rows // head_size // 16) * 16

    def pool_spec(j):
        return pl.BlockSpec((1, stretch, head_size), lambda r, slot, alive: (slot[2 * r + j], 0, 0))

    pos_rows = query_pos.shape[1]

    grid_spec = pltpu.PrefetchScalarGridSpec(
        num_scalar_prefetch=2,
        grid=(requests,),
        in_specs=[
            pl.BlockSpec((1, rows, head_size), lambda r, slot, alive: (r, 0, 0)),
            pool_spec(0),
            pool_spec(1),
            pool_spec(0),
            pool_spec(1),
            pl.BlockSpec((1, 2, 1, head_size), lambda r, slot, alive: (r, 0, 0, 0)),
            pl.BlockSpec((1, 2, 1, head_size), lambda r, slot, alive: (r, 0, 0, 0)),
            pl.BlockSpec((1, pos_rows, head_size), lambda r, slot, alive: (r, 0, 0)),
            pl.BlockSpec((1, 2, 1, stretch), lambda r, slot, alive: (r, 0, 0, 0)),
        ],
        out_specs=pl.BlockSpec((1, rows + stat_rows, head_size), lambda r, slot, alive: (r, 0, 0)),
    )
    return pl.pallas_call(
        held_block_kernel,
        grid_spec=grid_spec,
        out_shape=jax.ShapeDtypeStruct((requests, rows + stat_rows, head_size), jnp.bfloat16),
        compiler_params=pltpu.CompilerParams(dimension_semantics=("arbitrary",)),
    )(slots, alive, queries, key_pool, key_pool, value_pool, value_pool, cos_table, sin_table, query_pos, key_pos)


def reduce_rows(terms, tp_count):
    blocks = terms.reshape(tp_count, terms.shape[0] // tp_count, terms.shape[1])
    got = lax.all_to_all(blocks, "tp", 0, 0, tiled=False)
    return jnp.sum(got.astype(jnp.float32), axis=0)


def gather_rows(rows, tp_count):
    tp_index = lax.axis_index("tp")
    parts = [rows]
    for shift in range(1, tp_count):
        pairs = [(i, (i + shift) % tp_count) for i in range(tp_count)]
        parts.append(lax.ppermute(rows, "tp", pairs))
    stacked = jnp.stack(parts)
    source = (tp_index - jnp.arange(tp_count)) % tp_count
    ordered = jnp.take(stacked, jnp.argsort(source), axis=0)
    return ordered.reshape(tp_count * rows.shape[0], rows.shape[1])


def on_device(
    hidden_in,
    recompute_pos,
    req_lengths,
    stretch_order,
    page_table,
    cached_key_pool,
    cached_value_pool,
    attn_gain,
    w_query,
    w_key,
    value_weight,
    query_gain,
    key_norm_gain,
    w_out,
    ffn_gain,
    w_gate,
    w_up,
    w_down,
):
    req_count = lax.axis_size("req")
    my_index = lax.axis_index("req")
    head_size = query_gain.shape[0]
    query_heads = w_query.shape[1] // head_size
    key_heads = w_key.shape[1] // head_size
    groups = query_heads // key_heads
    count_of_rows = hidden_in.shape[0]
    local_reqs = REQ_DEV
    req_rows = RECOMPUTE_TOKENS
    entries = local_reqs * MOST_STRETCHES
    pair_cap = entries // req_count
    normed = norm_rows(hidden_in, attn_gain).astype(jnp.bfloat16)
    query_raw = jnp.dot(normed, w_query, preferred_element_type=jnp.float32)
    unnormed_keys = jnp.dot(normed, w_key, preferred_element_type=jnp.float32)
    recomputed_values = (
        jnp.dot(normed, value_weight, preferred_element_type=jnp.float32)
        .astype(jnp.bfloat16)
        .reshape(count_of_rows, key_heads, head_size)
    )
    my_positions = lax.dynamic_slice_in_dim(recompute_pos, my_index * local_reqs, local_reqs, 0)
    my_lengths = lax.dynamic_slice_in_dim(req_lengths, my_index * local_reqs, local_reqs, 0)
    flattened_position = my_positions.reshape(count_of_rows)
    queries = rotary_heads(query_raw, query_gain, flattened_position, query_heads)
    recomputed_keys = rotary_heads(unnormed_keys, key_norm_gain, flattened_position, key_heads)
    grouped_heads = queries.reshape(count_of_rows, key_heads, groups, head_size)
    row_owner = jnp.arange(count_of_rows) // req_rows
    own_mask = (row_owner[None, :] == row_owner[:, None]) & (
        flattened_position[None, :] <= flattened_position[:, None]
    )
    fresh_sum, fresh_peak, fresh_total = block_stats(
        grouped_heads, recomputed_keys, recomputed_values, own_mask
    )
    holder_table = page_table[0][stretch_order]
    slot_table = page_table[1][stretch_order]
    holder_hits = holder_table[:, :, None] == jnp.arange(req_count)[None, None, :]
    hit_counts = jnp.cumsum(holder_hits.astype(jnp.int32), axis=1)
    pair_rank = jnp.sum(jnp.where(holder_hits, hit_counts - 1, 0), axis=2)
    my_sends = (holder_table == my_index)[:, :, None] & (
        pair_rank[:, :, None] == jnp.arange(pair_cap)[None, None, :]
    )
    send_slot = jnp.sum(jnp.where(my_sends, slot_table[:, :, None], 0), axis=1)
    send_place = jnp.sum(jnp.where(my_sends, jnp.arange(MOST_STRETCHES)[None, :, None], 0), axis=1)
    request_count = holder_table.shape[0]
    pool_slots = cached_key_pool.shape[0]
    slot_live = send_place < req_lengths[:, None]
    last_live = lax.cummax(jnp.where(slot_live, jnp.arange(request_count)[:, None], -1), axis=0)
    fetch_slot = jnp.take_along_axis(send_slot, jnp.maximum(last_live, 0), axis=0)
    slots = jnp.clip(fetch_slot, 0, pool_slots - 1).reshape(request_count * pair_cap).astype(jnp.int32)
    held_angle = angles(send_place * STRETCH_TOKENS, head_size)
    cos_table = jnp.cos(held_angle)
    sin_table = jnp.sin(held_angle)
    cos_table = jnp.concatenate([cos_table, cos_table], axis=-1)[:, :, None, :]
    sin_table = jnp.concatenate([-sin_table, sin_table], axis=-1)[:, :, None, :]
    query_copies = jnp.broadcast_to(queries[None], (req_count,) + queries.shape)
    all_queries = lax.all_to_all(query_copies, "req", 0, 0, tiled=False)
    all_queries = all_queries.reshape(request_count, req_rows * groups, head_size)
    pos_lanes = jnp.repeat(recompute_pos, groups, axis=1).astype(jnp.float32).reshape(request_count, -1, head_size)
    pos_pad = -pos_lanes.shape[1] % 8
    query_pos = jnp.pad(pos_lanes, ((0, 0), (0, pos_pad), (0, 0)))
    key_pos = jnp.where(
        (send_place < req_lengths[:, None])[:, :, None],
        send_place[:, :, None] * STRETCH_TOKENS + jnp.arange(STRETCH_TOKENS)[None, None, :],
        far_position,
    ).astype(jnp.float32)[:, :, None, :]
    alive = (send_place < req_lengths[:, None]).reshape(request_count * pair_cap).astype(jnp.int32)
    held = held_blocks(
        slots, alive, all_queries, cached_key_pool, cached_value_pool, cos_table, sin_table, query_pos, key_pos
    )
    got = lax.all_to_all(held, "req", 0, 0, tiled=False)
    sum_rows = req_rows * groups
    chunks = sum_rows // head_size
    head_total = key_heads * groups
    got_sum = got[:, :sum_rows].astype(jnp.float32)

    def stat_of(k):
        base = sum_rows + 3 * k * chunks
        hi, mid, lo = (got[:, base + i * chunks:base + (i + 1) * chunks].astype(jnp.float32) for i in range(3))
        return ((hi + mid) + lo).reshape(req_count, count_of_rows, head_total)

    got_peak = stat_of(0)
    got_total = stat_of(1)
    attended = merge_stats(
        jnp.concatenate([got_sum.reshape(req_count, count_of_rows, head_total, head_size), fresh_sum[None]]),
        jnp.concatenate([got_peak, fresh_peak[None]]),
        jnp.concatenate([got_total, fresh_total[None]]),
    )
    tp_count = lax.axis_size("tp")
    tp_index = lax.axis_index("tp")
    block_rows = count_of_rows // tp_count
    attn_terms = jnp.dot(attended, w_out, preferred_element_type=jnp.float32).astype(jnp.bfloat16)
    attn_out = reduce_rows(attn_terms, tp_count)
    my_hidden = lax.dynamic_slice_in_dim(hidden_in, tp_index * block_rows, block_rows, 0)
    residual = (my_hidden.astype(jnp.float32) + attn_out).astype(jnp.bfloat16)
    normed_ffn = gather_rows(norm_rows(residual, ffn_gain).astype(jnp.bfloat16), tp_count)
    hidden = swiglu(normed_ffn, w_gate, w_up)
    down_terms = jnp.dot(hidden, w_down, preferred_element_type=jnp.float32).astype(jnp.bfloat16)
    ffn_out = reduce_rows(down_terms, tp_count)
    return gather_rows((residual.astype(jnp.float32) + ffn_out).astype(jnp.bfloat16), tp_count)


def solution(mesh):
    return jax.shard_map(
        on_device,
        mesh=mesh,
        in_specs=(
            P("req", None),
            P(),
            P(),
            P(),
            P(),
            P("req", None, "tp"),
            P("req", None, "tp"),
            P(),
            P(None, "tp"),
            P(None, "tp"),
            P(None, "tp"),
            P(),
            P(),
            P("tp", None),
            P(),
            P(None, "tp"),
            P(None, "tp"),
            P("tp", None),
        ),
        out_specs=P("req", None),
        check_vma=False,
    )
```

```python
import jax
import jax.numpy as jnp
from jax import lax
from jax.sharding import PartitionSpec as P
from jax.experimental import pallas as pl
from jax.experimental.pallas import tpu as pltpu

STRETCH_TOKENS = 512
MOST_STRETCHES = 32
REQ_DEV = 1
RECOMPUTE_TOKENS = 256


eps_norm = 1e-06
rope_base = 1000000.0
floor_score = -1e30


def norm_rows(matrix, gain_vec):
    wide = matrix.astype(jnp.float32)
    factor = lax.rsqrt(jnp.mean(wide * wide, axis=-1, keepdims=True) + eps_norm)
    return wide * factor * gain_vec


def angles(position, head_size):
    half_dim = head_size // 2
    frequency = rope_base ** (-jnp.arange(half_dim, dtype=jnp.float32) / half_dim)
    return position.astype(jnp.float32)[..., None] * frequency


def rotate_halves(vector, angle_arg):
    half_dim = vector.shape[-1] // 2
    lower_half = vector[..., :half_dim]
    upper_half = vector[..., half_dim:]
    cosine = jnp.cos(angle_arg)
    sine_part = jnp.sin(angle_arg)
    return jnp.concatenate(
        [
            lower_half * cosine - upper_half * sine_part,
            upper_half * cosine + lower_half * sine_part,
        ],
        axis=-1,
    )


def rotary_heads(raw_proj, gain_vec, position, head_count):
    head_size = gain_vec.shape[0]
    split_heads = raw_proj.reshape(raw_proj.shape[0], head_count, head_size)
    normed = norm_rows(split_heads, gain_vec)
    return rotate_halves(normed, angles(position, head_size)[:, None, :]).astype(jnp.bfloat16)


def block_stats(grouped_heads, gathered_stretch_keys, values, live_mask):
    count_of_rows, key_heads, groups, head_size = grouped_heads.shape
    scores = jnp.einsum(
        "mhgd,khd->hgmk", grouped_heads, gathered_stretch_keys, preferred_element_type=jnp.float32
    ) * head_size ** (-0.5)
    row_peak = jnp.max(jnp.where(live_mask, scores, floor_score), axis=-1)
    weights = jnp.where(live_mask, jnp.exp(scores - row_peak[..., None]), 0.0)
    weight_sum = jnp.sum(weights, axis=-1)
    weighted = jnp.einsum(
        "hgmk,khd->mhgd", weights.astype(jnp.bfloat16), values, preferred_element_type=jnp.float32
    )
    head_total = key_heads * groups
    return (
        weighted.reshape(count_of_rows, head_total, head_size),
        row_peak.transpose(2, 0, 1).reshape(count_of_rows, head_total),
        weight_sum.transpose(2, 0, 1).reshape(count_of_rows, head_total),
    )


def merge_stats(weighted, row_peak, weight_sum):
    row_top = jnp.max(row_peak, axis=0)
    factor = jnp.exp(row_peak - row_top[None])
    merged = jnp.sum(weighted * factor[..., None], axis=0)
    total_sum = jnp.sum(weight_sum * factor, axis=0)
    result = (merged / total_sum[..., None]).astype(jnp.bfloat16)
    return result.reshape(result.shape[0], -1)


def swiglu(rows_in, w_gate, w_up):
    gate_proj = jnp.dot(rows_in, w_gate, preferred_element_type=jnp.float32)
    up_proj = jnp.dot(rows_in, w_up, preferred_element_type=jnp.float32)
    return (jax.nn.silu(gate_proj) * up_proj).astype(jnp.bfloat16)


far_position = 1 << 30


def held_block_kernel(slot_ref, alive_ref, q_ref, k0_ref, k1_ref, v0_ref, v1_ref, cos_ref, sin_ref, qpos_ref, kpos_ref, out_ref):
    step = pl.program_id(0)
    key_refs = (k0_ref, k1_ref)

    def store_stats(peak_rows, total_rows):
        pieces = []
        for value in (peak_rows, total_rows):
            rest = value
            for _ in range(3):
                piece = rest.astype(jnp.bfloat16).astype(jnp.float32)
                pieces.append(piece)
                rest = rest - piece
        rows = q_ref.shape[1]
        spare = out_ref.shape[1] - rows - 6 * peak_rows.shape[0]
        pieces.append(jnp.zeros((spare, peak_rows.shape[1]), jnp.float32))
        out_ref[0, rows:] = jnp.concatenate(pieces, axis=0).astype(out_ref.dtype)

    def store(weighted, peak, total):
        rows, lanes = weighted.shape
        chunks = rows // lanes
        lane = lax.broadcasted_iota(jnp.int32, (rows, lanes), 1)
        packed = jnp.where(lane == 0, peak, jnp.where(lane == 1, total, 0.0)).T
        out_ref[0, :rows] = weighted.astype(out_ref.dtype)
        peak_rows = jnp.concatenate([packed[0:1, c * lanes:(c + 1) * lanes] for c in range(chunks)], axis=0)
        total_rows = jnp.concatenate([packed[1:2, c * lanes:(c + 1) * lanes] for c in range(chunks)], axis=0)
        store_stats(peak_rows, total_rows)
    value_refs = (v0_ref, v1_ref)

    def run(parts):
        query = q_ref[0]
        query_pos = qpos_ref[0]
        scale = (query.shape[-1]) ** (-0.5)
        masked = []
        for j in parts:
            key = key_refs[j][0].astype(jnp.float32)
            half = key.shape[-1] // 2
            rotated = (key * cos_ref[0, j] + pltpu.roll(key, half, 1) * sin_ref[0, j]).astype(jnp.bfloat16)
            raw = lax.dot_general(query, rotated, (((1,), (1,)), ((), ())), preferred_element_type=jnp.float32)
            masked.append(jnp.where(kpos_ref[0, j] < query_pos, raw * scale, floor_score))
        peak = jnp.max(masked[0], axis=1, keepdims=True)
        for extra in masked[1:]:
            peak = jnp.maximum(peak, jnp.max(extra, axis=1, keepdims=True))
        safe_peak = jnp.where(peak == floor_score, 0.0, peak)
        total = None
        weighted = None
        for j, block in zip(parts, masked):
            w = jnp.exp(block - safe_peak)
            part_total = jnp.sum(w, axis=1, keepdims=True)
            part_sum = jnp.dot(w.astype(jnp.bfloat16), value_refs[j][0], preferred_element_type=jnp.float32)
            total = part_total if total is None else total + part_total
            weighted = part_sum if weighted is None else weighted + part_sum
        store(weighted, peak, total)

    live0 = alive_ref[2 * step] > 0
    live1 = alive_ref[2 * step + 1] > 0
    pl.when(live0 & live1)(lambda: run((0, 1)))
    pl.when(live0 & jnp.logical_not(live1))(lambda: run((0,)))
    pl.when(jnp.logical_not(live0) & live1)(lambda: run((1,)))

    @pl.when(jnp.logical_not(live0) & jnp.logical_not(live1))
    def _():
        rows, lanes = q_ref.shape[1], q_ref.shape[2]
        out_ref[0, :rows] = jnp.zeros((rows, lanes), out_ref.dtype)
        chunks = rows // lanes
        store_stats(jnp.full((chunks, lanes), floor_score, jnp.float32), jnp.zeros((chunks, lanes), jnp.float32))


def held_blocks(slots, alive, queries, key_pool, value_pool, cos_table, sin_table, query_pos, key_pos):
    requests, rows, head_size = queries.shape
    stretch = key_pool.shape[1]
    stat_rows = -(-6 * rows // head_size // 16) * 16

    def pool_spec(j):
        return pl.BlockSpec((1, stretch, head_size), lambda r, slot, alive: (slot[2 * r + j], 0, 0))

    grid_spec = pltpu.PrefetchScalarGridSpec(
        num_scalar_prefetch=2,
        grid=(requests,),
        in_specs=[
            pl.BlockSpec((1, rows, head_size), lambda r, slot, alive: (r, 0, 0)),
            pool_spec(0),
            pool_spec(1),
            pool_spec(0),
            pool_spec(1),
            pl.BlockSpec((1, 2, 1, head_size), lambda r, slot, alive: (r, 0, 0, 0)),
            pl.BlockSpec((1, 2, 1, head_size), lambda r, slot, alive: (r, 0, 0, 0)),
            pl.BlockSpec((1, rows, 1), lambda r, slot, alive: (r, 0, 0)),
            pl.BlockSpec((1, 2, 1, stretch), lambda r, slot, alive: (r, 0, 0, 0)),
        ],
        out_specs=pl.BlockSpec((1, rows + stat_rows, head_size), lambda r, slot, alive: (r, 0, 0)),
    )
    return pl.pallas_call(
        held_block_kernel,
        grid_spec=grid_spec,
        out_shape=jax.ShapeDtypeStruct((requests, rows + stat_rows, head_size), jnp.bfloat16),
        compiler_params=pltpu.CompilerParams(dimension_semantics=("arbitrary",)),
    )(slots, alive, queries, key_pool, key_pool, value_pool, value_pool, cos_table, sin_table, query_pos, key_pos)


def reduce_rows(terms, tp_count):
    blocks = terms.reshape(tp_count, terms.shape[0] // tp_count, terms.shape[1])
    got = lax.all_to_all(blocks, "tp", 0, 0, tiled=False)
    return jnp.sum(got.astype(jnp.float32), axis=0)


def gather_rows(rows, tp_count):
    copies = jnp.broadcast_to(rows[None], (tp_count,) + rows.shape)
    got = lax.all_to_all(copies, "tp", 0, 0, tiled=False)
    return got.reshape(tp_count * rows.shape[0], rows.shape[1])


def on_device(
    hidden_in,
    recompute_pos,
    req_lengths,
    stretch_order,
    page_table,
    cached_key_pool,
    cached_value_pool,
    attn_gain,
    w_query,
    w_key,
    value_weight,
    query_gain,
    key_norm_gain,
    w_out,
    ffn_gain,
    w_gate,
    w_up,
    w_down,
):
    req_count = lax.axis_size("req")
    my_index = lax.axis_index("req")
    head_size = query_gain.shape[0]
    query_heads = w_query.shape[1] // head_size
    key_heads = w_key.shape[1] // head_size
    groups = query_heads // key_heads
    count_of_rows = hidden_in.shape[0]
    local_reqs = REQ_DEV
    req_rows = RECOMPUTE_TOKENS
    entries = local_reqs * MOST_STRETCHES
    pair_cap = entries // req_count
    normed = norm_rows(hidden_in, attn_gain).astype(jnp.bfloat16)
    query_raw = jnp.dot(normed, w_query, preferred_element_type=jnp.float32)
    unnormed_keys = jnp.dot(normed, w_key, preferred_element_type=jnp.float32)
    recomputed_values = (
        jnp.dot(normed, value_weight, preferred_element_type=jnp.float32)
        .astype(jnp.bfloat16)
        .reshape(count_of_rows, key_heads, head_size)
    )
    my_positions = lax.dynamic_slice_in_dim(recompute_pos, my_index * local_reqs, local_reqs, 0)
    my_lengths = lax.dynamic_slice_in_dim(req_lengths, my_index * local_reqs, local_reqs, 0)
    flattened_position = my_positions.reshape(count_of_rows)
    queries = rotary_heads(query_raw, query_gain, flattened_position, query_heads)
    recomputed_keys = rotary_heads(unnormed_keys, key_norm_gain, flattened_position, key_heads)
    grouped_heads = queries.reshape(count_of_rows, key_heads, groups, head_size)
    row_owner = jnp.arange(count_of_rows) // req_rows
    own_mask = (row_owner[None, :] == row_owner[:, None]) & (
        flattened_position[None, :] <= flattened_position[:, None]
    )
    fresh_sum, fresh_peak, fresh_total = block_stats(
        grouped_heads, recomputed_keys, recomputed_values, own_mask
    )
    holder_table = page_table[0][stretch_order]
    slot_table = page_table[1][stretch_order]
    holder_hits = holder_table[:, :, None] == jnp.arange(req_count)[None, None, :]
    hit_counts = jnp.cumsum(holder_hits.astype(jnp.int32), axis=1)
    pair_rank = jnp.sum(jnp.where(holder_hits, hit_counts - 1, 0), axis=2)
    my_sends = (holder_table == my_index)[:, :, None] & (
        pair_rank[:, :, None] == jnp.arange(pair_cap)[None, None, :]
    )
    send_slot = jnp.sum(jnp.where(my_sends, slot_table[:, :, None], 0), axis=1)
    send_place = jnp.sum(jnp.where(my_sends, jnp.arange(MOST_STRETCHES)[None, :, None], 0), axis=1)
    request_count = holder_table.shape[0]
    pool_slots = cached_key_pool.shape[0]
    slots = jnp.clip(send_slot, 0, pool_slots - 1).reshape(request_count * pair_cap).astype(jnp.int32)
    held_angle = angles(send_place * STRETCH_TOKENS, head_size)
    cos_table = jnp.cos(held_angle)
    sin_table = jnp.sin(held_angle)
    cos_table = jnp.concatenate([cos_table, cos_table], axis=-1)[:, :, None, :]
    sin_table = jnp.concatenate([-sin_table, sin_table], axis=-1)[:, :, None, :]
    query_copies = jnp.broadcast_to(queries[None], (req_count,) + queries.shape)
    all_queries = lax.all_to_all(query_copies, "req", 0, 0, tiled=False)
    all_queries = all_queries.reshape(request_count, req_rows * groups, head_size)
    query_pos = jnp.repeat(recompute_pos, groups, axis=1)[:, :, None]
    key_pos = jnp.where(
        (send_place < req_lengths[:, None])[:, :, None],
        send_place[:, :, None] * STRETCH_TOKENS + jnp.arange(STRETCH_TOKENS)[None, None, :],
        far_position,
    )[:, :, None, :]
    alive = (send_place < req_lengths[:, None]).reshape(request_count * pair_cap).astype(jnp.int32)
    held = held_blocks(
        slots, alive, all_queries, cached_key_pool, cached_value_pool, cos_table, sin_table, query_pos, key_pos
    )
    got = lax.all_to_all(held, "req", 0, 0, tiled=False)
    sum_rows = req_rows * groups
    chunks = sum_rows // head_size
    head_total = key_heads * groups
    got_sum = got[:, :sum_rows].astype(jnp.float32)

    def stat_of(k):
        base = sum_rows + 3 * k * chunks
        hi, mid, lo = (got[:, base + i * chunks:base + (i + 1) * chunks].astype(jnp.float32) for i in range(3))
        return ((hi + mid) + lo).reshape(req_count, count_of_rows, head_total)

    got_peak = stat_of(0)
    got_total = stat_of(1)
    attended = merge_stats(
        jnp.concatenate([got_sum.reshape(req_count, count_of_rows, head_total, head_size), fresh_sum[None]]),
        jnp.concatenate([got_peak, fresh_peak[None]]),
        jnp.concatenate([got_total, fresh_total[None]]),
    )
    tp_count = lax.axis_size("tp")
    tp_index = lax.axis_index("tp")
    block_rows = count_of_rows // tp_count
    attn_terms = jnp.dot(attended, w_out, preferred_element_type=jnp.float32).astype(jnp.bfloat16)
    attn_out = reduce_rows(attn_terms, tp_count)
    my_hidden = lax.dynamic_slice_in_dim(hidden_in, tp_index * block_rows, block_rows, 0)
    residual = (my_hidden.astype(jnp.float32) + attn_out).astype(jnp.bfloat16)
    normed_ffn = gather_rows(norm_rows(residual, ffn_gain).astype(jnp.bfloat16), tp_count)
    hidden = swiglu(normed_ffn, w_gate, w_up)
    down_terms = jnp.dot(hidden, w_down, preferred_element_type=jnp.float32).astype(jnp.bfloat16)
    ffn_out = reduce_rows(down_terms, tp_count)
    return gather_rows((residual.astype(jnp.float32) + ffn_out).astype(jnp.bfloat16), tp_count)


def solution(mesh):
    return jax.shard_map(
        on_device,
        mesh=mesh,
        in_specs=(
            P("req", None),
            P(),
            P(),
            P(),
            P(),
            P("req", None, "tp"),
            P("req", None, "tp"),
            P(),
            P(None, "tp"),
            P(None, "tp"),
            P(None, "tp"),
            P(),
            P(),
            P("tp", None),
            P(),
            P(None, "tp"),
            P(None, "tp"),
            P("tp", None),
        ),
        out_specs=P("req", None),
        check_vma=False,
    )
```

```python
import jax
import jax.numpy as jnp
from jax import lax
from jax.sharding import PartitionSpec as P
from jax.experimental import pallas as pl
from jax.experimental.pallas import tpu as pltpu

STRETCH_TOKENS = 512
MOST_STRETCHES = 32
REQ_DEV = 1
RECOMPUTE_TOKENS = 256


eps_norm = 1e-06
rope_base = 1000000.0
floor_score = -1e30


def norm_rows(matrix, gain_vec):
    wide = matrix.astype(jnp.float32)
    factor = lax.rsqrt(jnp.mean(wide * wide, axis=-1, keepdims=True) + eps_norm)
    return wide * factor * gain_vec


def angles(position, head_size):
    half_dim = head_size // 2
    frequency = rope_base ** (-jnp.arange(half_dim, dtype=jnp.float32) / half_dim)
    return position.astype(jnp.float32)[..., None] * frequency


def rotate_halves(vector, angle_arg):
    half_dim = vector.shape[-1] // 2
    lower_half = vector[..., :half_dim]
    upper_half = vector[..., half_dim:]
    cosine = jnp.cos(angle_arg)
    sine_part = jnp.sin(angle_arg)
    return jnp.concatenate(
        [
            lower_half * cosine - upper_half * sine_part,
            upper_half * cosine + lower_half * sine_part,
        ],
        axis=-1,
    )


def rotary_heads(raw_proj, gain_vec, position, head_count):
    head_size = gain_vec.shape[0]
    split_heads = raw_proj.reshape(raw_proj.shape[0], head_count, head_size)
    normed = norm_rows(split_heads, gain_vec)
    return rotate_halves(normed, angles(position, head_size)[:, None, :]).astype(jnp.bfloat16)


def block_stats(grouped_heads, gathered_stretch_keys, values, live_mask):
    count_of_rows, key_heads, groups, head_size = grouped_heads.shape
    scores = jnp.einsum(
        "mhgd,khd->hgmk", grouped_heads, gathered_stretch_keys, preferred_element_type=jnp.float32
    ) * head_size ** (-0.5)
    row_peak = jnp.max(jnp.where(live_mask, scores, floor_score), axis=-1)
    weights = jnp.where(live_mask, jnp.exp(scores - row_peak[..., None]), 0.0)
    weight_sum = jnp.sum(weights, axis=-1)
    weighted = jnp.einsum(
        "hgmk,khd->mhgd", weights.astype(jnp.bfloat16), values, preferred_element_type=jnp.float32
    )
    head_total = key_heads * groups
    return (
        weighted.reshape(count_of_rows, head_total, head_size),
        row_peak.transpose(2, 0, 1).reshape(count_of_rows, head_total),
        weight_sum.transpose(2, 0, 1).reshape(count_of_rows, head_total),
    )


def merge_stats(weighted, row_peak, weight_sum):
    row_top = jnp.max(row_peak, axis=0)
    factor = jnp.exp(row_peak - row_top[None])
    merged = jnp.sum(weighted * factor[..., None], axis=0)
    total_sum = jnp.sum(weight_sum * factor, axis=0)
    result = (merged / total_sum[..., None]).astype(jnp.bfloat16)
    return result.reshape(result.shape[0], -1)


def swiglu(rows_in, w_gate, w_up):
    gate_proj = jnp.dot(rows_in, w_gate, preferred_element_type=jnp.float32)
    up_proj = jnp.dot(rows_in, w_up, preferred_element_type=jnp.float32)
    return (jax.nn.silu(gate_proj) * up_proj).astype(jnp.bfloat16)


far_position = 1 << 30


def held_block_kernel(slot_ref, alive_ref, q_ref, k0_ref, k1_ref, v0_ref, v1_ref, cos_ref, sin_ref, qpos_ref, kpos_ref, out_ref):
    step = pl.program_id(0)
    key_refs = (k0_ref, k1_ref)

    def store_stats(peak_rows, total_rows):
        pieces = []
        for value in (peak_rows, total_rows):
            rest = value
            for _ in range(3):
                piece = rest.astype(jnp.bfloat16).astype(jnp.float32)
                pieces.append(piece)
                rest = rest - piece
        rows = q_ref.shape[1]
        spare = out_ref.shape[1] - rows - 6 * peak_rows.shape[0]
        pieces.append(jnp.zeros((spare, peak_rows.shape[1]), jnp.float32))
        out_ref[0, rows:] = jnp.concatenate(pieces, axis=0).astype(out_ref.dtype)

    def store(weighted, peak, total):
        rows, lanes = weighted.shape
        chunks = rows // lanes
        lane = lax.broadcasted_iota(jnp.int32, (rows, lanes), 1)
        packed = jnp.where(lane == 0, peak, jnp.where(lane == 1, total, 0.0)).T
        out_ref[0, :rows] = weighted.astype(out_ref.dtype)
        peak_rows = jnp.concatenate([packed[0:1, c * lanes:(c + 1) * lanes] for c in range(chunks)], axis=0)
        total_rows = jnp.concatenate([packed[1:2, c * lanes:(c + 1) * lanes] for c in range(chunks)], axis=0)
        store_stats(peak_rows, total_rows)
    value_refs = (v0_ref, v1_ref)

    def run(parts):
        query = q_ref[0]
        query_pos = qpos_ref[0]
        scale = (query.shape[-1]) ** (-0.5)
        masked = []
        for j in parts:
            key = key_refs[j][0].astype(jnp.float32)
            half = key.shape[-1] // 2
            rotated = (key * cos_ref[0, j] + pltpu.roll(key, half, 1) * sin_ref[0, j]).astype(jnp.bfloat16)
            raw = lax.dot_general(query, rotated, (((1,), (1,)), ((), ())), preferred_element_type=jnp.float32)
            masked.append(jnp.where(kpos_ref[0, j] < query_pos, raw * scale, floor_score))
        peak = jnp.max(masked[0], axis=1, keepdims=True)
        for extra in masked[1:]:
            peak = jnp.maximum(peak, jnp.max(extra, axis=1, keepdims=True))
        safe_peak = jnp.where(peak == floor_score, 0.0, peak)
        total = None
        weighted = None
        for j, block in zip(parts, masked):
            w = jnp.exp(block - safe_peak)
            part_total = jnp.sum(w, axis=1, keepdims=True)
            part_sum = jnp.dot(w.astype(jnp.bfloat16), value_refs[j][0], preferred_element_type=jnp.float32)
            total = part_total if total is None else total + part_total
            weighted = part_sum if weighted is None else weighted + part_sum
        store(weighted, peak, total)

    live0 = alive_ref[2 * step] > 0
    live1 = alive_ref[2 * step + 1] > 0
    pl.when(live0 & live1)(lambda: run((0, 1)))
    pl.when(live0 & jnp.logical_not(live1))(lambda: run((0,)))
    pl.when(jnp.logical_not(live0) & live1)(lambda: run((1,)))

    @pl.when(jnp.logical_not(live0) & jnp.logical_not(live1))
    def _():
        rows, lanes = q_ref.shape[1], q_ref.shape[2]
        out_ref[0, :rows] = jnp.zeros((rows, lanes), out_ref.dtype)
        chunks = rows // lanes
        store_stats(jnp.full((chunks, lanes), floor_score, jnp.float32), jnp.zeros((chunks, lanes), jnp.float32))


def held_blocks(slots, alive, queries, key_pool, value_pool, cos_table, sin_table, query_pos, key_pos):
    requests, rows, head_size = queries.shape
    stretch = key_pool.shape[1]
    stat_rows = -(-6 * rows // head_size // 16) * 16

    def pool_spec(j):
        return pl.BlockSpec((1, stretch, head_size), lambda r, slot, alive: (slot[2 * r + j], 0, 0))

    grid_spec = pltpu.PrefetchScalarGridSpec(
        num_scalar_prefetch=2,
        grid=(requests,),
        in_specs=[
            pl.BlockSpec((1, rows, head_size), lambda r, slot, alive: (r, 0, 0)),
            pool_spec(0),
            pool_spec(1),
            pool_spec(0),
            pool_spec(1),
            pl.BlockSpec((1, 2, 1, head_size), lambda r, slot, alive: (r, 0, 0, 0)),
            pl.BlockSpec((1, 2, 1, head_size), lambda r, slot, alive: (r, 0, 0, 0)),
            pl.BlockSpec((1, rows, 1), lambda r, slot, alive: (r, 0, 0)),
            pl.BlockSpec((1, 2, 1, stretch), lambda r, slot, alive: (r, 0, 0, 0)),
        ],
        out_specs=pl.BlockSpec((1, rows + stat_rows, head_size), lambda r, slot, alive: (r, 0, 0)),
    )
    return pl.pallas_call(
        held_block_kernel,
        grid_spec=grid_spec,
        out_shape=jax.ShapeDtypeStruct((requests, rows + stat_rows, head_size), jnp.bfloat16),
        compiler_params=pltpu.CompilerParams(dimension_semantics=("arbitrary",)),
    )(slots, alive, queries, key_pool, key_pool, value_pool, value_pool, cos_table, sin_table, query_pos, key_pos)


def reduce_rows(terms, tp_count):
    blocks = terms.reshape(tp_count, terms.shape[0] // tp_count, terms.shape[1])
    got = lax.all_to_all(blocks, "tp", 0, 0, tiled=False)
    return jnp.sum(got.astype(jnp.float32), axis=0)


def gather_rows(rows, tp_count):
    copies = jnp.broadcast_to(rows[None], (tp_count,) + rows.shape)
    got = lax.all_to_all(copies, "tp", 0, 0, tiled=False)
    return got.reshape(tp_count * rows.shape[0], rows.shape[1])


def on_device(
    hidden_in,
    recompute_pos,
    req_lengths,
    stretch_order,
    page_table,
    cached_key_pool,
    cached_value_pool,
    attn_gain,
    w_query,
    w_key,
    value_weight,
    query_gain,
    key_norm_gain,
    w_out,
    ffn_gain,
    w_gate,
    w_up,
    w_down,
):
    req_count = lax.axis_size("req")
    my_index = lax.axis_index("req")
    head_size = query_gain.shape[0]
    query_heads = w_query.shape[1] // head_size
    key_heads = w_key.shape[1] // head_size
    groups = query_heads // key_heads
    count_of_rows = hidden_in.shape[0]
    local_reqs = REQ_DEV
    req_rows = RECOMPUTE_TOKENS
    entries = local_reqs * MOST_STRETCHES
    pair_cap = entries // req_count
    normed = norm_rows(hidden_in, attn_gain).astype(jnp.bfloat16)
    query_raw = jnp.dot(normed, w_query, preferred_element_type=jnp.float32)
    unnormed_keys = jnp.dot(normed, w_key, preferred_element_type=jnp.float32)
    recomputed_values = (
        jnp.dot(normed, value_weight, preferred_element_type=jnp.float32)
        .astype(jnp.bfloat16)
        .reshape(count_of_rows, key_heads, head_size)
    )
    my_positions = lax.dynamic_slice_in_dim(recompute_pos, my_index * local_reqs, local_reqs, 0)
    my_lengths = lax.dynamic_slice_in_dim(req_lengths, my_index * local_reqs, local_reqs, 0)
    flattened_position = my_positions.reshape(count_of_rows)
    queries = rotary_heads(query_raw, query_gain, flattened_position, query_heads)
    recomputed_keys = rotary_heads(unnormed_keys, key_norm_gain, flattened_position, key_heads)
    grouped_heads = queries.reshape(count_of_rows, key_heads, groups, head_size)
    row_owner = jnp.arange(count_of_rows) // req_rows
    own_mask = (row_owner[None, :] == row_owner[:, None]) & (
        flattened_position[None, :] <= flattened_position[:, None]
    )
    fresh_sum, fresh_peak, fresh_total = block_stats(
        grouped_heads, recomputed_keys, recomputed_values, own_mask
    )
    holder_table = page_table[0][stretch_order]
    slot_table = page_table[1][stretch_order]
    holder_hits = holder_table[:, :, None] == jnp.arange(req_count)[None, None, :]
    hit_counts = jnp.cumsum(holder_hits.astype(jnp.int32), axis=1)
    pair_rank = jnp.sum(jnp.where(holder_hits, hit_counts - 1, 0), axis=2)
    my_sends = (holder_table == my_index)[:, :, None] & (
        pair_rank[:, :, None] == jnp.arange(pair_cap)[None, None, :]
    )
    send_slot = jnp.sum(jnp.where(my_sends, slot_table[:, :, None], 0), axis=1)
    send_place = jnp.sum(jnp.where(my_sends, jnp.arange(MOST_STRETCHES)[None, :, None], 0), axis=1)
    request_count = holder_table.shape[0]
    pool_slots = cached_key_pool.shape[0]
    slots = jnp.clip(send_slot, 0, pool_slots - 1).reshape(request_count * pair_cap).astype(jnp.int32)
    held_angle = angles(send_place * STRETCH_TOKENS, head_size)
    cos_table = jnp.cos(held_angle)
    sin_table = jnp.sin(held_angle)
    cos_table = jnp.concatenate([cos_table, cos_table], axis=-1)[:, :, None, :]
    sin_table = jnp.concatenate([-sin_table, sin_table], axis=-1)[:, :, None, :]
    query_copies = jnp.broadcast_to(queries[None], (req_count,) + queries.shape)
    all_queries = lax.all_to_all(query_copies, "req", 0, 0, tiled=False)
    all_queries = all_queries.reshape(request_count, req_rows * groups, head_size)
    query_pos = jnp.repeat(recompute_pos, groups, axis=1)[:, :, None]
    key_pos = jnp.where(
        (send_place < req_lengths[:, None])[:, :, None],
        send_place[:, :, None] * STRETCH_TOKENS + jnp.arange(STRETCH_TOKENS)[None, None, :],
        far_position,
    )[:, :, None, :]
    alive = (send_place < req_lengths[:, None]).reshape(request_count * pair_cap).astype(jnp.int32)
    held = held_blocks(
        slots, alive, all_queries, cached_key_pool, cached_value_pool, cos_table, sin_table, query_pos, key_pos
    )
    got = lax.all_to_all(held, "req", 0, 0, tiled=False)
    sum_rows = req_rows * groups
    chunks = sum_rows // head_size
    head_total = key_heads * groups
    got_sum = got[:, :sum_rows].astype(jnp.float32)

    def stat_of(k):
        base = sum_rows + 3 * k * chunks
        hi, mid, lo = (got[:, base + i * chunks:base + (i + 1) * chunks].astype(jnp.float32) for i in range(3))
        return ((hi + mid) + lo).reshape(req_count, count_of_rows, head_total)

    got_peak = stat_of(0)
    got_total = stat_of(1)
    got_sum = got_sum.reshape(req_count, count_of_rows, head_total, head_size)
    row_top = jnp.maximum(jnp.max(got_peak, axis=0), fresh_peak)
    held_factor = jnp.exp(got_peak - row_top[None])
    fresh_factor = jnp.exp(fresh_peak - row_top)
    merged = jnp.sum(got_sum * held_factor[..., None], axis=0) + fresh_sum * fresh_factor[..., None]
    merged_total = jnp.sum(got_total * held_factor, axis=0) + fresh_total * fresh_factor
    attended = (merged / merged_total[..., None]).astype(jnp.bfloat16).reshape(count_of_rows, -1)
    tp_count = lax.axis_size("tp")
    tp_index = lax.axis_index("tp")
    block_rows = count_of_rows // tp_count
    attn_terms = jnp.dot(attended, w_out, preferred_element_type=jnp.float32).astype(jnp.bfloat16)
    attn_out = reduce_rows(attn_terms, tp_count)
    my_hidden = lax.dynamic_slice_in_dim(hidden_in, tp_index * block_rows, block_rows, 0)
    residual = (my_hidden.astype(jnp.float32) + attn_out).astype(jnp.bfloat16)
    normed_ffn = gather_rows(norm_rows(residual, ffn_gain).astype(jnp.bfloat16), tp_count)
    hidden = swiglu(normed_ffn, w_gate, w_up)
    down_terms = jnp.dot(hidden, w_down, preferred_element_type=jnp.float32).astype(jnp.bfloat16)
    ffn_out = reduce_rows(down_terms, tp_count)
    return gather_rows((residual.astype(jnp.float32) + ffn_out).astype(jnp.bfloat16), tp_count)


def solution(mesh):
    return jax.shard_map(
        on_device,
        mesh=mesh,
        in_specs=(
            P("req", None),
            P(),
            P(),
            P(),
            P(),
            P("req", None, "tp"),
            P("req", None, "tp"),
            P(),
            P(None, "tp"),
            P(None, "tp"),
            P(None, "tp"),
            P(),
            P(),
            P("tp", None),
            P(),
            P(None, "tp"),
            P(None, "tp"),
            P("tp", None),
        ),
        out_specs=P("req", None),
        check_vma=False,
    )
```

```python
import jax
import jax.numpy as jnp
from jax import lax
from jax.sharding import PartitionSpec as P
from jax.experimental import pallas as pl
from jax.experimental.pallas import tpu as pltpu

STRETCH_TOKENS = 512
MOST_STRETCHES = 32
REQ_DEV = 1
RECOMPUTE_TOKENS = 256


eps_norm = 1e-06
rope_base = 1000000.0
floor_score = -1e30


def norm_rows(matrix, gain_vec):
    wide = matrix.astype(jnp.float32)
    factor = lax.rsqrt(jnp.mean(wide * wide, axis=-1, keepdims=True) + eps_norm)
    return wide * factor * gain_vec


def angles(position, head_size):
    half_dim = head_size // 2
    frequency = rope_base ** (-jnp.arange(half_dim, dtype=jnp.float32) / half_dim)
    return position.astype(jnp.float32)[..., None] * frequency


def rotate_halves(vector, angle_arg):
    half_dim = vector.shape[-1] // 2
    lower_half = vector[..., :half_dim]
    upper_half = vector[..., half_dim:]
    cosine = jnp.cos(angle_arg)
    sine_part = jnp.sin(angle_arg)
    return jnp.concatenate(
        [
            lower_half * cosine - upper_half * sine_part,
            upper_half * cosine + lower_half * sine_part,
        ],
        axis=-1,
    )


def rotary_heads(raw_proj, gain_vec, position, head_count):
    head_size = gain_vec.shape[0]
    split_heads = raw_proj.reshape(raw_proj.shape[0], head_count, head_size)
    normed = norm_rows(split_heads, gain_vec)
    return rotate_halves(normed, angles(position, head_size)[:, None, :]).astype(jnp.bfloat16)


def block_stats(grouped_heads, gathered_stretch_keys, values, live_mask):
    count_of_rows, key_heads, groups, head_size = grouped_heads.shape
    scores = jnp.einsum(
        "mhgd,khd->hgmk", grouped_heads, gathered_stretch_keys, preferred_element_type=jnp.float32
    ) * head_size ** (-0.5)
    row_peak = jnp.max(jnp.where(live_mask, scores, floor_score), axis=-1)
    weights = jnp.where(live_mask, jnp.exp(scores - row_peak[..., None]), 0.0)
    weight_sum = jnp.sum(weights, axis=-1)
    weighted = jnp.einsum(
        "hgmk,khd->mhgd", weights.astype(jnp.bfloat16), values, preferred_element_type=jnp.float32
    )
    head_total = key_heads * groups
    return (
        weighted.reshape(count_of_rows, head_total, head_size),
        row_peak.transpose(2, 0, 1).reshape(count_of_rows, head_total),
        weight_sum.transpose(2, 0, 1).reshape(count_of_rows, head_total),
    )


def merge_stats(weighted, row_peak, weight_sum):
    row_top = jnp.max(row_peak, axis=0)
    factor = jnp.exp(row_peak - row_top[None])
    merged = jnp.sum(weighted * factor[..., None], axis=0)
    total_sum = jnp.sum(weight_sum * factor, axis=0)
    result = (merged / total_sum[..., None]).astype(jnp.bfloat16)
    return result.reshape(result.shape[0], -1)


def swiglu(rows_in, w_gate, w_up):
    gate_proj = jnp.dot(rows_in, w_gate, preferred_element_type=jnp.float32)
    up_proj = jnp.dot(rows_in, w_up, preferred_element_type=jnp.float32)
    return (jax.nn.silu(gate_proj) * up_proj).astype(jnp.bfloat16)


far_position = 1 << 30


def held_block_kernel(slot_ref, alive_ref, q_ref, k0_ref, k1_ref, v0_ref, v1_ref, cos_ref, sin_ref, qpos_ref, kpos_ref, out_ref):
    step = pl.program_id(0)
    key_refs = (k0_ref, k1_ref)

    def store_stats(peak_rows, total_rows):
        pieces = []
        for value in (peak_rows, total_rows):
            rest = value
            for _ in range(3):
                piece = rest.astype(jnp.bfloat16).astype(jnp.float32)
                pieces.append(piece)
                rest = rest - piece
        rows = q_ref.shape[1]
        spare = out_ref.shape[1] - rows - 6 * peak_rows.shape[0]
        pieces.append(jnp.zeros((spare, peak_rows.shape[1]), jnp.float32))
        out_ref[0, rows:] = jnp.concatenate(pieces, axis=0).astype(out_ref.dtype)

    def store(weighted, peak, total):
        rows, lanes = weighted.shape
        chunks = rows // lanes
        lane = lax.broadcasted_iota(jnp.int32, (rows, lanes), 1)
        packed = jnp.where(lane == 0, peak, jnp.where(lane == 1, total, 0.0)).T
        out_ref[0, :rows] = weighted.astype(out_ref.dtype)
        peak_rows = jnp.concatenate([packed[0:1, c * lanes:(c + 1) * lanes] for c in range(chunks)], axis=0)
        total_rows = jnp.concatenate([packed[1:2, c * lanes:(c + 1) * lanes] for c in range(chunks)], axis=0)
        store_stats(peak_rows, total_rows)
    value_refs = (v0_ref, v1_ref)

    def run(parts):
        query = q_ref[0]
        query_pos = qpos_ref[0]
        scale = (query.shape[-1]) ** (-0.5)
        masked = []
        for j in parts:
            key = key_refs[j][0].astype(jnp.float32)
            half = key.shape[-1] // 2
            rotated = (key * cos_ref[0, j] + pltpu.roll(key, half, 1) * sin_ref[0, j]).astype(jnp.bfloat16)
            raw = lax.dot_general(query, rotated, (((1,), (1,)), ((), ())), preferred_element_type=jnp.float32)
            masked.append(jnp.where(kpos_ref[0, j] < query_pos, raw * scale, floor_score))
        peak = jnp.max(masked[0], axis=1, keepdims=True)
        for extra in masked[1:]:
            peak = jnp.maximum(peak, jnp.max(extra, axis=1, keepdims=True))
        safe_peak = jnp.where(peak == floor_score, 0.0, peak)
        total = None
        weighted = None
        for j, block in zip(parts, masked):
            w = jnp.exp(block - safe_peak)
            part_total = jnp.sum(w, axis=1, keepdims=True)
            part_sum = jnp.dot(w.astype(jnp.bfloat16), value_refs[j][0], preferred_element_type=jnp.float32)
            total = part_total if total is None else total + part_total
            weighted = part_sum if weighted is None else weighted + part_sum
        store(weighted, peak, total)

    live0 = alive_ref[2 * step] > 0
    live1 = alive_ref[2 * step + 1] > 0
    pl.when(live0 & live1)(lambda: run((0, 1)))
    pl.when(live0 & jnp.logical_not(live1))(lambda: run((0,)))
    pl.when(jnp.logical_not(live0) & live1)(lambda: run((1,)))

    @pl.when(jnp.logical_not(live0) & jnp.logical_not(live1))
    def _():
        rows, lanes = q_ref.shape[1], q_ref.shape[2]
        out_ref[0, :rows] = jnp.zeros((rows, lanes), out_ref.dtype)
        chunks = rows // lanes
        store_stats(jnp.full((chunks, lanes), floor_score, jnp.float32), jnp.zeros((chunks, lanes), jnp.float32))


def held_blocks(slots, alive, queries, key_pool, value_pool, cos_table, sin_table, query_pos, key_pos):
    requests, rows, head_size = queries.shape
    stretch = key_pool.shape[1]
    stat_rows = -(-6 * rows // head_size // 16) * 16

    def pool_spec(j):
        return pl.BlockSpec((1, stretch, head_size), lambda r, slot, alive: (slot[2 * r + j], 0, 0))

    grid_spec = pltpu.PrefetchScalarGridSpec(
        num_scalar_prefetch=2,
        grid=(requests,),
        in_specs=[
            pl.BlockSpec((1, rows, head_size), lambda r, slot, alive: (r, 0, 0)),
            pool_spec(0),
            pool_spec(1),
            pool_spec(0),
            pool_spec(1),
            pl.BlockSpec((1, 2, 1, head_size), lambda r, slot, alive: (r, 0, 0, 0)),
            pl.BlockSpec((1, 2, 1, head_size), lambda r, slot, alive: (r, 0, 0, 0)),
            pl.BlockSpec((1, rows, 1), lambda r, slot, alive: (r, 0, 0)),
            pl.BlockSpec((1, 2, 1, stretch), lambda r, slot, alive: (r, 0, 0, 0)),
        ],
        out_specs=pl.BlockSpec((1, rows + stat_rows, head_size), lambda r, slot, alive: (r, 0, 0)),
    )
    return pl.pallas_call(
        held_block_kernel,
        grid_spec=grid_spec,
        out_shape=jax.ShapeDtypeStruct((requests, rows + stat_rows, head_size), jnp.bfloat16),
        compiler_params=pltpu.CompilerParams(dimension_semantics=("arbitrary",)),
    )(slots, alive, queries, key_pool, key_pool, value_pool, value_pool, cos_table, sin_table, query_pos, key_pos)


def reduce_rows(terms, tp_count):
    blocks = terms.reshape(tp_count, terms.shape[0] // tp_count, terms.shape[1])
    got = lax.all_to_all(blocks, "tp", 0, 0, tiled=False)
    return jnp.sum(got.astype(jnp.float32), axis=0)


def gather_rows(rows, tp_count):
    copies = jnp.broadcast_to(rows[None], (tp_count,) + rows.shape)
    got = lax.all_to_all(copies, "tp", 0, 0, tiled=False)
    return got.reshape(tp_count * rows.shape[0], rows.shape[1])


def on_device(
    hidden_in,
    recompute_pos,
    req_lengths,
    stretch_order,
    page_table,
    cached_key_pool,
    cached_value_pool,
    attn_gain,
    w_query,
    w_key,
    value_weight,
    query_gain,
    key_norm_gain,
    w_out,
    ffn_gain,
    w_gate,
    w_up,
    w_down,
):
    req_count = lax.axis_size("req")
    my_index = lax.axis_index("req")
    head_size = query_gain.shape[0]
    query_heads = w_query.shape[1] // head_size
    key_heads = w_key.shape[1] // head_size
    groups = query_heads // key_heads
    count_of_rows = hidden_in.shape[0]
    local_reqs = REQ_DEV
    req_rows = RECOMPUTE_TOKENS
    entries = local_reqs * MOST_STRETCHES
    pair_cap = entries // req_count
    normed = norm_rows(hidden_in, attn_gain).astype(jnp.bfloat16)
    query_raw = jnp.dot(normed, w_query, preferred_element_type=jnp.float32)
    unnormed_keys = jnp.dot(normed, w_key, preferred_element_type=jnp.float32)
    recomputed_values = (
        jnp.dot(normed, value_weight, preferred_element_type=jnp.float32)
        .astype(jnp.bfloat16)
        .reshape(count_of_rows, key_heads, head_size)
    )
    my_positions = lax.dynamic_slice_in_dim(recompute_pos, my_index * local_reqs, local_reqs, 0)
    my_lengths = lax.dynamic_slice_in_dim(req_lengths, my_index * local_reqs, local_reqs, 0)
    flattened_position = my_positions.reshape(count_of_rows)
    queries = rotary_heads(query_raw, query_gain, flattened_position, query_heads)
    recomputed_keys = rotary_heads(unnormed_keys, key_norm_gain, flattened_position, key_heads)
    grouped_heads = queries.reshape(count_of_rows, key_heads, groups, head_size)
    row_owner = jnp.arange(count_of_rows) // req_rows
    own_mask = (row_owner[None, :] == row_owner[:, None]) & (
        flattened_position[None, :] <= flattened_position[:, None]
    )
    fresh_sum, fresh_peak, fresh_total = block_stats(
        grouped_heads, recomputed_keys, recomputed_values, own_mask
    )
    holder_table = page_table[0][stretch_order]
    slot_table = page_table[1][stretch_order]
    holder_hits = holder_table[:, :, None] == jnp.arange(req_count)[None, None, :]
    hit_counts = jnp.cumsum(holder_hits.astype(jnp.int32), axis=1)
    pair_rank = jnp.sum(jnp.where(holder_hits, hit_counts - 1, 0), axis=2)
    my_sends = (holder_table == my_index)[:, :, None] & (
        pair_rank[:, :, None] == jnp.arange(pair_cap)[None, None, :]
    )
    send_slot = jnp.sum(jnp.where(my_sends, slot_table[:, :, None], 0), axis=1)
    send_place = jnp.sum(jnp.where(my_sends, jnp.arange(MOST_STRETCHES)[None, :, None], 0), axis=1)
    request_count = holder_table.shape[0]
    pool_slots = cached_key_pool.shape[0]
    slot_live = send_place < req_lengths[:, None]
    last_live = lax.cummax(jnp.where(slot_live, jnp.arange(request_count)[:, None], -1), axis=0)
    fetch_slot = jnp.take_along_axis(send_slot, jnp.maximum(last_live, 0), axis=0)
    slots = jnp.clip(fetch_slot, 0, pool_slots - 1).reshape(request_count * pair_cap).astype(jnp.int32)
    held_angle = angles(send_place * STRETCH_TOKENS, head_size)
    cos_table = jnp.cos(held_angle)
    sin_table = jnp.sin(held_angle)
    cos_table = jnp.concatenate([cos_table, cos_table], axis=-1)[:, :, None, :]
    sin_table = jnp.concatenate([-sin_table, sin_table], axis=-1)[:, :, None, :]
    query_copies = jnp.broadcast_to(queries[None], (req_count,) + queries.shape)
    all_queries = lax.all_to_all(query_copies, "req", 0, 0, tiled=False)
    all_queries = all_queries.reshape(request_count, req_rows * groups, head_size)
    query_pos = jnp.repeat(recompute_pos, groups, axis=1)[:, :, None]
    key_pos = jnp.where(
        (send_place < req_lengths[:, None])[:, :, None],
        send_place[:, :, None] * STRETCH_TOKENS + jnp.arange(STRETCH_TOKENS)[None, None, :],
        far_position,
    )[:, :, None, :]
    alive = (send_place < req_lengths[:, None]).reshape(request_count * pair_cap).astype(jnp.int32)
    held = held_blocks(
        slots, alive, all_queries, cached_key_pool, cached_value_pool, cos_table, sin_table, query_pos, key_pos
    )
    got = lax.all_to_all(held, "req", 0, 0, tiled=False)
    sum_rows = req_rows * groups
    chunks = sum_rows // head_size
    head_total = key_heads * groups
    got_sum = got[:, :sum_rows].astype(jnp.float32)

    def stat_of(k):
        base = sum_rows + 3 * k * chunks
        hi, mid, lo = (got[:, base + i * chunks:base + (i + 1) * chunks].astype(jnp.float32) for i in range(3))
        return ((hi + mid) + lo).reshape(req_count, count_of_rows, head_total)

    got_peak = stat_of(0)
    got_total = stat_of(1)
    got_sum = got_sum.reshape(req_count, count_of_rows, head_total, head_size)
    row_top = jnp.maximum(jnp.max(got_peak, axis=0), fresh_peak)
    held_factor = jnp.exp(got_peak - row_top[None])
    fresh_factor = jnp.exp(fresh_peak - row_top)
    merged = jnp.sum(got_sum * held_factor[..., None], axis=0) + fresh_sum * fresh_factor[..., None]
    merged_total = jnp.sum(got_total * held_factor, axis=0) + fresh_total * fresh_factor
    attended = (merged / merged_total[..., None]).astype(jnp.bfloat16).reshape(count_of_rows, -1)
    tp_count = lax.axis_size("tp")
    tp_index = lax.axis_index("tp")
    block_rows = count_of_rows // tp_count
    attn_terms = jnp.dot(attended, w_out, preferred_element_type=jnp.float32).astype(jnp.bfloat16)
    attn_out = reduce_rows(attn_terms, tp_count)
    my_hidden = lax.dynamic_slice_in_dim(hidden_in, tp_index * block_rows, block_rows, 0)
    residual = (my_hidden.astype(jnp.float32) + attn_out).astype(jnp.bfloat16)
    normed_ffn = gather_rows(norm_rows(residual, ffn_gain).astype(jnp.bfloat16), tp_count)
    hidden = swiglu(normed_ffn, w_gate, w_up)
    down_terms = jnp.dot(hidden, w_down, preferred_element_type=jnp.float32).astype(jnp.bfloat16)
    ffn_out = reduce_rows(down_terms, tp_count)
    return gather_rows((residual.astype(jnp.float32) + ffn_out).astype(jnp.bfloat16), tp_count)


def solution(mesh):
    return jax.shard_map(
        on_device,
        mesh=mesh,
        in_specs=(
            P("req", None),
            P(),
            P(),
            P(),
            P(),
            P("req", None, "tp"),
            P("req", None, "tp"),
            P(),
            P(None, "tp"),
            P(None, "tp"),
            P(None, "tp"),
            P(),
            P(),
            P("tp", None),
            P(),
            P(None, "tp"),
            P(None, "tp"),
            P("tp", None),
        ),
        out_specs=P("req", None),
        check_vma=False,
    )
```

```python
import jax
import jax.numpy as jnp
from jax import lax
from jax.sharding import PartitionSpec as P
from jax.experimental import pallas as pl
from jax.experimental.pallas import tpu as pltpu

STRETCH_TOKENS = 512
MOST_STRETCHES = 32
REQ_DEV = 1
RECOMPUTE_TOKENS = 256


eps_norm = 1e-06
rope_base = 1000000.0
floor_score = -1e30


def norm_rows(matrix, gain_vec):
    wide = matrix.astype(jnp.float32)
    factor = lax.rsqrt(jnp.mean(wide * wide, axis=-1, keepdims=True) + eps_norm)
    return wide * factor * gain_vec


def angles(position, head_size):
    half_dim = head_size // 2
    frequency = rope_base ** (-jnp.arange(half_dim, dtype=jnp.float32) / half_dim)
    return position.astype(jnp.float32)[..., None] * frequency


def rotate_halves(vector, angle_arg):
    half_dim = vector.shape[-1] // 2
    lower_half = vector[..., :half_dim]
    upper_half = vector[..., half_dim:]
    cosine = jnp.cos(angle_arg)
    sine_part = jnp.sin(angle_arg)
    return jnp.concatenate(
        [
            lower_half * cosine - upper_half * sine_part,
            upper_half * cosine + lower_half * sine_part,
        ],
        axis=-1,
    )


def rotary_heads(raw_proj, gain_vec, position, head_count):
    head_size = gain_vec.shape[0]
    split_heads = raw_proj.reshape(raw_proj.shape[0], head_count, head_size)
    normed = norm_rows(split_heads, gain_vec)
    return rotate_halves(normed, angles(position, head_size)[:, None, :]).astype(jnp.bfloat16)


def block_stats(grouped_heads, gathered_stretch_keys, values, live_mask):
    count_of_rows, key_heads, groups, head_size = grouped_heads.shape
    scores = jnp.einsum(
        "mhgd,khd->hgmk", grouped_heads, gathered_stretch_keys, preferred_element_type=jnp.float32
    ) * head_size ** (-0.5)
    row_peak = jnp.max(jnp.where(live_mask, scores, floor_score), axis=-1)
    weights = jnp.where(live_mask, jnp.exp(scores - row_peak[..., None]), 0.0)
    weight_sum = jnp.sum(weights, axis=-1)
    weighted = jnp.einsum(
        "hgmk,khd->mhgd", weights.astype(jnp.bfloat16), values, preferred_element_type=jnp.float32
    )
    head_total = key_heads * groups
    return (
        weighted.reshape(count_of_rows, head_total, head_size),
        row_peak.transpose(2, 0, 1).reshape(count_of_rows, head_total),
        weight_sum.transpose(2, 0, 1).reshape(count_of_rows, head_total),
    )


def merge_stats(weighted, row_peak, weight_sum):
    row_top = jnp.max(row_peak, axis=0)
    factor = jnp.exp(row_peak - row_top[None])
    merged = jnp.sum(weighted * factor[..., None], axis=0)
    total_sum = jnp.sum(weight_sum * factor, axis=0)
    result = (merged / total_sum[..., None]).astype(jnp.bfloat16)
    return result.reshape(result.shape[0], -1)


def swiglu(rows_in, w_gate, w_up):
    gate_proj = jnp.dot(rows_in, w_gate, preferred_element_type=jnp.float32)
    up_proj = jnp.dot(rows_in, w_up, preferred_element_type=jnp.float32)
    return (jax.nn.silu(gate_proj) * up_proj).astype(jnp.bfloat16)


far_position = 1 << 30


def held_block_kernel(slot_ref, alive_ref, q_ref, k0_ref, k1_ref, v0_ref, v1_ref, cos_ref, sin_ref, qpos_ref, kpos_ref, out_ref):
    step = pl.program_id(0)
    key_refs = (k0_ref, k1_ref)

    def store_stats(peak_rows, total_rows):
        pieces = []
        for value in (peak_rows, total_rows):
            rest = value
            for _ in range(3):
                piece = rest.astype(jnp.bfloat16).astype(jnp.float32)
                pieces.append(piece)
                rest = rest - piece
        rows = q_ref.shape[1]
        spare = out_ref.shape[1] - rows - 6 * peak_rows.shape[0]
        pieces.append(jnp.zeros((spare, peak_rows.shape[1]), jnp.float32))
        out_ref[0, rows:] = jnp.concatenate(pieces, axis=0).astype(out_ref.dtype)

    def store(weighted, peak, total):
        rows, lanes = weighted.shape
        chunks = rows // lanes
        lane = lax.broadcasted_iota(jnp.int32, (rows, lanes), 1)
        packed = jnp.where(lane == 0, peak, jnp.where(lane == 1, total, 0.0)).T
        out_ref[0, :rows] = weighted.astype(out_ref.dtype)
        peak_rows = jnp.concatenate([packed[0:1, c * lanes:(c + 1) * lanes] for c in range(chunks)], axis=0)
        total_rows = jnp.concatenate([packed[1:2, c * lanes:(c + 1) * lanes] for c in range(chunks)], axis=0)
        store_stats(peak_rows, total_rows)
    value_refs = (v0_ref, v1_ref)

    def run(parts):
        query = q_ref[0]
        query_pos = qpos_ref[0]
        scale = (query.shape[-1]) ** (-0.5)
        masked = []
        for j in parts:
            key = key_refs[j][0].astype(jnp.float32)
            half = key.shape[-1] // 2
            rotated = (key * cos_ref[0, j] + pltpu.roll(key, half, 1) * sin_ref[0, j]).astype(jnp.bfloat16)
            raw = lax.dot_general(query, rotated, (((1,), (1,)), ((), ())), preferred_element_type=jnp.float32)
            masked.append(jnp.where(kpos_ref[0, j] < query_pos, raw * scale, floor_score))
        peak = jnp.max(masked[0], axis=1, keepdims=True)
        for extra in masked[1:]:
            peak = jnp.maximum(peak, jnp.max(extra, axis=1, keepdims=True))
        safe_peak = jnp.where(peak == floor_score, 0.0, peak)
        total = None
        weighted = None
        for j, block in zip(parts, masked):
            w = jnp.exp(block - safe_peak)
            part_total = jnp.sum(w, axis=1, keepdims=True)
            part_sum = jnp.dot(w.astype(jnp.bfloat16), value_refs[j][0], preferred_element_type=jnp.float32)
            total = part_total if total is None else total + part_total
            weighted = part_sum if weighted is None else weighted + part_sum
        store(weighted, peak, total)

    live0 = alive_ref[2 * step] > 0
    live1 = alive_ref[2 * step + 1] > 0
    pl.when(live0 & live1)(lambda: run((0, 1)))
    pl.when(live0 & jnp.logical_not(live1))(lambda: run((0,)))
    pl.when(jnp.logical_not(live0) & live1)(lambda: run((1,)))

    @pl.when(jnp.logical_not(live0) & jnp.logical_not(live1))
    def _():
        rows, lanes = q_ref.shape[1], q_ref.shape[2]
        out_ref[0, :rows] = jnp.zeros((rows, lanes), out_ref.dtype)
        chunks = rows // lanes
        store_stats(jnp.full((chunks, lanes), floor_score, jnp.float32), jnp.zeros((chunks, lanes), jnp.float32))


def held_blocks(slots, alive, queries, key_pool, value_pool, cos_table, sin_table, query_pos, key_pos):
    requests, rows, head_size = queries.shape
    stretch = key_pool.shape[1]
    stat_rows = -(-6 * rows // head_size // 16) * 16

    def pool_spec(j):
        return pl.BlockSpec((1, stretch, head_size), lambda r, slot, alive: (slot[2 * r + j], 0, 0))

    grid_spec = pltpu.PrefetchScalarGridSpec(
        num_scalar_prefetch=2,
        grid=(requests,),
        in_specs=[
            pl.BlockSpec((1, rows, head_size), lambda r, slot, alive: (r, 0, 0)),
            pool_spec(0),
            pool_spec(1),
            pool_spec(0),
            pool_spec(1),
            pl.BlockSpec((1, 2, 1, head_size), lambda r, slot, alive: (r, 0, 0, 0)),
            pl.BlockSpec((1, 2, 1, head_size), lambda r, slot, alive: (r, 0, 0, 0)),
            pl.BlockSpec((1, rows, 1), lambda r, slot, alive: (r, 0, 0)),
            pl.BlockSpec((1, 2, 1, stretch), lambda r, slot, alive: (r, 0, 0, 0)),
        ],
        out_specs=pl.BlockSpec((1, rows + stat_rows, head_size), lambda r, slot, alive: (r, 0, 0)),
    )
    return pl.pallas_call(
        held_block_kernel,
        grid_spec=grid_spec,
        out_shape=jax.ShapeDtypeStruct((requests, rows + stat_rows, head_size), jnp.bfloat16),
        compiler_params=pltpu.CompilerParams(dimension_semantics=("arbitrary",)),
    )(slots, alive, queries, key_pool, key_pool, value_pool, value_pool, cos_table, sin_table, query_pos, key_pos)


def reduce_rows(terms, tp_count):
    blocks = terms.reshape(tp_count, terms.shape[0] // tp_count, terms.shape[1])
    got = lax.all_to_all(blocks, "tp", 0, 0, tiled=False)
    return jnp.sum(got.astype(jnp.float32), axis=0)


def gather_rows(rows, tp_count):
    copies = jnp.broadcast_to(rows[None], (tp_count,) + rows.shape)
    got = lax.all_to_all(copies, "tp", 0, 0, tiled=False)
    return got.reshape(tp_count * rows.shape[0], rows.shape[1])


def on_device(
    hidden_in,
    recompute_pos,
    req_lengths,
    stretch_order,
    page_table,
    cached_key_pool,
    cached_value_pool,
    attn_gain,
    w_query,
    w_key,
    value_weight,
    query_gain,
    key_norm_gain,
    w_out,
    ffn_gain,
    w_gate,
    w_up,
    w_down,
):
    req_count = lax.axis_size("req")
    my_index = lax.axis_index("req")
    head_size = query_gain.shape[0]
    query_heads = w_query.shape[1] // head_size
    key_heads = w_key.shape[1] // head_size
    groups = query_heads // key_heads
    count_of_rows = hidden_in.shape[0]
    local_reqs = REQ_DEV
    req_rows = RECOMPUTE_TOKENS
    entries = local_reqs * MOST_STRETCHES
    pair_cap = entries // req_count
    normed = norm_rows(hidden_in, attn_gain).astype(jnp.bfloat16)
    query_raw = jnp.dot(normed, w_query, preferred_element_type=jnp.float32)
    unnormed_keys = jnp.dot(normed, w_key, preferred_element_type=jnp.float32)
    recomputed_values = (
        jnp.dot(normed, value_weight, preferred_element_type=jnp.float32)
        .astype(jnp.bfloat16)
        .reshape(count_of_rows, key_heads, head_size)
    )
    my_positions = lax.dynamic_slice_in_dim(recompute_pos, my_index * local_reqs, local_reqs, 0)
    my_lengths = lax.dynamic_slice_in_dim(req_lengths, my_index * local_reqs, local_reqs, 0)
    flattened_position = my_positions.reshape(count_of_rows)
    queries = rotary_heads(query_raw, query_gain, flattened_position, query_heads)
    recomputed_keys = rotary_heads(unnormed_keys, key_norm_gain, flattened_position, key_heads)
    grouped_heads = queries.reshape(count_of_rows, key_heads, groups, head_size)
    row_owner = jnp.arange(count_of_rows) // req_rows
    own_mask = (row_owner[None, :] == row_owner[:, None]) & (
        flattened_position[None, :] <= flattened_position[:, None]
    )
    fresh_sum, fresh_peak, fresh_total = block_stats(
        grouped_heads, recomputed_keys, recomputed_values, own_mask
    )
    holder_table = page_table[0][stretch_order]
    slot_table = page_table[1][stretch_order]
    holder_hits = holder_table[:, :, None] == jnp.arange(req_count)[None, None, :]
    hit_counts = jnp.cumsum(holder_hits.astype(jnp.int32), axis=1)
    pair_rank = jnp.sum(jnp.where(holder_hits, hit_counts - 1, 0), axis=2)
    my_sends = (holder_table == my_index)[:, :, None] & (
        pair_rank[:, :, None] == jnp.arange(pair_cap)[None, None, :]
    )
    send_slot = jnp.sum(jnp.where(my_sends, slot_table[:, :, None], 0), axis=1)
    send_place = jnp.sum(jnp.where(my_sends, jnp.arange(MOST_STRETCHES)[None, :, None], 0), axis=1)
    request_count = holder_table.shape[0]
    pool_slots = cached_key_pool.shape[0]
    slots = jnp.clip(send_slot, 0, pool_slots - 1).reshape(request_count * pair_cap).astype(jnp.int32)
    held_angle = angles(send_place * STRETCH_TOKENS, head_size)
    cos_table = jnp.cos(held_angle)
    sin_table = jnp.sin(held_angle)
    cos_table = jnp.concatenate([cos_table, cos_table], axis=-1)[:, :, None, :]
    sin_table = jnp.concatenate([-sin_table, sin_table], axis=-1)[:, :, None, :]
    query_rows = queries.reshape(count_of_rows * query_heads, head_size)
    query_copies = jnp.broadcast_to(query_rows[None], (req_count,) + query_rows.shape)
    all_queries = lax.all_to_all(query_copies, "req", 0, 0, tiled=False)
    all_queries = all_queries.reshape(request_count, req_rows * groups, head_size)
    query_pos = jnp.repeat(recompute_pos, groups, axis=1)[:, :, None]
    key_pos = jnp.where(
        (send_place < req_lengths[:, None])[:, :, None],
        send_place[:, :, None] * STRETCH_TOKENS + jnp.arange(STRETCH_TOKENS)[None, None, :],
        far_position,
    )[:, :, None, :]
    alive = (send_place < req_lengths[:, None]).reshape(request_count * pair_cap).astype(jnp.int32)
    held = held_blocks(
        slots, alive, all_queries, cached_key_pool, cached_value_pool, cos_table, sin_table, query_pos, key_pos
    )
    got = lax.all_to_all(held, "req", 0, 0, tiled=False)
    sum_rows = req_rows * groups
    chunks = sum_rows // head_size
    head_total = key_heads * groups
    got_sum = got[:, :sum_rows].astype(jnp.float32)

    def stat_of(k):
        base = sum_rows + 3 * k * chunks
        hi, mid, lo = (got[:, base + i * chunks:base + (i + 1) * chunks].astype(jnp.float32) for i in range(3))
        return ((hi + mid) + lo).reshape(req_count, count_of_rows, head_total)

    got_peak = stat_of(0)
    got_total = stat_of(1)
    got_sum = got_sum.reshape(req_count, count_of_rows, head_total, head_size)
    row_top = jnp.maximum(jnp.max(got_peak, axis=0), fresh_peak)
    held_factor = jnp.exp(got_peak - row_top[None])
    fresh_factor = jnp.exp(fresh_peak - row_top)
    merged = jnp.sum(got_sum * held_factor[..., None], axis=0) + fresh_sum * fresh_factor[..., None]
    merged_total = jnp.sum(got_total * held_factor, axis=0) + fresh_total * fresh_factor
    attended = (merged / merged_total[..., None]).astype(jnp.bfloat16).reshape(count_of_rows, -1)
    tp_count = lax.axis_size("tp")
    tp_index = lax.axis_index("tp")
    block_rows = count_of_rows // tp_count
    attn_terms = jnp.dot(attended, w_out, preferred_element_type=jnp.float32).astype(jnp.bfloat16)
    attn_out = reduce_rows(attn_terms, tp_count)
    my_hidden = lax.dynamic_slice_in_dim(hidden_in, tp_index * block_rows, block_rows, 0)
    residual = (my_hidden.astype(jnp.float32) + attn_out).astype(jnp.bfloat16)
    normed_ffn = gather_rows(norm_rows(residual, ffn_gain).astype(jnp.bfloat16), tp_count)
    hidden = swiglu(normed_ffn, w_gate, w_up)
    down_terms = jnp.dot(hidden, w_down, preferred_element_type=jnp.float32).astype(jnp.bfloat16)
    ffn_out = reduce_rows(down_terms, tp_count)
    return gather_rows((residual.astype(jnp.float32) + ffn_out).astype(jnp.bfloat16), tp_count)


def solution(mesh):
    return jax.shard_map(
        on_device,
        mesh=mesh,
        in_specs=(
            P("req", None),
            P(),
            P(),
            P(),
            P(),
            P("req", None, "tp"),
            P("req", None, "tp"),
            P(),
            P(None, "tp"),
            P(None, "tp"),
            P(None, "tp"),
            P(),
            P(),
            P("tp", None),
            P(),
            P(None, "tp"),
            P(None, "tp"),
            P("tp", None),
        ),
        out_specs=P("req", None),
        check_vma=False,
    )
```
